32 devices in a mesh: area: 16 (over z, y, core), depth: 2 (over x).
Axes of the slice: x: 2, y: 2, z: 4, core: 2. Of those that a mesh axis runs over, the one named last changes fastest.
Arguments:
- pressure: float32 [32, 128, 1024], P('depth', 'area'), may hold values from -2.5 to -0.3
- theta_old: float32 [32, 128, 1024], P('depth', 'area'), may hold values from 0.1 to 0.35
- source: float32 [32, 128, 1024], P('depth', 'area'), may hold values from -3 to 3
- soil_type: int32 [32, 128, 1024], P('depth', 'area'), may hold values from 0 to 11
- soil_params: float32 [5, 12], replicated, as said below
Outputs:
- new_pressure: float32 [32, 128, 1024], P('depth', 'area')
- coarse_head: float32 [128, 1024], P('area')
The draws below stay inside these ranges and needn't reach their ends.
Inputs may be any that keep to these rules, and one draw needn't show every extreme that they name: Each column of soil_params holds theta_r in 0.03 to 0.1, theta_s in 0.35 to 0.5, a in 0.5 to 3, n in 1.3 to 2.5, Ks in 0.2 to 2.
All inputs are finite; a program needn't handle non-finite values.
Results may differ from the reference program's by a relative error of at most 0.00002.
Values sent between devices are 32-bit elements; how exact they have to be, the bound alone decides.
No kernel may reach another device: no remote copies, remote signals or barrier semaphores. Data moves between devices by JAX's collectives and lax.ppermute only.
A program may use at most 64 MiB of HBM per device.

```python
import math
import jax
import jax.numpy as jnp
from jax import lax

NY = 1024
NSOIL = 12
NZ = 32
NX = 128


def draw_soil_params(key, part):
    subkeys = jax.random.split(key, 5)
    shape_row = (NSOIL,)
    residual_wc = jax.random.uniform(subkeys[0], shape_row, jnp.float32, 0.03, 0.1)
    saturated_wc = jax.random.uniform(subkeys[1], shape_row, jnp.float32, 0.35, 0.5)
    shape_n = jax.random.uniform(subkeys[3], shape_row, jnp.float32, 1.3, 2.5)
    alpha_vg = jnp.exp(jax.random.uniform(subkeys[2], shape_row, jnp.float32, math.log(0.5), math.log(3.0)))
    k_sat = jnp.exp(jax.random.uniform(subkeys[4], shape_row, jnp.float32, math.log(0.2), math.log(2.0)))
    return jnp.stack([residual_wc, saturated_wc, alpha_vg, shape_n, k_sat])


def with_ends(result, stream_key, low, high):
    dims = result.shape
    place = [jax.random.randint(jax.random.fold_in(stream_key, axis), (), 0, dims[axis]) for axis in range(len(dims))]
    result = result.at[tuple(place)].set(low)
    longest = dims.index(max(dims))
    place[longest] = (place[longest] + 1) % dims[longest]
    return result.at[tuple(place)].set(high)


def shard_levels(key, shape, shards, least, high):
    gain = 1.0
    for dim, shards_of in shards:
        steps = jax.random.uniform(jax.random.fold_in(jax.random.fold_in(key, 6), dim), (shards_of,), jnp.float32, least / len(shards), high / len(shards))
        gain = gain * jnp.repeat(jnp.exp(steps), shape[dim] // shards_of).reshape((-1,) + (1,) * (len(shape) - 1 - dim))
    return gain


def gaussian(own_key, dims, scale, limit, cuts=(), kind=jnp.bfloat16):
    factor_of = shard_levels(own_key, dims, cuts, -0.22, 0.18) if cuts else 1.0
    drawn = jax.random.normal(own_key, dims, jnp.float32) * scale * factor_of
    return jnp.minimum(jnp.maximum(drawn, -limit), limit).astype(kind)


def setup_inputs(seed: int = 0) -> dict:
    streams_of = jax.random.split(jax.random.key(seed), 6)
    return {
        "pressure": jnp.clip(-2.5 + 2.2 * jax.random.uniform(streams_of[0], (NZ, NX, NY), jnp.float32) ** shard_levels(streams_of[0], (NZ, NX, NY), ((0, 2), (1, 16)), -0.2, 0.2), -2.5, -0.3),
        "theta_old": jnp.clip(0.1 + 0.25 * jax.random.uniform(streams_of[1], (NZ, NX, NY), jnp.float32) ** shard_levels(streams_of[1], (NZ, NX, NY), ((0, 2), (1, 16)), -0.2, 0.2), 0.1, 0.35),
        "source": gaussian(streams_of[2], (NZ, NX, NY), 0.5, 3.0, ((0, 2), (1, 16)), jnp.float32),
        "soil_type": with_ends(jax.random.randint(streams_of[3], (NZ, NX, NY), 0, NSOIL), jax.random.fold_in(streams_of[3], 1), 0, NSOIL - 1).astype(jnp.int32),
        "soil_params": draw_soil_params(jax.random.fold_in(streams_of[5], 71), 0),
    }


step_time = 0.1
relax = 0.8
small_suction = 0.04

def soil_fields(soil_type, soil_params):
    fields = []
    for row_id in range(5):
        picked = jnp.zeros(soil_type.shape, jnp.float32)
        for kind_id in range(soil_params.shape[1]):
            picked = jnp.where(soil_type == kind_id, soil_params[row_id, kind_id], picked)
        fields.append(picked)
    return fields

def hydraulics(pressure, params):
    theta_r, theta_s, alpha_vg, shape_n, k_sat = params
    suction = jnp.sqrt(pressure * pressure + small_suction)
    shape_m = 1.0 - 1.0 / shape_n
    power_term = jnp.exp(shape_n * jnp.log(alpha_vg * suction))
    one_plus = 1.0 + power_term
    saturation = jnp.exp(-shape_m * jnp.log(one_plus))
    content = theta_r + (theta_s - theta_r) * saturation
    capacity = (theta_s - theta_r) * shape_m * shape_n * power_term * saturation / (one_plus * suction)
    ratio_term = power_term / one_plus
    conduct = k_sat * jnp.sqrt(saturation) * jnp.square(1.0 - jnp.exp(shape_m * jnp.log(ratio_term)))
    return (content, capacity, conduct)

def fine_balance(padded_head, padded_cond, content, capacity, theta_old, source):
    centre_h = padded_head[1:-1, 1:-1, 1:-1]
    centre_k = padded_cond[1:-1, 1:-1, 1:-1]
    inflow = jnp.zeros_like(centre_h)
    totals = jnp.zeros_like(centre_h)
    for axis_pos in range(3):
        for offset, weight in ((0, 1.0), (2, -1.0)):
            window = [slice(1, -1)] * 3
            window[axis_pos] = slice(offset, offset + centre_h.shape[axis_pos])
            near_h = padded_head[tuple(window)]
            near_k = padded_cond[tuple(window)]
            face_k = jnp.sqrt(centre_k * near_k)
            inflow = inflow + face_k * (near_h - centre_h)
            totals = totals + face_k
            if axis_pos == 0:
                inflow = inflow + weight * face_k
    balance = (content - theta_old) / step_time - inflow - source
    diagonal = capacity / step_time + totals
    return (balance, diagonal)

def coarse_balance(padded_head, padded_trans, storage, base):
    centre_h = padded_head[1:-1, 1:-1]
    centre_t = padded_trans[1:-1, 1:-1]
    inflow = jnp.zeros_like(centre_h)
    totals = jnp.zeros_like(centre_h)
    for axis_pos in range(2):
        for offset in (0, 2):
            window = [slice(1, -1)] * 2
            window[axis_pos] = slice(offset, offset + centre_h.shape[axis_pos])
            face_t = jnp.sqrt(centre_t * padded_trans[tuple(window)])
            inflow = inflow + face_t * (padded_head[tuple(window)] - centre_h)
            totals = totals + face_t
    balance = storage / step_time * (centre_h - base) - inflow
    diagonal = storage / step_time + totals
    return (balance, diagonal)

def reference(pressure, theta_old, source, soil_type, soil_params):
    params = soil_fields(soil_type, soil_params)
    content, capacity, conduct = hydraulics(pressure, params)
    balance, diagonal = fine_balance(jnp.pad(pressure, 1), jnp.pad(conduct, 1), content, capacity, theta_old, source)
    smoothed = pressure - relax * balance / diagonal
    content, capacity, conduct = hydraulics(smoothed, params)
    balance, diagonal = fine_balance(jnp.pad(smoothed, 1), jnp.pad(conduct, 1), content, capacity, theta_old, source)
    column_kh = lax.optimization_barrier(jnp.sum(conduct * smoothed, axis=0))
    column_k = lax.optimization_barrier(jnp.sum(conduct, axis=0))
    storage = lax.optimization_barrier(jnp.sum(capacity, axis=0))
    restricted = -lax.optimization_barrier(jnp.sum(balance, axis=0))
    column_rate = lax.optimization_barrier(jnp.sum(params[2], axis=0)) / NZ
    base = column_kh / column_k
    start_flow, start_diag = coarse_balance(jnp.pad(base, 1), jnp.pad(column_k, 1), storage, base)
    coarse_rhs = start_flow + restricted
    first = base - relax * (start_flow - coarse_rhs) / start_diag
    transmit = column_k * jnp.exp(column_rate * jnp.tanh(first - base))
    first_flow, first_diag = coarse_balance(jnp.pad(first, 1), jnp.pad(transmit, 1), storage, base)
    second = first - relax * (first_flow - coarse_rhs) / first_diag
    return (smoothed + (second - base)[None], second)
```

```python
import functools
import math

import jax
import jax.numpy as jnp
from jax import lax
from jax.experimental import pallas as pl
from jax.experimental.pallas import tpu as pltpu
from jax.sharding import PartitionSpec as P

INV_DT = 10.0
RELAX = 0.8
SMALL = 0.04
LOG2E = math.log2(math.e)
LANES = 128
F32 = jnp.float32

T_A, T_N, T_C, T_SK, T_D, T_R, T_CAP, T_RATE = range(8)


def whole(count):
    return [pl.BlockSpec(memory_space=pltpu.VMEM)] * count


def build_table(params_ref, tab_ref):
    kinds = params_ref.shape[1]
    theta_r = params_ref[0:1, :]
    theta_s = params_ref[1:2, :]
    alpha = params_ref[2:3, :]
    shape_n = params_ref[3:4, :]
    k_sat = params_ref[4:5, :]
    shape_m = 1.0 - 1.0 / shape_n
    spread = theta_s - theta_r
    rows = {
        T_A: shape_n * (jnp.log(alpha) * LOG2E),
        T_N: shape_n * (0.5 * LOG2E),
        T_C: shape_m * (-0.25 * LOG2E),
        T_SK: jnp.sqrt(k_sat),
        T_D: spread * INV_DT,
        T_R: theta_r * INV_DT,
        T_CAP: spread * shape_m * shape_n * INV_DT,
        T_RATE: alpha,
    }
    for row_id, value in rows.items():
        tab_ref[row_id, :, 0:kinds] = jnp.broadcast_to(value, (8, kinds))


def lookup(table, kinds):
    rows = []
    for r in range(0, kinds.shape[0], 8):
        cols = []
        for c in range(0, kinds.shape[1], LANES):
            cols.append(
                jnp.take_along_axis(
                    table, kinds[r : r + 8, c : c + LANES], axis=1, mode="promise_in_bounds"
                )
            )
        rows.append(jnp.concatenate(cols, axis=1))
    return rows[0] if len(rows) == 1 else jnp.concatenate(rows, axis=0)


def hydraulics(h, pa, pn, pc, psk):
    q = h * h + SMALL
    u = jnp.exp2(pa + pn * jnp.log(q))
    one_plus = 1.0 + u
    inv = 1.0 / one_plus
    ratio = u * inv
    quarter = jnp.exp2(pc * jnp.log(one_plus))
    w = jnp.exp2((-4.0 * pc) * jnp.log(ratio))
    kappa = psk * quarter * (1.0 - w)
    half = quarter * quarter
    return kappa, half * half, ratio * lax.rsqrt(q)


def kappa_only(h, kinds, tab_ref):
    return hydraulics(
        h,
        lookup(tab_ref[T_A], kinds),
        lookup(tab_ref[T_N], kinds),
        lookup(tab_ref[T_C], kinds),
        lookup(tab_ref[T_SK], kinds),
    )[0]


def pack_kernel(swap, p_ref, soil_ref, params_ref, fwd_ref, bwd_ref, *rest):
    layers, rows, _ = p_ref.shape
    tab_ref = rest[-1]
    build_table(params_ref, tab_ref)
    for out_ref, row in ((fwd_ref, rows - 1), (bwd_ref, 0)):
        h = p_ref[:, row, :]
        out_ref[0] = h
        out_ref[1] = kappa_only(h, soil_ref[:, row, :], tab_ref)
    if swap:
        spots = [jnp.where(lax.axis_index("depth") == 0, layers - 1, 0)]
    else:
        spots = [layers - 1, 0]
    for out_ref, spot in zip(rest[:-1], spots):
        h = p_ref[spot]
        out_ref[0] = h
        out_ref[1] = kappa_only(h, soil_ref[spot], tab_ref)


def row_iota(shape):
    return lax.broadcasted_iota(jnp.int32, shape, 0)


def lane_iota(shape):
    return lax.broadcasted_iota(jnp.int32, shape, 1)


def from_above(x, edge):
    return jnp.where(row_iota(x.shape) == 0, edge, pltpu.roll(x, 1, 0))


def from_below(x, edge):
    last = x.shape[0] - 1
    return jnp.where(row_iota(x.shape) == last, edge, pltpu.roll(x, last, 0))


def from_left(x):
    return jnp.where(lane_iota(x.shape) == 0, 0.0, pltpu.roll(x, 1, 1))


def from_right(x):
    last = x.shape[1] - 1
    return jnp.where(lane_iota(x.shape) == last, 0.0, pltpu.roll(x, last, 1))


def main_kernel(
    swap,
    p_ref,
    theta_ref,
    source_ref,
    soil_ref,
    params_ref,
    lo_ref,
    hi_ref,
    *rest,
):
    layers, rows, width = p_ref.shape
    if swap:
        vert_ref, rest = rest[0], rest[1:]
    else:
        top_ref, bottom_ref, rest = rest[0], rest[1], rest[2:]
    smooth_ref, sums_ref, fwd_ref, bwd_ref, tab_ref, kap_ref, head_ref = rest
    build_table(params_ref, tab_ref)

    if swap:
        d = lax.axis_index("depth")
        vert_k = vert_ref[1]
        kap_ref[0] = jnp.where(d == 0, 0.0, vert_k)
        kap_ref[layers + 1] = jnp.where(d == 0, vert_k, 0.0)
        head_ref[0] = vert_ref[0]
        head_ref[layers + 1] = vert_ref[0]
    else:
        kap_ref[0] = top_ref[1]
        kap_ref[layers + 1] = bottom_ref[1]
        head_ref[0] = top_ref[0]
        head_ref[layers + 1] = bottom_ref[0]

    def first(layer, carry):
        h = p_ref[layer]
        kap_ref[layer + 1] = kappa_only(h, soil_ref[layer], tab_ref)
        head_ref[layer + 1] = h
        return carry

    lax.fori_loop(0, layers, first, 0)

    def step(layer, carry):
        sum_kh, sum_k, sum_cap, sum_rest, sum_rate, flux_x, flux_y = carry
        kinds = soil_ref[layer]
        pa = lookup(tab_ref[T_A], kinds)
        pn = lookup(tab_ref[T_N], kinds)
        pc = lookup(tab_ref[T_C], kinds)
        psk = lookup(tab_ref[T_SK], kinds)
        pd = lookup(tab_ref[T_D], kinds)
        pr = lookup(tab_ref[T_R], kinds)
        pcap = lookup(tab_ref[T_CAP], kinds)
        rate = lookup(tab_ref[T_RATE], kinds)
        h = p_ref[layer]
        kap, sat, over = hydraulics(h, pa, pn, pc, psk)
        fixed = pr - INV_DT * theta_ref[layer] - source_ref[layer]
        k_up = kap_ref[layer]
        k_dn = kap_ref[layer + 2]
        lo_k = lo_ref[1, pl.ds(layer, 1), :]
        hi_k = hi_ref[1, pl.ds(layer, 1), :]
        lo_h = lo_ref[0, pl.ds(layer, 1), :]
        hi_h = hi_ref[0, pl.ds(layer, 1), :]
        g = kap * h
        sum_n = (
            k_up
            + k_dn
            + from_above(kap, lo_k)
            + from_below(kap, hi_k)
            + from_left(kap)
            + from_right(kap)
        )
        sum_g = (
            k_up * head_ref[layer]
            + k_dn * head_ref[layer + 2]
            + from_above(g, lo_k * lo_h)
            + from_below(g, hi_k * hi_h)
            + from_left(g)
            + from_right(g)
        )
        inflow = kap * (sum_g - h * sum_n + (k_up - k_dn))
        balance = pd * sat + fixed - inflow
        diagonal = pcap * sat * over + kap * sum_n
        h = h - RELAX * balance / diagonal
        smooth_ref[layer] = h

        kap, sat, over = hydraulics(h, pa, pn, pc, psk)
        cond = kap * kap
        flux_x = flux_x + kap * from_below(kap, 0.0) * (pltpu.roll(h, rows - 1, 0) - h)
        flux_y = flux_y + kap * from_right(kap) * (pltpu.roll(h, width - 1, 1) - h)
        fwd_ref[pl.ds(layer, 1), :] = h[rows - 1 : rows, :]
        fwd_ref[pl.ds(layers + layer, 1), :] = kap[rows - 1 : rows, :]
        bwd_ref[pl.ds(layer, 1), :] = h[0:1, :]
        bwd_ref[pl.ds(layers + layer, 1), :] = kap[0:1, :]
        return (
            sum_kh + cond * h,
            sum_k + cond,
            sum_cap + pcap * sat * over,
            sum_rest + (pd * sat + fixed),
            sum_rate + rate,
            flux_x,
            flux_y,
        )

    zero = jnp.zeros((rows, width), F32)
    sum_kh, sum_k, sum_cap, sum_rest, sum_rate, flux_x, flux_y = lax.fori_loop(
        0, layers, step, (zero,) * 7
    )
    restricted = (flux_x - from_above(flux_x, 0.0)) + (flux_y - from_left(flux_y)) - sum_rest
    for spot, value in enumerate((sum_kh, sum_k, sum_cap, restricted, sum_rate)):
        sums_ref[spot] = value
    at = 2 * layers
    for out_ref, edge, inner in ((fwd_ref, rows - 1, rows - 2), (bwd_ref, 0, 1)):
        tail = [
            sum_kh[edge : edge + 1],
            sum_k[edge : edge + 1],
            sum_kh[inner : inner + 1],
            sum_k[inner : inner + 1],
            sum_cap[edge : edge + 1],
            restricted[edge : edge + 1],
            sum_rate[edge : edge + 1],
            zero[0:1],
        ]
        out_ref[at : at + 8, :] = jnp.concatenate(tail, axis=0)


def edge_kernel(fwd_ref, bwd_ref, lo_ref, hi_ref, halo_ref):
    layers = (fwd_ref.shape[0] - 8) // 2
    at = 2 * layers
    fluxes = []
    for mine_ref, their_ref in ((bwd_ref, lo_ref), (fwd_ref, hi_ref)):
        flux = (
            mine_ref[layers:at, :]
            * their_ref[layers:at, :]
            * (their_ref[0:layers, :] - mine_ref[0:layers, :])
        )
        fluxes.append(jnp.sum(flux, axis=0, keepdims=True))
    lo = lo_ref[at : at + 8, :]
    hi = hi_ref[at : at + 8, :]
    for side, (block, flux) in enumerate(((lo, fluxes[0]), (hi, fluxes[1]))):
        spot = row_iota(block.shape)
        block = jnp.where(spot == 5, block - flux, block)
        halo_ref[side] = jnp.where(spot == 7, flux, block)


def coarse_kernel(
    depth_total, smooth_ref, sums_ref, their_sums_ref, halo_ref, their_halo_ref, out_ref, head_ref
):
    rows = smooth_ref.shape[1]
    kh, kk, cap, rest, rate = [sums_ref[i] + their_sums_ref[i] for i in range(5)]
    lo = halo_ref[0] + their_halo_ref[0]
    hi = halo_ref[1] + their_halo_ref[1]
    spot = row_iota(rest.shape)
    rest = jnp.where(spot == 0, rest + lo[7:8], rest)
    rest = jnp.where(spot == rows - 1, rest + hi[7:8], rest)

    def pair(i):
        return jnp.where(spot == 0, lo[i : i + 1], jnp.where(spot == rows - 1, hi[i : i + 1], 0.0))

    h_kh, h_k, o_kh, o_k, h_cap, h_rest, h_rate = [pair(i) for i in range(7)]
    edge_lane = lane_iota(rest.shape)

    def sides(x):
        return from_left(x) + from_right(x)

    base = kh / kk
    root = jnp.sqrt(kk)
    h_live = h_k > 0.0
    h_base = jnp.where(h_live, h_kh / jnp.where(h_live, h_k, 1.0), 0.0)
    h_root = jnp.sqrt(h_k)
    o_root = jnp.sqrt(o_k)

    def around(x, halo):
        return from_above(x, halo[0:1]), from_below(x, halo[rows - 1 : rows])

    def flow(head, halo_head, tau, halo_tau):
        tau_u, tau_d = around(tau, halo_tau)
        head_u, head_d = around(head, halo_head)
        tau_l, tau_r = from_left(tau), from_right(tau)
        head_l, head_r = from_left(head), from_right(head)
        inflow = (
            tau_u * (head_u - head)
            + tau_d * (head_d - head)
            + tau_l * (head_l - head)
            + tau_r * (head_r - head)
        )
        return tau * inflow, tau * (tau_u + tau_d + tau_l + tau_r)

    start_in, start_sum = flow(base, h_base, root, h_root)
    rhs = rest - start_in
    first = base + RELAX * rest / (cap + start_sum)
    h_diag = h_cap + h_root * (o_root + root + sides(h_root))
    h_first = h_base + jnp.where(h_live, RELAX * h_rest / jnp.where(h_live, h_diag, 1.0), 0.0)
    half = 0.5 / depth_total
    tau = root * jnp.exp(half * rate * jnp.tanh(first - base))
    h_tau = h_root * jnp.exp(half * h_rate * jnp.tanh(h_first - h_base))
    first_in, first_sum = flow(first, h_first, tau, h_tau)
    first_flow = cap * (first - base) - first_in
    second = first - RELAX * (first_flow - rhs) / (cap + first_sum)
    head_ref[...] = second
    shift = second - base
    out_ref[...] = smooth_ref[...] + shift[None]


def shards(pressure, theta_old, source, soil_type, soil_params):
    layers, rows, width = pressure.shape
    areas = lax.axis_size("area")
    depths = lax.axis_size("depth")
    swap = depths == 2
    forward = [(i, i + 1) for i in range(areas - 1)]
    backward = [(b, a) for a, b in forward]
    down = [(i, i + 1) for i in range(depths - 1)]
    up = [(b, a) for a, b in down]
    swapped = [(0, 1), (1, 0)]

    def shape(*dims):
        return jax.ShapeDtypeStruct(dims, F32)

    params = pltpu.CompilerParams(vmem_limit_bytes=48 << 20)
    tab = pltpu.VMEM((8, 8, LANES), F32)
    verts = 1 if swap else 2
    packed = pl.pallas_call(
        functools.partial(pack_kernel, swap),
        out_shape=[shape(2, layers, width)] * 2 + [shape(2, rows, width)] * verts,
        in_specs=whole(3),
        out_specs=whole(2 + verts),
        scratch_shapes=[tab],
        compiler_params=params,
        name="pack",
    )(pressure, soil_type, soil_params)
    lo = lax.ppermute(packed[0], "area", forward)
    hi = lax.ppermute(packed[1], "area", backward)
    if swap:
        vert = [lax.ppermute(packed[2], "depth", swapped)]
    else:
        vert = [lax.ppermute(packed[2], "depth", down), lax.ppermute(packed[3], "depth", up)]
    smooth, sums, fwd, bwd = pl.pallas_call(
        functools.partial(main_kernel, swap),
        out_shape=[
            shape(layers, rows, width),
            shape(5, rows, width),
            shape(2 * layers + 8, width),
            shape(2 * layers + 8, width),
        ],
        in_specs=whole(7 + verts),
        out_specs=whole(4),
        scratch_shapes=[
            tab,
            pltpu.VMEM((layers + 2, rows, width), F32),
            pltpu.VMEM((layers + 2, rows, width), F32),
        ],
        compiler_params=params,
        name="fine",
    )(pressure, theta_old, source, soil_type, soil_params, lo, hi, *vert)
    lo = lax.ppermute(fwd, "area", forward)
    hi = lax.ppermute(bwd, "area", backward)
    if swap:
        their_sums = lax.ppermute(sums, "depth", swapped)
    else:
        their_sums = lax.psum(sums, "depth") - sums
    halo = pl.pallas_call(
        edge_kernel,
        out_shape=shape(2, 8, width),
        in_specs=whole(4),
        out_specs=whole(1)[0],
        compiler_params=params,
        name="edge",
    )(fwd, bwd, lo, hi)
    if swap:
        their_halo = lax.ppermute(halo, "depth", swapped)
    else:
        their_halo = lax.psum(halo, "depth") - halo
    out, head = pl.pallas_call(
        functools.partial(coarse_kernel, layers * depths),
        out_shape=[shape(layers, rows, width), shape(rows, width)],
        in_specs=whole(5),
        out_specs=whole(2),
        compiler_params=params,
        name="coarse",
    )(smooth, sums, their_sums, halo, their_halo)
    return out, head


def solution(mesh):
    in_specs = (
        P("depth", "area", None),
        P("depth", "area", None),
        P("depth", "area", None),
        P("depth", "area", None),
        P(),
    )
    out_specs = (P("depth", "area", None), P("area", None))
    return jax.shard_map(shards, mesh=mesh, in_specs=in_specs, out_specs=out_specs, check_vma=False)
```

```python
import functools
import math

import jax
import jax.numpy as jnp
from jax import lax
from jax.experimental import pallas as pl
from jax.experimental.pallas import tpu as pltpu
from jax.sharding import PartitionSpec as P

INV_DT = 10.0
RELAX = 0.8
SMALL = 0.04
LOG2E = math.log2(math.e)
LANES = 128
F32 = jnp.float32

T_A, T_N, T_C, T_SK, T_D, T_R, T_CAP, T_RATE = range(8)


def whole(count):
    return [pl.BlockSpec(memory_space=pltpu.VMEM)] * count


def build_table(params_ref, tab_ref):
    kinds = params_ref.shape[1]
    theta_r = params_ref[0:1, :]
    theta_s = params_ref[1:2, :]
    alpha = params_ref[2:3, :]
    shape_n = params_ref[3:4, :]
    k_sat = params_ref[4:5, :]
    shape_m = 1.0 - 1.0 / shape_n
    spread = theta_s - theta_r
    rows = {
        T_A: shape_n * (jnp.log(alpha) * LOG2E),
        T_N: shape_n * (0.5 * LOG2E),
        T_C: shape_m * (-0.25 * LOG2E),
        T_SK: jnp.sqrt(k_sat),
        T_D: spread * INV_DT,
        T_R: theta_r * INV_DT,
        T_CAP: spread * shape_m * shape_n * INV_DT,
        T_RATE: alpha,
    }
    for row_id, value in rows.items():
        tab_ref[row_id, :, 0:kinds] = jnp.broadcast_to(value, (8, kinds))


def lookup(table, kinds):
    rows = []
    for r in range(0, kinds.shape[0], 8):
        cols = []
        for c in range(0, kinds.shape[1], LANES):
            cols.append(
                jnp.take_along_axis(
                    table, kinds[r : r + 8, c : c + LANES], axis=1, mode="promise_in_bounds"
                )
            )
        rows.append(jnp.concatenate(cols, axis=1))
    return rows[0] if len(rows) == 1 else jnp.concatenate(rows, axis=0)


def hydraulics(h, pa, pn, pc, psk):
    q = h * h + SMALL
    u = jnp.exp2(pa + pn * jnp.log(q))
    one_plus = 1.0 + u
    inv = 1.0 / one_plus
    ratio = u * inv
    quarter = jnp.exp2(pc * jnp.log(one_plus))
    w = jnp.exp2((-4.0 * pc) * jnp.log(ratio))
    kappa = psk * quarter * (1.0 - w)
    half = quarter * quarter
    return kappa, half * half, ratio * lax.rsqrt(q)


def kappa_only(h, kinds, tab_ref):
    return hydraulics(
        h,
        lookup(tab_ref[T_A], kinds),
        lookup(tab_ref[T_N], kinds),
        lookup(tab_ref[T_C], kinds),
        lookup(tab_ref[T_SK], kinds),
    )[0]


def even_area():
    return lax.rem(lax.axis_index("area"), 2) == 0


def pack_kernel(swap, p_ref, soil_ref, params_ref, even_ref, odd_ref, *rest):
    layers, rows, _ = p_ref.shape
    tab_ref = rest[-1]
    build_table(params_ref, tab_ref)
    even = even_area()
    low_h, high_h = p_ref[:, 0, :], p_ref[:, rows - 1, :]
    low_k = kappa_only(low_h, soil_ref[:, 0, :], tab_ref)
    high_k = kappa_only(high_h, soil_ref[:, rows - 1, :], tab_ref)
    even_ref[0] = jnp.where(even, high_h, low_h)
    even_ref[1] = jnp.where(even, high_k, low_k)
    odd_ref[0] = jnp.where(even, low_h, high_h)
    odd_ref[1] = jnp.where(even, low_k, high_k)
    if swap:
        spots = [jnp.where(lax.axis_index("depth") == 0, layers - 1, 0)]
    else:
        spots = [layers - 1, 0]
    for out_ref, spot in zip(rest[:-1], spots):
        h = p_ref[spot]
        out_ref[0] = h
        out_ref[1] = kappa_only(h, soil_ref[spot], tab_ref)


def row_iota(shape):
    return lax.broadcasted_iota(jnp.int32, shape, 0)


def lane_iota(shape):
    return lax.broadcasted_iota(jnp.int32, shape, 1)


def from_above(x, edge):
    return jnp.where(row_iota(x.shape) == 0, edge, pltpu.roll(x, 1, 0))


def from_below(x, edge):
    last = x.shape[0] - 1
    return jnp.where(row_iota(x.shape) == last, edge, pltpu.roll(x, last, 0))


def from_left(x):
    return jnp.where(lane_iota(x.shape) == 0, 0.0, pltpu.roll(x, 1, 1))


def from_right(x):
    last = x.shape[1] - 1
    return jnp.where(lane_iota(x.shape) == last, 0.0, pltpu.roll(x, last, 1))


def main_kernel(
    swap,
    p_ref,
    theta_ref,
    source_ref,
    soil_ref,
    params_ref,
    from_even_ref,
    from_odd_ref,
    *rest,
):
    layers, rows, width = p_ref.shape
    if swap:
        vert_ref, rest = rest[0], rest[1:]
    else:
        top_ref, bottom_ref, rest = rest[0], rest[1], rest[2:]
    smooth_ref, sums_ref, to_even_ref, to_odd_ref, tab_ref, kap_ref, head_ref = rest
    build_table(params_ref, tab_ref)
    even = even_area()

    if swap:
        d = lax.axis_index("depth")
        vert_k = vert_ref[1]
        kap_ref[0] = jnp.where(d == 0, 0.0, vert_k)
        kap_ref[layers + 1] = jnp.where(d == 0, vert_k, 0.0)
        head_ref[0] = vert_ref[0]
        head_ref[layers + 1] = vert_ref[0]
    else:
        kap_ref[0] = top_ref[1]
        kap_ref[layers + 1] = bottom_ref[1]
        head_ref[0] = top_ref[0]
        head_ref[layers + 1] = bottom_ref[0]

    def first(layer, carry):
        h = p_ref[layer]
        kap_ref[layer + 1] = kappa_only(h, soil_ref[layer], tab_ref)
        head_ref[layer + 1] = h
        return carry

    lax.fori_loop(0, layers, first, 0)

    def step(layer, carry):
        sum_kh, sum_k, sum_cap, sum_rest, sum_rate, flux_x, flux_y = carry
        kinds = soil_ref[layer]
        pa = lookup(tab_ref[T_A], kinds)
        pn = lookup(tab_ref[T_N], kinds)
        pc = lookup(tab_ref[T_C], kinds)
        psk = lookup(tab_ref[T_SK], kinds)
        pd = lookup(tab_ref[T_D], kinds)
        pr = lookup(tab_ref[T_R], kinds)
        pcap = lookup(tab_ref[T_CAP], kinds)
        rate = lookup(tab_ref[T_RATE], kinds)
        h = p_ref[layer]
        kap, sat, over = hydraulics(h, pa, pn, pc, psk)
        fixed = pr - INV_DT * theta_ref[layer] - source_ref[layer]
        k_up = kap_ref[layer]
        k_dn = kap_ref[layer + 2]
        even_k = from_even_ref[1, pl.ds(layer, 1), :]
        odd_k = from_odd_ref[1, pl.ds(layer, 1), :]
        even_h = from_even_ref[0, pl.ds(layer, 1), :]
        odd_h = from_odd_ref[0, pl.ds(layer, 1), :]
        lo_k = jnp.where(even, odd_k, even_k)
        hi_k = jnp.where(even, even_k, odd_k)
        lo_h = jnp.where(even, odd_h, even_h)
        hi_h = jnp.where(even, even_h, odd_h)
        g = kap * h
        sum_n = (
            k_up
            + k_dn
            + from_above(kap, lo_k)
            + from_below(kap, hi_k)
            + from_left(kap)
            + from_right(kap)
        )
        sum_g = (
            k_up * head_ref[layer]
            + k_dn * head_ref[layer + 2]
            + from_above(g, lo_k * lo_h)
            + from_below(g, hi_k * hi_h)
            + from_left(g)
            + from_right(g)
        )
        inflow = kap * (sum_g - h * sum_n + (k_up - k_dn))
        balance = pd * sat + fixed - inflow
        diagonal = pcap * sat * over + kap * sum_n
        h = h - RELAX * balance / diagonal
        smooth_ref[layer] = h

        kap, sat, over = hydraulics(h, pa, pn, pc, psk)
        cond = kap * kap
        flux_x = flux_x + kap * from_below(kap, 0.0) * (pltpu.roll(h, rows - 1, 0) - h)
        flux_y = flux_y + kap * from_right(kap) * (pltpu.roll(h, width - 1, 1) - h)
        for at, value in ((0, h), (layers, kap)):
            low, high = value[0:1, :], value[rows - 1 : rows, :]
            to_even_ref[pl.ds(at + layer, 1), :] = jnp.where(even, high, low)
            to_odd_ref[pl.ds(at + layer, 1), :] = jnp.where(even, low, high)
        return (
            sum_kh + cond * h,
            sum_k + cond,
            sum_cap + pcap * sat * over,
            sum_rest + (pd * sat + fixed),
            sum_rate + rate,
            flux_x,
            flux_y,
        )

    zero = jnp.zeros((rows, width), F32)
    sum_kh, sum_k, sum_cap, sum_rest, sum_rate, flux_x, flux_y = lax.fori_loop(
        0, layers, step, (zero,) * 7
    )
    restricted = (flux_x - from_above(flux_x, 0.0)) + (flux_y - from_left(flux_y)) - sum_rest
    for spot, value in enumerate((sum_kh, sum_k, sum_cap, restricted, sum_rate)):
        sums_ref[spot] = value
    at = 2 * layers
    tails = []
    for edge, inner in ((rows - 1, rows - 2), (0, 1)):
        tail = [
            sum_kh[edge : edge + 1],
            sum_k[edge : edge + 1],
            sum_kh[inner : inner + 1],
            sum_k[inner : inner + 1],
            sum_cap[edge : edge + 1],
            restricted[edge : edge + 1],
            sum_rate[edge : edge + 1],
            zero[0:1],
        ]
        tails.append(jnp.concatenate(tail, axis=0))
    high, low = tails
    to_even_ref[at : at + 8, :] = jnp.where(even, high, low)
    to_odd_ref[at : at + 8, :] = jnp.where(even, low, high)


def edge_kernel(to_even_ref, to_odd_ref, from_even_ref, from_odd_ref, halo_ref):
    layers = (to_even_ref.shape[0] - 8) // 2
    at = 2 * layers
    for side, (mine_ref, their_ref) in enumerate(
        ((to_even_ref, from_even_ref), (to_odd_ref, from_odd_ref))
    ):
        flux = (
            mine_ref[layers:at, :]
            * their_ref[layers:at, :]
            * (their_ref[0:layers, :] - mine_ref[0:layers, :])
        )
        flux = jnp.sum(flux, axis=0, keepdims=True)
        block = their_ref[at : at + 8, :]
        spot = row_iota(block.shape)
        block = jnp.where(spot == 5, block - flux, block)
        halo_ref[side] = jnp.where(spot == 7, flux, block)


def coarse_kernel(
    depth_total, smooth_ref, sums_ref, their_sums_ref, halo_ref, their_halo_ref, out_ref, head_ref
):
    rows = smooth_ref.shape[1]
    kh, kk, cap, rest, rate = [sums_ref[i] + their_sums_ref[i] for i in range(5)]
    by_even = halo_ref[0] + their_halo_ref[0]
    by_odd = halo_ref[1] + their_halo_ref[1]
    even = even_area()
    lo = jnp.where(even, by_odd, by_even)
    hi = jnp.where(even, by_even, by_odd)
    spot = row_iota(rest.shape)
    rest = jnp.where(spot == 0, rest + lo[7:8], rest)
    rest = jnp.where(spot == rows - 1, rest + hi[7:8], rest)

    def pair(i):
        return jnp.where(spot == 0, lo[i : i + 1], jnp.where(spot == rows - 1, hi[i : i + 1], 0.0))

    h_kh, h_k, o_kh, o_k, h_cap, h_rest, h_rate = [pair(i) for i in range(7)]
    edge_lane = lane_iota(rest.shape)

    def sides(x):
        return from_left(x) + from_right(x)

    base = kh / kk
    root = jnp.sqrt(kk)
    h_live = h_k > 0.0
    h_base = jnp.where(h_live, h_kh / jnp.where(h_live, h_k, 1.0), 0.0)
    h_root = jnp.sqrt(h_k)
    o_root = jnp.sqrt(o_k)

    def around(x, halo):
        return from_above(x, halo[0:1]), from_below(x, halo[rows - 1 : rows])

    def flow(head, halo_head, tau, halo_tau):
        tau_u, tau_d = around(tau, halo_tau)
        head_u, head_d = around(head, halo_head)
        tau_l, tau_r = from_left(tau), from_right(tau)
        head_l, head_r = from_left(head), from_right(head)
        inflow = (
            tau_u * (head_u - head)
            + tau_d * (head_d - head)
            + tau_l * (head_l - head)
            + tau_r * (head_r - head)
        )
        return tau * inflow, tau * (tau_u + tau_d + tau_l + tau_r)

    start_in, start_sum = flow(base, h_base, root, h_root)
    rhs = rest - start_in
    first = base + RELAX * rest / (cap + start_sum)
    h_diag = h_cap + h_root * (o_root + root + sides(h_root))
    h_first = h_base + jnp.where(h_live, RELAX * h_rest / jnp.where(h_live, h_diag, 1.0), 0.0)
    half = 0.5 / depth_total
    tau = root * jnp.exp(half * rate * jnp.tanh(first - base))
    h_tau = h_root * jnp.exp(half * h_rate * jnp.tanh(h_first - h_base))
    first_in, first_sum = flow(first, h_first, tau, h_tau)
    first_flow = cap * (first - base) - first_in
    second = first - RELAX * (first_flow - rhs) / (cap + first_sum)
    head_ref[...] = second
    shift = second - base
    out_ref[...] = smooth_ref[...] + shift[None]


def shards(pressure, theta_old, source, soil_type, soil_params):
    layers, rows, width = pressure.shape
    areas = lax.axis_size("area")
    depths = lax.axis_size("depth")
    swap = depths == 2
    even_pairs = [p for i in range(0, areas - 1, 2) for p in ((i, i + 1), (i + 1, i))]
    odd_pairs = [p for i in range(1, areas - 1, 2) for p in ((i, i + 1), (i + 1, i))]
    down = [(i, i + 1) for i in range(depths - 1)]
    up = [(b, a) for a, b in down]
    swapped = [(0, 1), (1, 0)]

    def shape(*dims):
        return jax.ShapeDtypeStruct(dims, F32)

    params = pltpu.CompilerParams(vmem_limit_bytes=48 << 20)
    tab = pltpu.VMEM((8, 8, LANES), F32)
    verts = 1 if swap else 2
    packed = pl.pallas_call(
        functools.partial(pack_kernel, swap),
        out_shape=[shape(2, layers, width)] * 2 + [shape(2, rows, width)] * verts,
        in_specs=whole(3),
        out_specs=whole(2 + verts),
        scratch_shapes=[tab],
        compiler_params=params,
        name="pack",
    )(pressure, soil_type, soil_params)
    from_even = lax.ppermute(packed[0], "area", even_pairs)
    from_odd = lax.ppermute(packed[1], "area", odd_pairs)
    if swap:
        vert = [lax.ppermute(packed[2], "depth", swapped)]
    else:
        vert = [lax.ppermute(packed[2], "depth", down), lax.ppermute(packed[3], "depth", up)]
    smooth, sums, to_even, to_odd = pl.pallas_call(
        functools.partial(main_kernel, swap),
        out_shape=[
            shape(layers, rows, width),
            shape(5, rows, width),
            shape(2 * layers + 8, width),
            shape(2 * layers + 8, width),
        ],
        in_specs=whole(7 + verts),
        out_specs=whole(4),
        scratch_shapes=[
            tab,
            pltpu.VMEM((layers + 2, rows, width), F32),
            pltpu.VMEM((layers + 2, rows, width), F32),
        ],
        compiler_params=params,
        name="fine",
    )(pressure, theta_old, source, soil_type, soil_params, from_even, from_odd, *vert)
    from_even = lax.ppermute(to_even, "area", even_pairs)
    from_odd = lax.ppermute(to_odd, "area", odd_pairs)
    if swap:
        their_sums = lax.ppermute(sums, "depth", swapped)
    else:
        sums, their_sums = lax.psum(sums, "depth"), jnp.zeros_like(sums)
    halo = pl.pallas_call(
        edge_kernel,
        out_shape=shape(2, 8, width),
        in_specs=whole(4),
        out_specs=whole(1)[0],
        compiler_params=params,
        name="edge",
    )(to_even, to_odd, from_even, from_odd)
    if swap:
        their_halo = lax.ppermute(halo, "depth", swapped)
    else:
        halo, their_halo = lax.psum(halo, "depth"), jnp.zeros_like(halo)
    out, head = pl.pallas_call(
        functools.partial(coarse_kernel, layers * depths),
        out_shape=[shape(layers, rows, width), shape(rows, width)],
        in_specs=whole(5),
        out_specs=whole(2),
        compiler_params=params,
        name="coarse",
    )(smooth, sums, their_sums, halo, their_halo)
    return out, head


def solution(mesh):
    in_specs = (
        P("depth", "area", None),
        P("depth", "area", None),
        P("depth", "area", None),
        P("depth", "area", None),
        P(),
    )
    out_specs = (P("depth", "area", None), P("area", None))
    return jax.shard_map(shards, mesh=mesh, in_specs=in_specs, out_specs=out_specs, check_vma=False)
```

```python
import functools
import math

import jax
import jax.numpy as jnp
from jax import lax
from jax.experimental import pallas as pl
from jax.experimental.pallas import tpu as pltpu
from jax.sharding import PartitionSpec as P

INV_DT = 10.0
RELAX = 0.8
SMALL = 0.04
LOG2E = math.log2(math.e)
LANES = 128
F32 = jnp.float32

T_A, T_N, T_SK, T_D, T_R = range(5)


def whole(count):
    return [pl.BlockSpec(memory_space=pltpu.VMEM)] * count


def build_table(params_ref):
    alpha = params_ref[2:3, :]
    return {
        T_A: jnp.log(alpha) * LOG2E,
        T_N: params_ref[3:4, :],
        T_SK: jnp.sqrt(params_ref[4:5, :]),
        T_D: (params_ref[1:2, :] - params_ref[0:1, :]) * INV_DT,
        T_R: params_ref[0:1, :] * INV_DT,
    }


def gather(row, kinds):
    table = jnp.broadcast_to(jnp.pad(row, ((0, 0), (0, LANES - row.shape[1]))), (8, LANES))
    rows = []
    for r in range(0, kinds.shape[0], 8):
        cols = []
        for c in range(0, kinds.shape[1], LANES):
            cols.append(
                jnp.take_along_axis(
                    table, kinds[r : r + 8, c : c + LANES], axis=1, mode="promise_in_bounds"
                )
            )
        rows.append(jnp.concatenate(cols, axis=1))
    return rows[0] if len(rows) == 1 else jnp.concatenate(rows, axis=0)


def spread_table(table, tab_ref):
    for row_id, row in table.items():
        for kind in range(row.shape[1]):
            tab_ref[row_id, kind] = jnp.broadcast_to(row[:, kind : kind + 1], (8, LANES))


def pick(tab_ref, row_id, bits, width):
    level = [
        jnp.concatenate([tab_ref[row_id, kind]] * (width // LANES), axis=1)
        for kind in range(tab_ref.shape[1])
    ]
    for bit in bits:
        pairs = [
            jnp.where(bit, level[i + 1], level[i]) for i in range(0, len(level) - 1, 2)
        ]
        level = pairs + ([level[-1]] if len(level) % 2 else [])
    return level[0]


def type_bits(kinds, count):
    return [(kinds & (1 << i)) != 0 for i in range((count - 1).bit_length())]


def hydraulics(h, pa, pn, psk):
    pc = (1.0 / pn - 1.0) * (0.25 * LOG2E)
    q = h * h + SMALL
    u = jnp.exp2(pn * (pa + (0.5 * LOG2E) * jnp.log(q)))
    one_plus = 1.0 + u
    inv = 1.0 / one_plus
    ratio = u * inv
    quarter = jnp.exp2(pc * jnp.log(one_plus))
    w = jnp.exp2((-4.0 * pc) * jnp.log(ratio))
    kappa = psk * quarter * (1.0 - w)
    half = quarter * quarter
    return kappa, half * half, ratio * lax.rsqrt(q)


def kappa_by_gather(h, kinds, table):
    return hydraulics(
        h, gather(table[T_A], kinds), gather(table[T_N], kinds), gather(table[T_SK], kinds)
    )[0]


def even_area():
    return lax.rem(lax.axis_index("area"), 2) == 0


def pack_kernel(swap, p_ref, soil_ref, params_ref, even_ref, odd_ref, *rest):
    layers, rows, _ = p_ref.shape
    count = 1 if swap else 2
    vert_refs = rest[:count]
    p_buf, soil_buf, vert_p, vert_soil, params_buf, sems = rest[count:]
    even = even_area()
    if swap:
        spots = [jnp.where(lax.axis_index("depth") == 0, layers - 1, 0)]
    else:
        spots = [layers - 1, 0]
    copies = [(params_ref, params_buf)]
    for side, row in enumerate((0, rows - 1)):
        copies.append((p_ref.at[:, row, :], p_buf.at[side]))
        copies.append((soil_ref.at[:, row, :], soil_buf.at[side]))
    for side, spot in enumerate(spots):
        copies.append((p_ref.at[spot], vert_p.at[side]))
        copies.append((soil_ref.at[spot], vert_soil.at[side]))
    copies = [
        pltpu.make_async_copy(source, target, sems.at[i])
        for i, (source, target) in enumerate(copies)
    ]
    for copy in copies:
        copy.start()
    for copy in copies:
        copy.wait()
    table = build_table(params_buf)
    low_h, high_h = p_buf[0], p_buf[1]
    low_k = kappa_by_gather(low_h, soil_buf[0], table)
    high_k = kappa_by_gather(high_h, soil_buf[1], table)
    even_ref[0] = jnp.where(even, high_h, low_h)
    even_ref[1] = jnp.where(even, high_k, low_k)
    odd_ref[0] = jnp.where(even, low_h, high_h)
    odd_ref[1] = jnp.where(even, low_k, high_k)
    for side, out_ref in enumerate(vert_refs):
        h = vert_p[side]
        out_ref[0] = h
        out_ref[1] = kappa_by_gather(h, vert_soil[side], table)


def row_iota(shape):
    return lax.broadcasted_iota(jnp.int32, shape, 0)


def lane_iota(shape):
    return lax.broadcasted_iota(jnp.int32, shape, 1)


def from_above(x, edge):
    return jnp.where(row_iota(x.shape) == 0, edge, pltpu.roll(x, 1, 0))


def from_below(x, edge):
    last = x.shape[0] - 1
    return jnp.where(row_iota(x.shape) == last, edge, pltpu.roll(x, last, 0))


def from_left(x):
    return jnp.where(lane_iota(x.shape) == 0, 0.0, pltpu.roll(x, 1, 1))


def from_right(x):
    last = x.shape[1] - 1
    return jnp.where(lane_iota(x.shape) == last, 0.0, pltpu.roll(x, last, 1))


def local_kernel(
    p_hbm,
    theta_hbm,
    source_hbm,
    soil_hbm,
    params_hbm,
    kept_ref,
    kap_ref,
    p_ref,
    sums_ref,
    theta_ref,
    source_ref,
    soil_ref,
    params_ref,
    tab_ref,
    sems,
    params_sem,
):
    layers, rows, width = p_hbm.shape
    chunks = sems.shape[1]
    part = layers // chunks
    pairs = (
        (soil_hbm, soil_ref),
        (p_hbm, p_ref),
        (theta_hbm, theta_ref),
        (source_hbm, source_ref),
    )

    def copy(i, chunk):
        at = pl.ds(chunk * part, part)
        return pltpu.make_async_copy(pairs[i][0].at[at], pairs[i][1].at[at], sems.at[i, chunk])

    params_copy = pltpu.make_async_copy(params_hbm, params_ref, params_sem)
    params_copy.start()
    for chunk in range(chunks):
        for i in range(4):
            copy(i, chunk).start()
    params_copy.wait()
    kind_count = params_ref.shape[1]
    spread_table(build_table(params_ref), tab_ref)

    def step(layer, carry):
        sum_fixed, sum_rate = carry
        bits = type_bits(soil_ref[layer], kind_count)
        pa, pn, psk, pd, pr = [pick(tab_ref, i, bits, width) for i in range(5)]
        h = p_ref[layer]
        kap, sat, over = hydraulics(h, pa, pn, psk)
        fixed = pr - INV_DT * theta_ref[layer] - source_ref[layer]
        k_l, k_r = from_left(kap), from_right(kap)
        k_u, k_d = from_above(kap, 0.0), from_below(kap, 0.0)
        inflow = (
            k_l * (pltpu.roll(h, 1, 1) - h)
            + k_r * (pltpu.roll(h, width - 1, 1) - h)
            + k_u * (pltpu.roll(h, 1, 0) - h)
            + k_d * (pltpu.roll(h, rows - 1, 0) - h)
        )
        kap_ref[layer] = kap
        kept_ref[0, layer] = pd * sat + fixed - kap * inflow
        kept_ref[1, layer] = pd * (pn - 1.0) * sat * over + kap * ((k_l + k_r) + (k_u + k_d))
        kept_ref[2, layer] = pa
        kept_ref[3, layer] = pn
        kept_ref[4, layer] = psk
        kept_ref[5, layer] = pd
        return sum_fixed + fixed, sum_rate + jnp.exp2(pa)

    def part_step(chunk, carry):
        for i in range(4):
            copy(i, chunk).wait()
        return lax.fori_loop(chunk * part, (chunk + 1) * part, step, carry)

    zero = jnp.zeros((rows, width), F32)
    sum_fixed, sum_rate = lax.fori_loop(0, chunks, part_step, (zero, zero))
    sums_ref[0] = sum_fixed
    sums_ref[1] = sum_rate


def fine_kernel(swap, p_ref, kept_ref, kap_ref, local_ref, from_even_ref, from_odd_ref, *rest):
    layers, rows, width = p_ref.shape
    if swap:
        vert_ref, rest = rest[0], rest[1:]
    else:
        top_ref, bottom_ref, rest = rest[0], rest[1], rest[2:]
    smooth_ref, sums_ref, to_even_ref, to_odd_ref = rest
    even = even_area()
    spot = row_iota((rows, width))
    is_first, is_last = spot == 0, spot == rows - 1

    if swap:
        at_top = lax.axis_index("depth") == 0
        top_k = jnp.where(at_top, 0.0, vert_ref[1])
        bottom_k = jnp.where(at_top, vert_ref[1], 0.0)
        top_h = bottom_h = vert_ref[0]
    else:
        top_h, top_k = top_ref[0], top_ref[1]
        bottom_h, bottom_k = bottom_ref[0], bottom_ref[1]

    def step(layer, carry):
        sum_kh, sum_k, sum_cap, sum_sat, flux_x, flux_y = carry
        h = p_ref[layer]
        above, below = jnp.maximum(layer - 1, 0), jnp.minimum(layer + 1, layers - 1)
        k_u = jnp.where(layer == 0, top_k, kap_ref[above])
        h_u = jnp.where(layer == 0, top_h, p_ref[above])
        k_d = jnp.where(layer == layers - 1, bottom_k, kap_ref[below])
        h_d = jnp.where(layer == layers - 1, bottom_h, p_ref[below])
        even_k = from_even_ref[1, pl.ds(layer, 1), :]
        odd_k = from_odd_ref[1, pl.ds(layer, 1), :]
        even_h = from_even_ref[0, pl.ds(layer, 1), :]
        odd_h = from_odd_ref[0, pl.ds(layer, 1), :]
        lo_k = jnp.where(even, odd_k, even_k)
        hi_k = jnp.where(even, even_k, odd_k)
        lo_h = jnp.where(even, odd_h, even_h)
        hi_h = jnp.where(even, even_h, odd_h)
        side_k = jnp.where(is_first, lo_k, jnp.where(is_last, hi_k, 0.0))
        side_h = jnp.where(is_first, lo_h, hi_h)
        kap = kap_ref[layer]
        inflow = k_u * (h_u - h + 1.0) + k_d * (h_d - h - 1.0) + side_k * (side_h - h)
        balance = kept_ref[0, layer] - kap * inflow
        diagonal = kept_ref[1, layer] + kap * (k_u + k_d + side_k)
        h = h - RELAX * balance / diagonal
        smooth_ref[layer] = h

        pn = kept_ref[3, layer]
        pd = kept_ref[5, layer]
        kap, sat, over = hydraulics(h, kept_ref[2, layer], pn, kept_ref[4, layer])
        cond = kap * kap
        flux_x = flux_x + kap * from_below(kap, 0.0) * (pltpu.roll(h, rows - 1, 0) - h)
        flux_y = flux_y + kap * from_right(kap) * (pltpu.roll(h, width - 1, 1) - h)
        for at, value in ((0, h), (layers, kap)):
            low, high = value[0:1, :], value[rows - 1 : rows, :]
            to_even_ref[pl.ds(at + layer, 1), :] = jnp.where(even, high, low)
            to_odd_ref[pl.ds(at + layer, 1), :] = jnp.where(even, low, high)
        return (
            sum_kh + cond * h,
            sum_k + cond,
            sum_cap + pd * (pn - 1.0) * sat * over,
            sum_sat + pd * sat,
            flux_x,
            flux_y,
        )

    zero = jnp.zeros((rows, width), F32)
    sum_kh, sum_k, sum_cap, sum_sat, flux_x, flux_y = lax.fori_loop(0, layers, step, (zero,) * 6)
    sum_rate = local_ref[1]
    restricted = (
        (flux_x - from_above(flux_x, 0.0)) + (flux_y - from_left(flux_y)) - sum_sat - local_ref[0]
    )
    for at, value in enumerate((sum_kh, sum_k, sum_cap, restricted, sum_rate)):
        sums_ref[at] = value
    at = 2 * layers
    tails = []
    for edge, inner in ((rows - 1, rows - 2), (0, 1)):
        tail = [
            sum_kh[edge : edge + 1],
            sum_k[edge : edge + 1],
            sum_kh[inner : inner + 1],
            sum_k[inner : inner + 1],
            sum_cap[edge : edge + 1],
            restricted[edge : edge + 1],
            sum_rate[edge : edge + 1],
            zero[0:1],
        ]
        tails.append(jnp.concatenate(tail, axis=0))
    high, low = tails
    to_even_ref[at : at + 8, :] = jnp.where(even, high, low)
    to_odd_ref[at : at + 8, :] = jnp.where(even, low, high)


def edge_kernel(to_even_ref, to_odd_ref, from_even_ref, from_odd_ref, halo_ref):
    layers = (to_even_ref.shape[0] - 8) // 2
    at = 2 * layers
    for side, (mine_ref, their_ref) in enumerate(
        ((to_even_ref, from_even_ref), (to_odd_ref, from_odd_ref))
    ):
        flux = (
            mine_ref[layers:at, :]
            * their_ref[layers:at, :]
            * (their_ref[0:layers, :] - mine_ref[0:layers, :])
        )
        flux = jnp.sum(flux, axis=0, keepdims=True)
        block = their_ref[at : at + 8, :]
        spot = row_iota(block.shape)
        block = jnp.where(spot == 5, block - flux, block)
        halo_ref[side] = jnp.where(spot == 7, flux, block)


def coarse_kernel(
    depth_total, smooth_ref, sums_ref, their_sums_ref, halo_ref, their_halo_ref, out_ref, head_ref
):
    rows = smooth_ref.shape[1]
    kh, kk, cap, rest, rate = [sums_ref[i] + their_sums_ref[i] for i in range(5)]
    by_even = halo_ref[0] + their_halo_ref[0]
    by_odd = halo_ref[1] + their_halo_ref[1]
    even = even_area()
    lo = jnp.where(even, by_odd, by_even)
    hi = jnp.where(even, by_even, by_odd)
    spot = row_iota(rest.shape)
    rest = jnp.where(spot == 0, rest + lo[7:8], rest)
    rest = jnp.where(spot == rows - 1, rest + hi[7:8], rest)

    def pair(i):
        return jnp.where(spot == 0, lo[i : i + 1], jnp.where(spot == rows - 1, hi[i : i + 1], 0.0))

    h_kh, h_k, o_kh, o_k, h_cap, h_rest, h_rate = [pair(i) for i in range(7)]
    edge_lane = lane_iota(rest.shape)

    def sides(x):
        return from_left(x) + from_right(x)

    base = kh / kk
    root = jnp.sqrt(kk)
    h_live = h_k > 0.0
    h_base = jnp.where(h_live, h_kh / jnp.where(h_live, h_k, 1.0), 0.0)
    h_root = jnp.sqrt(h_k)
    o_root = jnp.sqrt(o_k)

    def around(x, halo):
        return from_above(x, halo[0:1]), from_below(x, halo[rows - 1 : rows])

    def flow(head, halo_head, tau, halo_tau):
        tau_u, tau_d = around(tau, halo_tau)
        head_u, head_d = around(head, halo_head)
        tau_l, tau_r = from_left(tau), from_right(tau)
        head_l, head_r = from_left(head), from_right(head)
        inflow = (
            tau_u * (head_u - head)
            + tau_d * (head_d - head)
            + tau_l * (head_l - head)
            + tau_r * (head_r - head)
        )
        return tau * inflow, tau * (tau_u + tau_d + tau_l + tau_r)

    start_in, start_sum = flow(base, h_base, root, h_root)
    rhs = rest - start_in
    first = base + RELAX * rest / (cap + start_sum)
    h_diag = h_cap + h_root * (o_root + root + sides(h_root))
    h_first = h_base + jnp.where(h_live, RELAX * h_rest / jnp.where(h_live, h_diag, 1.0), 0.0)
    half = 0.5 / depth_total
    tau = root * jnp.exp(half * rate * jnp.tanh(first - base))
    h_tau = h_root * jnp.exp(half * h_rate * jnp.tanh(h_first - h_base))
    first_in, first_sum = flow(first, h_first, tau, h_tau)
    first_flow = cap * (first - base) - first_in
    second = first - RELAX * (first_flow - rhs) / (cap + first_sum)
    head_ref[...] = second
    shift = second - base
    out_ref[...] = smooth_ref[...] + shift[None]


def shards(pressure, theta_old, source, soil_type, soil_params):
    layers, rows, width = pressure.shape
    areas = lax.axis_size("area")
    depths = lax.axis_size("depth")
    swap = depths == 2
    even_pairs = [p for i in range(0, areas - 1, 2) for p in ((i, i + 1), (i + 1, i))]
    odd_pairs = [p for i in range(1, areas - 1, 2) for p in ((i, i + 1), (i + 1, i))]
    down = [(i, i + 1) for i in range(depths - 1)]
    up = [(b, a) for a, b in down]
    swapped = [(0, 1), (1, 0)]

    def shape(*dims):
        return jax.ShapeDtypeStruct(dims, F32)

    params = pltpu.CompilerParams(vmem_limit_bytes=48 << 20)
    verts = 1 if swap else 2
    kind_count = soil_params.shape[1]
    in_hbm = [
        pltpu.with_memory_space_constraint(x, pltpu.HBM)
        for x in (pressure, theta_old, source, soil_type, soil_params)
    ]
    packed = pl.pallas_call(
        functools.partial(pack_kernel, swap),
        out_shape=[shape(2, layers, width)] * 2 + [shape(2, rows, width)] * verts,
        in_specs=[pl.BlockSpec(memory_space=pltpu.HBM)] * 3,
        out_specs=whole(2 + verts),
        scratch_shapes=[
            pltpu.VMEM((2, layers, width), F32),
            pltpu.VMEM((2, layers, width), jnp.int32),
            pltpu.VMEM((verts, rows, width), F32),
            pltpu.VMEM((verts, rows, width), jnp.int32),
            pltpu.VMEM(soil_params.shape, F32),
            pltpu.SemaphoreType.DMA((5 + 2 * verts,)),
        ],
        compiler_params=params,
        name="pack",
    )(in_hbm[0], in_hbm[3], in_hbm[4])
    from_even = lax.ppermute(packed[0], "area", even_pairs)
    from_odd = lax.ppermute(packed[1], "area", odd_pairs)
    if swap:
        vert = [lax.ppermute(packed[2], "depth", swapped)]
    else:
        vert = [lax.ppermute(packed[2], "depth", down), lax.ppermute(packed[3], "depth", up)]
    chunks = math.gcd(layers, 4)
    block = (layers, rows, width)
    kept, kap, head, local_sums = pl.pallas_call(
        local_kernel,
        out_shape=[shape(6, *block), shape(*block), shape(*block), shape(2, rows, width)],
        in_specs=[pl.BlockSpec(memory_space=pltpu.HBM)] * 5,
        out_specs=whole(4),
        scratch_shapes=[
            pltpu.VMEM(block, F32),
            pltpu.VMEM(block, F32),
            pltpu.VMEM(block, jnp.int32),
            pltpu.VMEM(soil_params.shape, F32),
            pltpu.VMEM((5, kind_count, 8, LANES), F32),
            pltpu.SemaphoreType.DMA((4, chunks)),
            pltpu.SemaphoreType.DMA(()),
        ],
        compiler_params=params,
        name="local",
    )(in_hbm[0], in_hbm[1], in_hbm[2], in_hbm[3], in_hbm[4])
    smooth, sums, to_even, to_odd = pl.pallas_call(
        functools.partial(fine_kernel, swap),
        out_shape=[
            shape(layers, rows, width),
            shape(5, rows, width),
            shape(2 * layers + 8, width),
            shape(2 * layers + 8, width),
        ],
        in_specs=whole(6 + verts),
        out_specs=whole(4),
        compiler_params=params,
        name="fine",
    )(head, kept, kap, local_sums, from_even, from_odd, *vert)
    from_even = lax.ppermute(to_even, "area", even_pairs)
    from_odd = lax.ppermute(to_odd, "area", odd_pairs)
    if swap:
        their_sums = lax.ppermute(sums, "depth", swapped)
    else:
        sums, their_sums = lax.psum(sums, "depth"), jnp.zeros_like(sums)
    halo = pl.pallas_call(
        edge_kernel,
        out_shape=shape(2, 8, width),
        in_specs=whole(4),
        out_specs=whole(1)[0],
        compiler_params=params,
        name="edge",
    )(to_even, to_odd, from_even, from_odd)
    if swap:
        their_halo = lax.ppermute(halo, "depth", swapped)
    else:
        halo, their_halo = lax.psum(halo, "depth"), jnp.zeros_like(halo)
    out, head = pl.pallas_call(
        functools.partial(coarse_kernel, layers * depths),
        out_shape=[shape(layers, rows, width), shape(rows, width)],
        in_specs=whole(5),
        out_specs=whole(2),
        compiler_params=params,
        name="coarse",
    )(smooth, sums, their_sums, halo, their_halo)
    return out, head


def solution(mesh):
    in_specs = (
        P("depth", "area", None),
        P("depth", "area", None),
        P("depth", "area", None),
        P("depth", "area", None),
        P(),
    )
    out_specs = (P("depth", "area", None), P("area", None))
    return jax.shard_map(shards, mesh=mesh, in_specs=in_specs, out_specs=out_specs, check_vma=False)
```

```python
import functools
import math

import jax
import jax.numpy as jnp
from jax import lax
from jax.experimental import pallas as pl
from jax.experimental.pallas import tpu as pltpu
from jax.sharding import PartitionSpec as P

INV_DT = 10.0
RELAX = 0.8
SMALL = 0.04
LOG2E = math.log2(math.e)
LANES = 128
PACK_COST = 4_000_000_000
F32 = jnp.float32

T_A, T_N, T_SK, T_D, T_R = range(5)


def whole(count):
    return [pl.BlockSpec(memory_space=pltpu.VMEM)] * count


def build_table(params_ref):
    alpha = params_ref[2:3, :]
    return {
        T_A: jnp.log(alpha) * LOG2E,
        T_N: params_ref[3:4, :],
        T_SK: jnp.sqrt(params_ref[4:5, :]),
        T_D: (params_ref[1:2, :] - params_ref[0:1, :]) * INV_DT,
        T_R: params_ref[0:1, :] * INV_DT,
    }


def gather(row, kinds):
    table = jnp.broadcast_to(jnp.pad(row, ((0, 0), (0, LANES - row.shape[1]))), (8, LANES))
    rows = []
    for r in range(0, kinds.shape[0], 8):
        cols = []
        for c in range(0, kinds.shape[1], LANES):
            cols.append(
                jnp.take_along_axis(
                    table, kinds[r : r + 8, c : c + LANES], axis=1, mode="promise_in_bounds"
                )
            )
        rows.append(jnp.concatenate(cols, axis=1))
    return rows[0] if len(rows) == 1 else jnp.concatenate(rows, axis=0)


def spread_table(table, tab_ref):
    for row_id, row in table.items():
        for kind in range(row.shape[1]):
            tab_ref[row_id, kind] = jnp.broadcast_to(row[:, kind : kind + 1], (8, LANES))


def pick(tab_ref, row_id, bits, width):
    level = [
        jnp.concatenate([tab_ref[row_id, kind]] * (width // LANES), axis=1)
        for kind in range(tab_ref.shape[1])
    ]
    for bit in bits:
        pairs = [
            jnp.where(bit, level[i + 1], level[i]) for i in range(0, len(level) - 1, 2)
        ]
        level = pairs + ([level[-1]] if len(level) % 2 else [])
    return level[0]


def type_bits(kinds, count):
    return [(kinds & (1 << i)) != 0 for i in range((count - 1).bit_length())]


def hydraulics(h, pa, pn, psk):
    pc = (1.0 / pn - 1.0) * (0.25 * LOG2E)
    q = h * h + SMALL
    u = jnp.exp2(pn * (pa + (0.5 * LOG2E) * jnp.log(q)))
    one_plus = 1.0 + u
    inv = 1.0 / one_plus
    ratio = u * inv
    quarter = jnp.exp2(pc * jnp.log(one_plus))
    w = jnp.exp2((-4.0 * pc) * jnp.log(ratio))
    kappa = psk * quarter * (1.0 - w)
    half = quarter * quarter
    return kappa, half * half, ratio * lax.rsqrt(q)


def kappa_by_gather(h, kinds, table):
    return hydraulics(
        h, gather(table[T_A], kinds), gather(table[T_N], kinds), gather(table[T_SK], kinds)
    )[0]


def even_area():
    return lax.rem(lax.axis_index("area"), 2) == 0


def pack_kernel(swap, p_ref, soil_ref, params_ref, tab_ref, even_ref, odd_ref, *rest):
    layers, rows, _ = p_ref.shape
    count = 1 if swap else 2
    vert_refs = rest[:count]
    p_buf, soil_buf, vert_p, vert_soil, params_buf, sems = rest[count:]
    even = even_area()
    if swap:
        spots = [jnp.where(lax.axis_index("depth") == 0, layers - 1, 0)]
    else:
        spots = [layers - 1, 0]
    copies = [(params_ref, params_buf)]
    for side, row in enumerate((0, rows - 1)):
        copies.append((p_ref.at[:, row, :], p_buf.at[side]))
        copies.append((soil_ref.at[:, row, :], soil_buf.at[side]))
    for side, spot in enumerate(spots):
        copies.append((p_ref.at[spot], vert_p.at[side]))
        copies.append((soil_ref.at[spot], vert_soil.at[side]))
    copies = [
        pltpu.make_async_copy(source, target, sems.at[i])
        for i, (source, target) in enumerate(copies)
    ]
    for copy in copies:
        copy.start()
    copies[0].wait()
    table = build_table(params_buf)
    spread_table(table, tab_ref)
    for copy in copies[1:]:
        copy.wait()
    low_h, high_h = p_buf[0], p_buf[1]
    low_k = kappa_by_gather(low_h, soil_buf[0], table)
    high_k = kappa_by_gather(high_h, soil_buf[1], table)
    even_ref[0] = jnp.where(even, high_h, low_h)
    even_ref[1] = jnp.where(even, high_k, low_k)
    odd_ref[0] = jnp.where(even, low_h, high_h)
    odd_ref[1] = jnp.where(even, low_k, high_k)
    for side, out_ref in enumerate(vert_refs):
        h = vert_p[side]
        out_ref[0] = h
        out_ref[1] = kappa_by_gather(h, vert_soil[side], table)


def row_iota(shape):
    return lax.broadcasted_iota(jnp.int32, shape, 0)


def lane_iota(shape):
    return lax.broadcasted_iota(jnp.int32, shape, 1)


def from_above(x, edge):
    return jnp.where(row_iota(x.shape) == 0, edge, pltpu.roll(x, 1, 0))


def from_below(x, edge):
    last = x.shape[0] - 1
    return jnp.where(row_iota(x.shape) == last, edge, pltpu.roll(x, last, 0))


def from_left(x):
    return jnp.where(lane_iota(x.shape) == 0, 0.0, pltpu.roll(x, 1, 1))


def from_right(x):
    last = x.shape[1] - 1
    return jnp.where(lane_iota(x.shape) == last, 0.0, pltpu.roll(x, last, 1))


def local_kernel(
    p_ref, theta_ref, source_ref, soil_ref, tab_ref, kept_ref, kap_ref, sums_ref
):
    layers, rows, width = p_ref.shape
    kind_count = tab_ref.shape[1]

    def step(layer, carry):
        sum_fixed, sum_rate = carry
        bits = type_bits(soil_ref[layer], kind_count)
        pa, pn, psk, pd, pr = [pick(tab_ref, i, bits, width) for i in range(5)]
        h = p_ref[layer]
        kap, sat, over = hydraulics(h, pa, pn, psk)
        fixed = pr - INV_DT * theta_ref[layer] - source_ref[layer]
        k_l, k_r = from_left(kap), from_right(kap)
        k_u, k_d = from_above(kap, 0.0), from_below(kap, 0.0)
        inflow = (
            k_l * (pltpu.roll(h, 1, 1) - h)
            + k_r * (pltpu.roll(h, width - 1, 1) - h)
            + k_u * (pltpu.roll(h, 1, 0) - h)
            + k_d * (pltpu.roll(h, rows - 1, 0) - h)
        )
        kap_ref[layer] = kap
        kept_ref[0, layer] = pd * sat + fixed - kap * inflow
        kept_ref[1, layer] = pd * (pn - 1.0) * sat * over + kap * ((k_l + k_r) + (k_u + k_d))
        kept_ref[2, layer] = pa
        kept_ref[3, layer] = pn
        kept_ref[4, layer] = psk
        kept_ref[5, layer] = pd
        return sum_fixed + fixed, sum_rate + jnp.exp2(pa)

    zero = jnp.zeros((rows, width), F32)
    sum_fixed, sum_rate = lax.fori_loop(0, layers, step, (zero, zero), unroll=True)
    sums_ref[0] = sum_fixed
    sums_ref[1] = sum_rate


def fine_kernel(swap, p_ref, kept_ref, kap_ref, local_ref, from_even_ref, from_odd_ref, *rest):
    layers, rows, width = p_ref.shape
    if swap:
        vert_ref, rest = rest[0], rest[1:]
    else:
        top_ref, bottom_ref, rest = rest[0], rest[1], rest[2:]
    smooth_ref, sums_ref, to_even_ref, to_odd_ref = rest
    even = even_area()
    spot = row_iota((rows, width))
    is_first, is_last = spot == 0, spot == rows - 1

    if swap:
        at_top = lax.axis_index("depth") == 0
        top_k = jnp.where(at_top, 0.0, vert_ref[1])
        bottom_k = jnp.where(at_top, vert_ref[1], 0.0)
        top_h = bottom_h = vert_ref[0]
    else:
        top_h, top_k = top_ref[0], top_ref[1]
        bottom_h, bottom_k = bottom_ref[0], bottom_ref[1]

    def step(layer, carry):
        sum_kh, sum_k, sum_cap, sum_sat, flux_x, flux_y = carry
        h = p_ref[layer]
        above, below = jnp.maximum(layer - 1, 0), jnp.minimum(layer + 1, layers - 1)
        k_u = jnp.where(layer == 0, top_k, kap_ref[above])
        h_u = jnp.where(layer == 0, top_h, p_ref[above])
        k_d = jnp.where(layer == layers - 1, bottom_k, kap_ref[below])
        h_d = jnp.where(layer == layers - 1, bottom_h, p_ref[below])
        even_k = from_even_ref[1, pl.ds(layer, 1), :]
        odd_k = from_odd_ref[1, pl.ds(layer, 1), :]
        even_h = from_even_ref[0, pl.ds(layer, 1), :]
        odd_h = from_odd_ref[0, pl.ds(layer, 1), :]
        lo_k = jnp.where(even, odd_k, even_k)
        hi_k = jnp.where(even, even_k, odd_k)
        lo_h = jnp.where(even, odd_h, even_h)
        hi_h = jnp.where(even, even_h, odd_h)
        side_k = jnp.where(is_first, lo_k, jnp.where(is_last, hi_k, 0.0))
        side_h = jnp.where(is_first, lo_h, hi_h)
        kap = kap_ref[layer]
        inflow = k_u * (h_u - h + 1.0) + k_d * (h_d - h - 1.0) + side_k * (side_h - h)
        balance = kept_ref[0, layer] - kap * inflow
        diagonal = kept_ref[1, layer] + kap * (k_u + k_d + side_k)
        h = h - RELAX * balance / diagonal
        smooth_ref[layer] = h

        pn = kept_ref[3, layer]
        pd = kept_ref[5, layer]
        kap, sat, over = hydraulics(h, kept_ref[2, layer], pn, kept_ref[4, layer])
        cond = kap * kap
        flux_x = flux_x + kap * from_below(kap, 0.0) * (pltpu.roll(h, rows - 1, 0) - h)
        flux_y = flux_y + kap * from_right(kap) * (pltpu.roll(h, width - 1, 1) - h)
        for at, value in ((0, h), (layers, kap)):
            low, high = value[0:1, :], value[rows - 1 : rows, :]
            to_even_ref[pl.ds(at + layer, 1), :] = jnp.where(even, high, low)
            to_odd_ref[pl.ds(at + layer, 1), :] = jnp.where(even, low, high)
        return (
            sum_kh + cond * h,
            sum_k + cond,
            sum_cap + pd * (pn - 1.0) * sat * over,
            sum_sat + pd * sat,
            flux_x,
            flux_y,
        )

    zero = jnp.zeros((rows, width), F32)
    sum_kh, sum_k, sum_cap, sum_sat, flux_x, flux_y = lax.fori_loop(
        0, layers, step, (zero,) * 6, unroll=True
    )
    sum_rate = local_ref[1]
    restricted = (
        (flux_x - from_above(flux_x, 0.0)) + (flux_y - from_left(flux_y)) - sum_sat - local_ref[0]
    )
    for at, value in enumerate((sum_kh, sum_k, sum_cap, restricted, sum_rate)):
        sums_ref[at] = value
    at = 2 * layers
    tails = []
    for edge, inner in ((rows - 1, rows - 2), (0, 1)):
        tail = [
            sum_kh[edge : edge + 1],
            sum_k[edge : edge + 1],
            sum_kh[inner : inner + 1],
            sum_k[inner : inner + 1],
            sum_cap[edge : edge + 1],
            restricted[edge : edge + 1],
            sum_rate[edge : edge + 1],
            zero[0:1],
        ]
        tails.append(jnp.concatenate(tail, axis=0))
    high, low = tails
    to_even_ref[at : at + 8, :] = jnp.where(even, high, low)
    to_odd_ref[at : at + 8, :] = jnp.where(even, low, high)


def edge_kernel(to_even_ref, to_odd_ref, from_even_ref, from_odd_ref, halo_ref):
    layers = (to_even_ref.shape[0] - 8) // 2
    at = 2 * layers
    for side, (mine_ref, their_ref) in enumerate(
        ((to_even_ref, from_even_ref), (to_odd_ref, from_odd_ref))
    ):
        flux = (
            mine_ref[layers:at, :]
            * their_ref[layers:at, :]
            * (their_ref[0:layers, :] - mine_ref[0:layers, :])
        )
        flux = jnp.sum(flux, axis=0, keepdims=True)
        block = their_ref[at : at + 8, :]
        spot = row_iota(block.shape)
        block = jnp.where(spot == 5, block - flux, block)
        halo_ref[side] = jnp.where(spot == 7, flux, block)


def coarse_kernel(
    depth_total, smooth_ref, sums_ref, their_sums_ref, halo_ref, their_halo_ref, out_ref, head_ref
):
    rows = smooth_ref.shape[1]
    kh, kk, cap, rest, rate = [sums_ref[i] + their_sums_ref[i] for i in range(5)]
    by_even = halo_ref[0] + their_halo_ref[0]
    by_odd = halo_ref[1] + their_halo_ref[1]
    even = even_area()
    lo = jnp.where(even, by_odd, by_even)
    hi = jnp.where(even, by_even, by_odd)
    spot = row_iota(rest.shape)
    rest = jnp.where(spot == 0, rest + lo[7:8], rest)
    rest = jnp.where(spot == rows - 1, rest + hi[7:8], rest)

    def pair(i):
        return jnp.where(spot == 0, lo[i : i + 1], jnp.where(spot == rows - 1, hi[i : i + 1], 0.0))

    h_kh, h_k, o_kh, o_k, h_cap, h_rest, h_rate = [pair(i) for i in range(7)]
    edge_lane = lane_iota(rest.shape)

    def sides(x):
        return from_left(x) + from_right(x)

    base = kh / kk
    root = jnp.sqrt(kk)
    h_live = h_k > 0.0
    h_base = jnp.where(h_live, h_kh / jnp.where(h_live, h_k, 1.0), 0.0)
    h_root = jnp.sqrt(h_k)
    o_root = jnp.sqrt(o_k)

    def around(x, halo):
        return from_above(x, halo[0:1]), from_below(x, halo[rows - 1 : rows])

    def flow(head, halo_head, tau, halo_tau):
        tau_u, tau_d = around(tau, halo_tau)
        head_u, head_d = around(head, halo_head)
        tau_l, tau_r = from_left(tau), from_right(tau)
        head_l, head_r = from_left(head), from_right(head)
        inflow = (
            tau_u * (head_u - head)
            + tau_d * (head_d - head)
            + tau_l * (head_l - head)
            + tau_r * (head_r - head)
        )
        return tau * inflow, tau * (tau_u + tau_d + tau_l + tau_r)

    start_in, start_sum = flow(base, h_base, root, h_root)
    rhs = rest - start_in
    first = base + RELAX * rest / (cap + start_sum)
    h_diag = h_cap + h_root * (o_root + root + sides(h_root))
    h_first = h_base + jnp.where(h_live, RELAX * h_rest / jnp.where(h_live, h_diag, 1.0), 0.0)
    half = 0.5 / depth_total
    tau = root * jnp.exp(half * rate * jnp.tanh(first - base))
    h_tau = h_root * jnp.exp(half * h_rate * jnp.tanh(h_first - h_base))
    first_in, first_sum = flow(first, h_first, tau, h_tau)
    first_flow = cap * (first - base) - first_in
    second = first - RELAX * (first_flow - rhs) / (cap + first_sum)
    head_ref[...] = second
    shift = second - base
    out_ref[...] = smooth_ref[...] + shift[None]


def shards(pressure, theta_old, source, soil_type, soil_params):
    layers, rows, width = pressure.shape
    areas = lax.axis_size("area")
    depths = lax.axis_size("depth")
    swap = depths == 2
    even_pairs = [p for i in range(0, areas - 1, 2) for p in ((i, i + 1), (i + 1, i))]
    odd_pairs = [p for i in range(1, areas - 1, 2) for p in ((i, i + 1), (i + 1, i))]
    down = [(i, i + 1) for i in range(depths - 1)]
    up = [(b, a) for a, b in down]
    swapped = [(0, 1), (1, 0)]

    def shape(*dims):
        return jax.ShapeDtypeStruct(dims, F32)

    params = pltpu.CompilerParams(vmem_limit_bytes=48 << 20)
    verts = 1 if swap else 2
    kind_count = soil_params.shape[1]
    in_hbm = [
        pltpu.with_memory_space_constraint(x, pltpu.HBM)
        for x in (pressure, soil_type, soil_params)
    ]
    packed = pl.pallas_call(
        functools.partial(pack_kernel, swap),
        out_shape=[shape(5, kind_count, 8, LANES)]
        + [shape(2, layers, width)] * 2
        + [shape(2, rows, width)] * verts,
        in_specs=[pl.BlockSpec(memory_space=pltpu.HBM)] * 3,
        out_specs=whole(3 + verts),
        scratch_shapes=[
            pltpu.VMEM((2, layers, width), F32),
            pltpu.VMEM((2, layers, width), jnp.int32),
            pltpu.VMEM((verts, rows, width), F32),
            pltpu.VMEM((verts, rows, width), jnp.int32),
            pltpu.VMEM(soil_params.shape, F32),
            pltpu.SemaphoreType.DMA((5 + 2 * verts,)),
        ],
        compiler_params=params,
        cost_estimate=pl.CostEstimate(flops=PACK_COST, transcendentals=0, bytes_accessed=0),
        name="pack",
    )(*in_hbm)
    from_even = lax.ppermute(packed[1], "area", even_pairs)
    from_odd = lax.ppermute(packed[2], "area", odd_pairs)
    if swap:
        vert = [lax.ppermute(packed[3], "depth", swapped)]
    else:
        vert = [lax.ppermute(packed[3], "depth", down), lax.ppermute(packed[4], "depth", up)]
    kept, kap, local_sums = pl.pallas_call(
        local_kernel,
        out_shape=[shape(6, layers, rows, width), shape(layers, rows, width), shape(2, rows, width)],
        in_specs=whole(5),
        out_specs=whole(3),
        compiler_params=params,
        name="local",
    )(pressure, theta_old, source, soil_type, packed[0])
    smooth, sums, to_even, to_odd = pl.pallas_call(
        functools.partial(fine_kernel, swap),
        out_shape=[
            shape(layers, rows, width),
            shape(5, rows, width),
            shape(2 * layers + 8, width),
            shape(2 * layers + 8, width),
        ],
        in_specs=whole(6 + verts),
        out_specs=whole(4),
        compiler_params=params,
        name="fine",
    )(pressure, kept, kap, local_sums, from_even, from_odd, *vert)
    from_even = lax.ppermute(to_even, "area", even_pairs)
    from_odd = lax.ppermute(to_odd, "area", odd_pairs)
    if swap:
        their_sums = lax.ppermute(sums, "depth", swapped)
    else:
        sums, their_sums = lax.psum(sums, "depth"), jnp.zeros_like(sums)
    halo = pl.pallas_call(
        edge_kernel,
        out_shape=shape(2, 8, width),
        in_specs=whole(4),
        out_specs=whole(1)[0],
        compiler_params=params,
        name="edge",
    )(to_even, to_odd, from_even, from_odd)
    if swap:
        their_halo = lax.ppermute(halo, "depth", swapped)
    else:
        halo, their_halo = lax.psum(halo, "depth"), jnp.zeros_like(halo)
    out, head = pl.pallas_call(
        functools.partial(coarse_kernel, layers * depths),
        out_shape=[shape(layers, rows, width), shape(rows, width)],
        in_specs=whole(5),
        out_specs=whole(2),
        compiler_params=params,
        name="coarse",
    )(smooth, sums, their_sums, halo, their_halo)
    return out, head


def solution(mesh):
    in_specs = (
        P("depth", "area", None),
        P("depth", "area", None),
        P("depth", "area", None),
        P("depth", "area", None),
        P(),
    )
    out_specs = (P("depth", "area", None), P("area", None))
    return jax.shard_map(shards, mesh=mesh, in_specs=in_specs, out_specs=out_specs, check_vma=False)
```

```python
import functools
import math

import jax
import jax.numpy as jnp
from jax import lax
from jax.experimental import pallas as pl
from jax.experimental.pallas import tpu as pltpu
from jax.sharding import PartitionSpec as P

INV_DT = 10.0
RELAX = 0.8
SMALL = 0.04
LOG2E = math.log2(math.e)
LANES = 128
PACK_COST = 4_000_000_000
F32 = jnp.float32

T_A, T_N, T_SK, T_D, T_R = range(5)


def whole(count):
    return [pl.BlockSpec(memory_space=pltpu.VMEM)] * count


def build_table(params_ref):
    alpha = params_ref[2:3, :]
    return {
        T_A: jnp.log(alpha) * LOG2E,
        T_N: params_ref[3:4, :],
        T_SK: jnp.sqrt(params_ref[4:5, :]),
        T_D: (params_ref[1:2, :] - params_ref[0:1, :]) * INV_DT,
        T_R: params_ref[0:1, :] * INV_DT,
    }


def spread_table(table, tab_ref):
    for row_id, row in table.items():
        for kind in range(row.shape[1]):
            tab_ref[row_id, kind] = jnp.broadcast_to(row[:, kind : kind + 1], (8, LANES))


def pick(tab_ref, row_id, bits, width):
    level = [
        jnp.tile(tab_ref[row_id, kind], (bits[0].shape[0] // 8, width // LANES))
        for kind in range(tab_ref.shape[1])
    ]
    for bit in bits:
        pairs = [
            jnp.where(bit, level[i + 1], level[i]) for i in range(0, len(level) - 1, 2)
        ]
        level = pairs + ([level[-1]] if len(level) % 2 else [])
    return level[0]


def type_bits(kinds, count):
    return [(kinds & (1 << i)) != 0 for i in range((count - 1).bit_length())]


def hydraulics(h, pa, pn, psk):
    pc = (1.0 / pn - 1.0) * (0.25 * LOG2E)
    q = h * h + SMALL
    u = jnp.exp2(pn * (pa + (0.5 * LOG2E) * jnp.log(q)))
    one_plus = 1.0 + u
    inv = 1.0 / one_plus
    ratio = u * inv
    quarter = jnp.exp2(pc * jnp.log(one_plus))
    w = jnp.exp2((-4.0 * pc) * jnp.log(ratio))
    kappa = psk * quarter * (1.0 - w)
    half = quarter * quarter
    return kappa, half * half, ratio * lax.rsqrt(q)


def code(kinds):
    return (kinds + 1).astype(F32)


def code_params(codes, tab_ref):
    kinds = jnp.maximum(codes.astype(jnp.int32) - 1, 0)
    bits = type_bits(kinds, tab_ref.shape[1])
    pa, pn, psk = [pick(tab_ref, i, bits, codes.shape[1]) for i in (T_A, T_N, T_SK)]
    return pa, pn, jnp.where(codes > 0.5, psk, 0.0)


def even_area():
    return lax.rem(lax.axis_index("area"), 2) == 0


def paired():
    area, last = lax.axis_index("area"), lax.axis_size("area") - 1
    is_even = even_area()
    return (
        jnp.logical_or(jnp.logical_not(is_even), area < last),
        jnp.where(is_even, area, last - area) > 0,
    )


def full_swap(pairs, areas, depths):
    target = {a: b for a, b in pairs}
    target.update({b: a for a, b in pairs})
    moves = []
    for a in range(areas):
        for d in range(depths):
            other = d if a in target else d ^ 1
            if other < depths:
                moves.append((a * depths + d, target.get(a, a) * depths + other))
    return moves


def pack_kernel(swap, p_ref, soil_ref, params_ref, tab_ref, even_ref, odd_ref, *rest):
    layers, rows, _ = p_ref.shape
    count = 1 if swap else 2
    vert_refs = rest[:count]
    p_buf, soil_buf, vert_p, vert_soil, params_buf, sems = rest[count:]
    even = even_area()
    if swap:
        spots = [jnp.where(lax.axis_index("depth") == 0, layers - 1, 0)]
    else:
        spots = [layers - 1, 0]
    copies = [(params_ref, params_buf)]
    for side, row in enumerate((0, rows - 1)):
        copies.append((p_ref.at[:, row, :], p_buf.at[side]))
        copies.append((soil_ref.at[:, row, :], soil_buf.at[side]))
    for side, spot in enumerate(spots):
        copies.append((p_ref.at[spot], vert_p.at[side]))
        copies.append((soil_ref.at[spot], vert_soil.at[side]))
    copies = [
        pltpu.make_async_copy(source, target, sems.at[i])
        for i, (source, target) in enumerate(copies)
    ]
    for copy in copies:
        copy.start()
    copies[0].wait()
    spread_table(build_table(params_buf), tab_ref)
    for copy in copies[1:]:
        copy.wait()
    for i, low, high in ((0, p_buf[0], p_buf[1]), (1, code(soil_buf[0]), code(soil_buf[1]))):
        even_ref[i] = jnp.where(even, high, low)
        odd_ref[i] = jnp.where(even, low, high)
    for side, out_ref in enumerate(vert_refs):
        out_ref[0] = vert_p[side]
        out_ref[1] = code(vert_soil[side])


def row_iota(shape):
    return lax.broadcasted_iota(jnp.int32, shape, 0)


def lane_iota(shape):
    return lax.broadcasted_iota(jnp.int32, shape, 1)


def from_above(x, edge):
    return jnp.where(row_iota(x.shape) == 0, edge, pltpu.roll(x, 1, 0))


def from_below(x, edge):
    last = x.shape[0] - 1
    return jnp.where(row_iota(x.shape) == last, edge, pltpu.roll(x, last, 0))


def from_left(x):
    return jnp.where(lane_iota(x.shape) == 0, 0.0, pltpu.roll(x, 1, 1))


def from_right(x):
    last = x.shape[1] - 1
    return jnp.where(lane_iota(x.shape) == last, 0.0, pltpu.roll(x, last, 1))


def local_kernel(
    p_ref, theta_ref, source_ref, soil_ref, tab_ref, kept_ref, kap_ref, sums_ref
):
    layers, rows, width = p_ref.shape
    kind_count = tab_ref.shape[1]

    def step(layer, carry):
        sum_fixed, sum_rate = carry
        bits = type_bits(soil_ref[layer], kind_count)
        pa, pn, psk, pd, pr = [pick(tab_ref, i, bits, width) for i in range(5)]
        h = p_ref[layer]
        kap, sat, over = hydraulics(h, pa, pn, psk)
        fixed = pr - INV_DT * theta_ref[layer] - source_ref[layer]
        k_l, k_r = from_left(kap), from_right(kap)
        k_u, k_d = from_above(kap, 0.0), from_below(kap, 0.0)
        inflow = (
            k_l * (pltpu.roll(h, 1, 1) - h)
            + k_r * (pltpu.roll(h, width - 1, 1) - h)
            + k_u * (pltpu.roll(h, 1, 0) - h)
            + k_d * (pltpu.roll(h, rows - 1, 0) - h)
        )
        kap_ref[layer] = kap
        kept_ref[0, layer] = pd * sat + fixed - kap * inflow
        kept_ref[1, layer] = pd * (pn - 1.0) * sat * over + kap * ((k_l + k_r) + (k_u + k_d))
        kept_ref[2, layer] = pa
        kept_ref[3, layer] = pn
        kept_ref[4, layer] = psk
        kept_ref[5, layer] = pd
        return sum_fixed + fixed, sum_rate + jnp.exp2(pa)

    zero = jnp.zeros((rows, width), F32)
    sum_fixed, sum_rate = lax.fori_loop(0, layers, step, (zero, zero), unroll=True)
    sums_ref[0] = sum_fixed
    sums_ref[1] = sum_rate


def fine_kernel(swap, p_ref, kept_ref, kap_ref, local_ref, tab_ref, *rest):
    layers, rows, width = p_ref.shape
    left = iter(rest)
    from_even_ref = next(left)
    from_odd_ref = next(left)
    vert_refs = [next(left) for _ in range(1 if swap else 2)]
    smooth_ref, sums_ref, to_even_ref, to_odd_ref, rim_ref, side_ref = left
    even = even_area()
    spot = row_iota((rows, width))
    is_first, is_last = spot == 0, spot == rows - 1

    if swap:
        at_top = lax.axis_index("depth") == 0
        (vert_ref,) = vert_refs
        top_h = bottom_h = vert_ref[0]
        vert_k = hydraulics(top_h, *code_params(vert_ref[1], tab_ref))[0]
        top_k = jnp.where(at_top, 0.0, vert_k)
        bottom_k = jnp.where(at_top, vert_k, 0.0)
    else:
        top_ref, bottom_ref = vert_refs
        top_h, bottom_h = top_ref[0], bottom_ref[0]
        top_k = hydraulics(top_h, *code_params(top_ref[1], tab_ref))[0]
        bottom_k = hydraulics(bottom_h, *code_params(bottom_ref[1], tab_ref))[0]
    def side_step(i, carry):
        at = pl.ds(i * 8, 8)
        for side, (from_ref, live) in enumerate(zip((from_even_ref, from_odd_ref), paired())):
            fields = code_params(jnp.where(live, from_ref[1, at, :], 0.0), tab_ref)
            for spot, field in enumerate(fields):
                rim_ref[side, spot, at, :] = field
            side_ref[side, at, :] = hydraulics(from_ref[0, at, :], *fields)[0]
        return carry

    lax.fori_loop(0, layers // 8, side_step, 0)

    def step(layer, carry):
        sum_kh, sum_k, sum_cap, sum_sat, flux_x, flux_y = carry
        h = p_ref[layer]
        above, below = jnp.maximum(layer - 1, 0), jnp.minimum(layer + 1, layers - 1)
        k_u = jnp.where(layer == 0, top_k, kap_ref[above])
        h_u = jnp.where(layer == 0, top_h, p_ref[above])
        k_d = jnp.where(layer == layers - 1, bottom_k, kap_ref[below])
        h_d = jnp.where(layer == layers - 1, bottom_h, p_ref[below])
        even_k = side_ref[0, pl.ds(layer, 1), :]
        odd_k = side_ref[1, pl.ds(layer, 1), :]
        even_h = from_even_ref[0, pl.ds(layer, 1), :]
        odd_h = from_odd_ref[0, pl.ds(layer, 1), :]
        lo_k = jnp.where(even, odd_k, even_k)
        hi_k = jnp.where(even, even_k, odd_k)
        lo_h = jnp.where(even, odd_h, even_h)
        hi_h = jnp.where(even, even_h, odd_h)
        side_k = jnp.where(is_first, lo_k, jnp.where(is_last, hi_k, 0.0))
        side_h = jnp.where(is_first, lo_h, hi_h)
        kap = kap_ref[layer]
        inflow = k_u * (h_u - h + 1.0) + k_d * (h_d - h - 1.0) + side_k * (side_h - h)
        balance = kept_ref[0, layer] - kap * inflow
        diagonal = kept_ref[1, layer] + kap * (k_u + k_d + side_k)
        h = h - RELAX * balance / diagonal
        smooth_ref[layer] = h

        pn = kept_ref[3, layer]
        pd = kept_ref[5, layer]
        kap, sat, over = hydraulics(h, kept_ref[2, layer], pn, kept_ref[4, layer])
        cond = kap * kap
        flux_x = flux_x + kap * from_below(kap, 0.0) * (pltpu.roll(h, rows - 1, 0) - h)
        flux_y = flux_y + kap * from_right(kap) * (pltpu.roll(h, width - 1, 1) - h)
        for even_at, odd_at, value in (
            (to_even_ref, to_odd_ref, h),
            (rim_ref.at[0, 3], rim_ref.at[1, 3], kap),
        ):
            low, high = value[0:1, :], value[rows - 1 : rows, :]
            even_at[pl.ds(layer, 1), :] = jnp.where(even, high, low)
            odd_at[pl.ds(layer, 1), :] = jnp.where(even, low, high)
        return (
            sum_kh + cond * h,
            sum_k + cond,
            sum_cap + pd * (pn - 1.0) * sat * over,
            sum_sat + pd * sat,
            flux_x,
            flux_y,
        )

    zero = jnp.zeros((rows, width), F32)
    sum_kh, sum_k, sum_cap, sum_sat, flux_x, flux_y = lax.fori_loop(
        0, layers, step, (zero,) * 6, unroll=True
    )
    sum_rate = local_ref[1]
    restricted = (
        (flux_x - from_above(flux_x, 0.0)) + (flux_y - from_left(flux_y)) - sum_sat - local_ref[0]
    )
    for at, value in enumerate((sum_kh, sum_k, sum_cap, restricted, sum_rate)):
        sums_ref[at] = value
    at = layers
    tails = []
    for edge, inner in ((rows - 1, rows - 2), (0, 1)):
        tail = [
            sum_kh[edge : edge + 1],
            sum_k[edge : edge + 1],
            sum_kh[inner : inner + 1],
            sum_k[inner : inner + 1],
            sum_cap[edge : edge + 1],
            restricted[edge : edge + 1],
            sum_rate[edge : edge + 1],
            zero[0:1],
        ]
        tails.append(jnp.concatenate(tail, axis=0))
    high, low = tails
    to_even_ref[at : at + 8, :] = jnp.where(even, high, low)
    to_odd_ref[at : at + 8, :] = jnp.where(even, low, high)


def edge_kernel(rim_ref, to_odd_ref, to_even_ref, from_odd_ref, from_even_ref, halo_ref):
    layers = rim_ref.shape[2]
    at = layers
    for side, (mine_ref, their_ref, live) in enumerate(
        zip((to_even_ref, to_odd_ref), (from_even_ref, from_odd_ref), paired())
    ):
        theirs = their_ref[0:layers, :]
        kap = hydraulics(theirs, rim_ref[side, 0], rim_ref[side, 1], rim_ref[side, 2])[0]
        flux = rim_ref[side, 3] * kap * (theirs - mine_ref[0:layers, :])
        flux = jnp.sum(flux, axis=0, keepdims=True)
        block = jnp.where(live, their_ref[at : at + 8, :], 0.0)
        spot = row_iota(block.shape)
        block = jnp.where(spot == 5, block - flux, block)
        halo_ref[side] = jnp.where(spot == 7, flux, block)


def coarse_kernel(
    depth_total, smooth_ref, sums_ref, their_sums_ref, halo_ref, their_halo_ref, out_ref, head_ref
):
    rows = smooth_ref.shape[1]
    kh, kk, cap, rest, rate = [sums_ref[i] + their_sums_ref[i] for i in range(5)]
    by_even = halo_ref[0] + their_halo_ref[0]
    by_odd = halo_ref[1] + their_halo_ref[1]
    even = even_area()
    lo = jnp.where(even, by_odd, by_even)
    hi = jnp.where(even, by_even, by_odd)
    spot = row_iota(rest.shape)
    rest = jnp.where(spot == 0, rest + lo[7:8], rest)
    rest = jnp.where(spot == rows - 1, rest + hi[7:8], rest)

    def pair(i):
        return jnp.where(spot == 0, lo[i : i + 1], jnp.where(spot == rows - 1, hi[i : i + 1], 0.0))

    h_kh, h_k, o_kh, o_k, h_cap, h_rest, h_rate = [pair(i) for i in range(7)]
    edge_lane = lane_iota(rest.shape)

    def sides(x):
        return from_left(x) + from_right(x)

    base = kh / kk
    root = jnp.sqrt(kk)
    h_live = h_k > 0.0
    h_base = jnp.where(h_live, h_kh / jnp.where(h_live, h_k, 1.0), 0.0)
    h_root = jnp.sqrt(h_k)
    o_root = jnp.sqrt(o_k)

    def around(x, halo):
        return from_above(x, halo[0:1]), from_below(x, halo[rows - 1 : rows])

    def flow(head, halo_head, tau, halo_tau):
        tau_u, tau_d = around(tau, halo_tau)
        head_u, head_d = around(head, halo_head)
        tau_l, tau_r = from_left(tau), from_right(tau)
        head_l, head_r = from_left(head), from_right(head)
        inflow = (
            tau_u * (head_u - head)
            + tau_d * (head_d - head)
            + tau_l * (head_l - head)
            + tau_r * (head_r - head)
        )
        return tau * inflow, tau * (tau_u + tau_d + tau_l + tau_r)

    start_in, start_sum = flow(base, h_base, root, h_root)
    rhs = rest - start_in
    first = base + RELAX * rest / (cap + start_sum)
    h_diag = h_cap + h_root * (o_root + root + sides(h_root))
    h_first = h_base + jnp.where(h_live, RELAX * h_rest / jnp.where(h_live, h_diag, 1.0), 0.0)
    half = 0.5 / depth_total
    tau = root * jnp.exp(half * rate * jnp.tanh(first - base))
    h_tau = h_root * jnp.exp(half * h_rate * jnp.tanh(h_first - h_base))
    first_in, first_sum = flow(first, h_first, tau, h_tau)
    first_flow = cap * (first - base) - first_in
    second = first - RELAX * (first_flow - rhs) / (cap + first_sum)
    head_ref[...] = second
    shift = second - base
    out_ref[...] = smooth_ref[...] + shift[None]


def shards(pressure, theta_old, source, soil_type, soil_params):
    layers, rows, width = pressure.shape
    areas = lax.axis_size("area")
    depths = lax.axis_size("depth")
    swap = depths == 2
    both = ("area", "depth")
    even_moves = full_swap([(i, i + 1) for i in range(0, areas - 1, 2)], areas, depths)
    odd_moves = full_swap([(i, i + 1) for i in range(1, areas - 1, 2)], areas, depths)
    down = [(i, i + 1) for i in range(depths - 1)]
    up = [(b, a) for a, b in down]
    swapped = [(0, 1), (1, 0)]

    def shape(*dims):
        return jax.ShapeDtypeStruct(dims, F32)

    params = pltpu.CompilerParams(vmem_limit_bytes=16 << 20)
    verts = 1 if swap else 2
    kind_count = soil_params.shape[1]
    in_hbm = [
        pltpu.with_memory_space_constraint(x, pltpu.HBM)
        for x in (pressure, soil_type, soil_params)
    ]
    packed = pl.pallas_call(
        functools.partial(pack_kernel, swap),
        out_shape=[shape(5, kind_count, 8, LANES)]
        + [shape(2, layers, width)] * 2
        + [shape(2, rows, width)] * verts,
        in_specs=[pl.BlockSpec(memory_space=pltpu.HBM)] * 3,
        out_specs=whole(3 + verts),
        scratch_shapes=[
            pltpu.VMEM((2, layers, width), F32),
            pltpu.VMEM((2, layers, width), jnp.int32),
            pltpu.VMEM((verts, rows, width), F32),
            pltpu.VMEM((verts, rows, width), jnp.int32),
            pltpu.VMEM(soil_params.shape, F32),
            pltpu.SemaphoreType.DMA((5 + 2 * verts,)),
        ],
        compiler_params=params,
        cost_estimate=pl.CostEstimate(flops=PACK_COST, transcendentals=0, bytes_accessed=0),
        name="pack",
    )(*in_hbm)
    from_odd = lax.ppermute(packed[2], both, odd_moves)
    from_even = lax.ppermute(packed[1], both, even_moves)
    if swap:
        vert = [lax.ppermute(packed[3], "depth", swapped)]
    else:
        vert = [lax.ppermute(packed[3], "depth", down), lax.ppermute(packed[4], "depth", up)]
    kept, kap, local_sums = pl.pallas_call(
        local_kernel,
        out_shape=[shape(6, layers, rows, width), shape(layers, rows, width), shape(2, rows, width)],
        in_specs=whole(5),
        out_specs=whole(3),
        compiler_params=params,
        name="local",
    )(pressure, theta_old, source, soil_type, packed[0])
    smooth, sums, to_even, to_odd, rim = pl.pallas_call(
        functools.partial(fine_kernel, swap),
        out_shape=[
            shape(layers, rows, width),
            shape(5, rows, width),
            shape(layers + 8, width),
            shape(layers + 8, width),
            shape(2, 4, layers, width),
        ],
        in_specs=whole(7 + verts),
        out_specs=whole(5),
        scratch_shapes=[pltpu.VMEM((2, layers, width), F32)],
        compiler_params=params,
        name="fine",
    )(pressure, kept, kap, local_sums, packed[0], from_even, from_odd, *vert)
    from_odd = lax.ppermute(to_odd, both, odd_moves)
    from_even = lax.ppermute(to_even, both, even_moves)
    if swap:
        their_sums = lax.ppermute(sums, "depth", swapped)
    else:
        sums, their_sums = lax.psum(sums, "depth"), jnp.zeros_like(sums)
    halo = pl.pallas_call(
        edge_kernel,
        out_shape=shape(2, 8, width),
        in_specs=whole(5),
        out_specs=whole(1)[0],
        compiler_params=params,
        name="edge",
    )(rim, to_odd, to_even, from_odd, from_even)
    if swap:
        their_halo = lax.ppermute(halo, "depth", swapped)
    else:
        halo, their_halo = lax.psum(halo, "depth"), jnp.zeros_like(halo)
    out, head = pl.pallas_call(
        functools.partial(coarse_kernel, layers * depths),
        out_shape=[shape(layers, rows, width), shape(rows, width)],
        in_specs=whole(5),
        out_specs=whole(2),
        compiler_params=params,
        name="coarse",
    )(smooth, sums, their_sums, halo, their_halo)
    return out, head


def solution(mesh):
    in_specs = (
        P("depth", "area", None),
        P("depth", "area", None),
        P("depth", "area", None),
        P("depth", "area", None),
        P(),
    )
    out_specs = (P("depth", "area", None), P("area", None))
    return jax.shard_map(shards, mesh=mesh, in_specs=in_specs, out_specs=out_specs, check_vma=False)
```

```python
import functools
import math

import jax
import jax.numpy as jnp
from jax import lax
from jax.experimental import pallas as pl
from jax.experimental.pallas import tpu as pltpu
from jax.sharding import PartitionSpec as P

INV_DT = 10.0
RELAX = 0.8
SMALL = 0.04
LOG2E = math.log2(math.e)
LANES = 128
PACK_COST = 4_000_000_000
EDGE_COST = 1_000_000_000
F32 = jnp.float32

T_A, T_N, T_SK, T_D, T_R = range(5)


def whole(count):
    return [pl.BlockSpec(memory_space=pltpu.VMEM)] * count


def build_table(params_ref):
    alpha = params_ref[2:3, :]
    return {
        T_A: jnp.log(alpha) * LOG2E,
        T_N: params_ref[3:4, :],
        T_SK: jnp.sqrt(params_ref[4:5, :]),
        T_D: (params_ref[1:2, :] - params_ref[0:1, :]) * INV_DT,
        T_R: params_ref[0:1, :] * INV_DT,
    }


def spread_table(table, tab_ref):
    for row_id, row in table.items():
        for kind in range(row.shape[1]):
            tab_ref[row_id, kind] = jnp.broadcast_to(row[:, kind : kind + 1], (8, LANES))


def pick(tab_ref, row_id, bits, width):
    level = [
        jnp.tile(tab_ref[row_id, kind], (bits[0].shape[0] // 8, width // LANES))
        for kind in range(tab_ref.shape[1])
    ]
    for bit in bits:
        pairs = [
            jnp.where(bit, level[i + 1], level[i]) for i in range(0, len(level) - 1, 2)
        ]
        level = pairs + ([level[-1]] if len(level) % 2 else [])
    return level[0]


def type_bits(kinds, count):
    return [(kinds & (1 << i)) != 0 for i in range((count - 1).bit_length())]


def power(pn):
    return (1.0 / pn - 1.0) * (0.25 * LOG2E)


def hydraulics(h, pa, pn, pc, psk):
    q = h * h + SMALL
    u = jnp.exp2(pn * (pa + (0.5 * LOG2E) * jnp.log(q)))
    one_plus = 1.0 + u
    inv = 1.0 / one_plus
    ratio = u * inv
    quarter = jnp.exp2(pc * jnp.log(one_plus))
    w = jnp.exp2((-4.0 * pc) * jnp.log(ratio))
    kappa = psk * quarter * (1.0 - w)
    half = quarter * quarter
    return kappa, half * half, ratio * lax.rsqrt(q)


def code(kinds):
    return (kinds + 1).astype(F32)


def code_params(codes, tab_ref):
    kinds = jnp.maximum(codes.astype(jnp.int32) - 1, 0)
    bits = type_bits(kinds, tab_ref.shape[1])
    pa, pn, psk, pd = [pick(tab_ref, i, bits, codes.shape[1]) for i in (T_A, T_N, T_SK, T_D)]
    return pa, pn, power(pn), jnp.where(codes > 0.5, psk, 0.0), pd


def even_area():
    return lax.rem(lax.axis_index("area"), 2) == 0


def paired():
    area, last = lax.axis_index("area"), lax.axis_size("area") - 1
    is_even = even_area()
    return (
        jnp.logical_or(jnp.logical_not(is_even), area < last),
        jnp.where(is_even, area, last - area) > 0,
    )


def full_swap(pairs, areas, depths):
    target = {a: b for a, b in pairs}
    target.update({b: a for a, b in pairs})
    moves = []
    for a in range(areas):
        for d in range(depths):
            other = d if a in target else d ^ 1
            if other < depths:
                moves.append((a * depths + d, target.get(a, a) * depths + other))
    return moves


def pack_kernel(swap, p_ref, soil_ref, params_ref, tab_ref, even_ref, odd_ref, *rest):
    layers, rows, _ = p_ref.shape
    count = 1 if swap else 2
    vert_refs = rest[:count]
    p_buf, soil_buf, vert_p, vert_soil, params_buf, sems = rest[count:]
    even = even_area()
    if swap:
        spots = [jnp.where(lax.axis_index("depth") == 0, layers - 1, 0)]
    else:
        spots = [layers - 1, 0]
    copies = [(params_ref, params_buf)]
    for side, row in enumerate((0, rows - 1)):
        copies.append((p_ref.at[:, row, :], p_buf.at[side]))
        copies.append((soil_ref.at[:, row, :], soil_buf.at[side]))
    for side, spot in enumerate(spots):
        copies.append((p_ref.at[spot], vert_p.at[side]))
        copies.append((soil_ref.at[spot], vert_soil.at[side]))
    copies = [
        pltpu.make_async_copy(source, target, sems.at[i])
        for i, (source, target) in enumerate(copies)
    ]
    for copy in copies:
        copy.start()
    copies[0].wait()
    spread_table(build_table(params_buf), tab_ref)
    for copy in copies[1:]:
        copy.wait()
    for i, low, high in ((0, p_buf[0], p_buf[1]), (1, code(soil_buf[0]), code(soil_buf[1]))):
        even_ref[i] = jnp.where(even, high, low)
        odd_ref[i] = jnp.where(even, low, high)
    for side, out_ref in enumerate(vert_refs):
        out_ref[0] = vert_p[side]
        out_ref[1] = code(vert_soil[side])


def row_iota(shape):
    return lax.broadcasted_iota(jnp.int32, shape, 0)


def lane_iota(shape):
    return lax.broadcasted_iota(jnp.int32, shape, 1)


def from_above(x, edge):
    return jnp.where(row_iota(x.shape) == 0, edge, pltpu.roll(x, 1, 0))


def from_below(x, edge):
    last = x.shape[0] - 1
    return jnp.where(row_iota(x.shape) == last, edge, pltpu.roll(x, last, 0))


def from_left(x):
    return jnp.where(lane_iota(x.shape) == 0, 0.0, pltpu.roll(x, 1, 1))


def from_right(x):
    last = x.shape[1] - 1
    return jnp.where(lane_iota(x.shape) == last, 0.0, pltpu.roll(x, last, 1))


def local_kernel(
    p_ref, theta_ref, source_ref, soil_ref, tab_ref, kept_ref, kap_ref, sums_ref
):
    layers, rows, width = p_ref.shape
    kind_count = tab_ref.shape[1]

    sum_fixed = sum_rate = jnp.zeros((rows, width), F32)
    held = None
    for layer in range(layers):
        bits = type_bits(soil_ref[layer], kind_count)
        pa, pn, psk, pd, pr = [pick(tab_ref, i, bits, width) for i in range(5)]
        pc, pcap = power(pn), pd * (pn - 1.0)
        h = p_ref[layer]
        kap, sat, over = hydraulics(h, pa, pn, pc, psk)
        fixed = pr - INV_DT * theta_ref[layer] - source_ref[layer]
        k_l, k_r = from_left(kap), from_right(kap)
        k_u, k_d = from_above(kap, 0.0), from_below(kap, 0.0)
        inflow = (
            k_l * (pltpu.roll(h, 1, 1) - h)
            + k_r * (pltpu.roll(h, width - 1, 1) - h)
            + k_u * (pltpu.roll(h, 1, 0) - h)
            + k_d * (pltpu.roll(h, rows - 1, 0) - h)
        )
        total = (k_l + k_r) + (k_u + k_d)
        kap_ref[layer] = kap
        for i, field in enumerate((pa, pn, pc, psk, pd, pcap)):
            kept_ref[2 + i, layer] = field
        sum_fixed, sum_rate = sum_fixed + fixed, sum_rate + jnp.exp2(pa)
        if held is not None:
            o_h, o_kap, o_inflow, o_total, o_fixed, o_cap = held
            inflow = inflow + o_kap * (o_h - h + 1.0)
            total = total + o_kap
            o_inflow = o_inflow + kap * (h - o_h - 1.0)
            kept_ref[0, layer - 1] = o_fixed - o_kap * o_inflow
            kept_ref[1, layer - 1] = o_cap + o_kap * (o_total + kap)
        held = (h, kap, inflow, total, pd * sat + fixed, pcap * sat * over)
    _, kap, inflow, total, fixed, cap = held
    kept_ref[0, layers - 1] = fixed - kap * inflow
    kept_ref[1, layers - 1] = cap + kap * total
    sums_ref[0] = sum_fixed
    sums_ref[1] = sum_rate


def rim_kernel(odd, from_ref, tab_ref, rim_ref):
    live = paired()[odd]

    def step(i, carry):
        at = pl.ds(i * 8, 8)
        fields = code_params(jnp.where(live, from_ref[1, at, :], 0.0), tab_ref)
        for spot, field in enumerate(fields):
            rim_ref[spot, at, :] = field
        rim_ref[5, at, :] = hydraulics(from_ref[0, at, :], *fields[:4])[0]
        return carry

    lax.fori_loop(0, from_ref.shape[1] // 8, step, 0, unroll=True)


def tail_spots(layers, width):
    chunks = 2 * width // LANES
    return [(j % layers, width + j // layers * LANES) for j in range(chunks)]


def sent_width(layers, width):
    return width + pl.cdiv(2 * width // LANES, layers) * LANES


def fine_kernel(
    swap,
    p_ref,
    kept_ref,
    kap_ref,
    local_ref,
    tab_ref,
    from_even_ref,
    from_odd_ref,
    rim_even_ref,
    rim_odd_ref,
    *rest,
):
    layers, rows, width = p_ref.shape
    verts = 1 if swap else 2
    vert_refs = rest[:verts]
    smooth_ref, sums_ref, to_even_ref, to_odd_ref, mine_ref, side_ref, edge_ref = rest[verts:]
    even = even_area()
    spot = row_iota((rows, width))
    is_first, is_last = spot == 0, spot == rows - 1

    for i, by_even, by_odd in (
        (0, rim_even_ref[5], rim_odd_ref[5]),
        (2, from_even_ref[0], from_odd_ref[0]),
    ):
        side_ref[i] = jnp.where(even, by_odd, by_even)
        side_ref[i + 1] = jnp.where(even, by_even, by_odd)
    vert = [(ref[0], hydraulics(ref[0], *code_params(ref[1], tab_ref)[:4])[0]) for ref in vert_refs]
    if swap:
        at_top = lax.axis_index("depth") == 0
        ((vert_h, vert_k),) = vert
        top_h = bottom_h = vert_h
        top_k = jnp.where(at_top, 0.0, vert_k)
        bottom_k = jnp.where(at_top, vert_k, 0.0)
    else:
        (top_h, top_k), (bottom_h, bottom_k) = vert

    sum_kh = sum_k = sum_cap = sum_sat = flux_x = flux_y = jnp.zeros((rows, width), F32)
    for layer in range(layers):
        h = p_ref[layer]
        kap = kap_ref[layer]
        lo_k, hi_k, lo_h, hi_h = [side_ref[i, layer : layer + 1, :] for i in range(4)]
        total = jnp.where(is_first, lo_k, jnp.where(is_last, hi_k, 0.0))
        inflow = total * (jnp.where(is_first, lo_h, hi_h) - h)
        if layer == 0:
            inflow, total = inflow + top_k * (top_h - h + 1.0), total + top_k
        if layer == layers - 1:
            inflow, total = inflow + bottom_k * (bottom_h - h - 1.0), total + bottom_k
        balance = kept_ref[0, layer] - kap * inflow
        diagonal = kept_ref[1, layer] + kap * total
        h = h - RELAX * balance / diagonal
        smooth_ref[layer] = h

        pa, pn, pc, psk, pd, pcap = [kept_ref[2 + i, layer] for i in range(6)]
        kap, sat, over = hydraulics(h, pa, pn, pc, psk)
        cond = kap * kap
        flux_x = flux_x + kap * from_below(kap, 0.0) * (pltpu.roll(h, rows - 1, 0) - h)
        flux_y = flux_y + kap * from_right(kap) * (pltpu.roll(h, width - 1, 1) - h)
        for i, value in enumerate((h, kap)):
            edge_ref[2 * i, layer : layer + 1, :] = value[0:1, :]
            edge_ref[2 * i + 1, layer : layer + 1, :] = value[rows - 1 : rows, :]
        sum_kh = sum_kh + cond * h
        sum_k = sum_k + cond
        sum_cap = sum_cap + pcap * sat * over
        sum_sat = sum_sat + pd * sat

    restricted = (
        (flux_x - from_above(flux_x, 0.0)) + (flux_y - from_left(flux_y)) - sum_sat - local_ref[0]
    )
    for at, value in enumerate((sum_kh, sum_k, sum_cap, restricted, local_ref[1])):
        sums_ref[at] = value
    low_h, high_h, low_k, high_k = [edge_ref[i] for i in range(4)]
    to_even_ref[:, 0:width] = jnp.where(even, high_h, low_h)
    to_odd_ref[:, 0:width] = jnp.where(even, low_h, high_h)
    mine_ref[0] = jnp.where(even, high_k, low_k)
    mine_ref[1] = jnp.where(even, low_k, high_k)
    low_tail = jnp.concatenate([restricted[0:1], sum_k[1:2]], axis=1)
    high_tail = jnp.concatenate([restricted[rows - 1 : rows], sum_k[rows - 2 : rows - 1]], axis=1)
    for out_ref, tail in (
        (to_even_ref, jnp.where(even, high_tail, low_tail)),
        (to_odd_ref, jnp.where(even, low_tail, high_tail)),
    ):
        for j, (row, lane) in enumerate(tail_spots(layers, width)):
            out_ref[row : row + 1, lane : lane + LANES] = tail[:, j * LANES : (j + 1) * LANES]


def edge_kernel(
    rim_odd_ref,
    rim_even_ref,
    mine_ref,
    to_odd_ref,
    to_even_ref,
    from_odd_ref,
    from_even_ref,
    halo_ref,
):
    _, layers, width = rim_odd_ref.shape
    sides = (
        (rim_even_ref, to_even_ref, from_even_ref),
        (rim_odd_ref, to_odd_ref, from_odd_ref),
    )
    for side, (live, (rim_ref, to_ref, from_ref)) in enumerate(zip(paired(), sides)):
        pa, pn, pc, psk, pd = [rim_ref[i] for i in range(5)]
        theirs = from_ref[:, 0:width]
        kap, sat, over = hydraulics(theirs, pa, pn, pc, psk)
        cond = kap * kap
        tail = jnp.concatenate(
            [
                from_ref[row : row + 1, lane : lane + LANES]
                for row, lane in tail_spots(layers, width)
            ],
            axis=1,
        )

        def total(x):
            return jnp.sum(x, axis=0, keepdims=True)

        flux = total(mine_ref[side] * kap * (theirs - to_ref[:, 0:width]))
        block = jnp.concatenate(
            [
                total(cond * theirs),
                total(cond),
                total(pd * (pn - 1.0) * sat * over),
                tail[:, 0:width] - flux,
                tail[:, width:],
                total(jnp.exp2(pa)),
                flux,
                jnp.zeros_like(flux),
            ],
            axis=0,
        )
        halo_ref[side] = jnp.where(live, block, 0.0)


def columns_kernel(sums_ref, their_sums_ref, columns_ref):
    kh, kk, cap, rest, rate = [sums_ref[i] + their_sums_ref[i] for i in range(5)]
    for i, value in enumerate((kh / kk, jnp.sqrt(kk), cap, rest, rate)):
        columns_ref[i] = value


def coarse_kernel(
    depth_total, smooth_ref, columns_ref, halo_ref, their_halo_ref, out_ref, head_ref
):
    rows = smooth_ref.shape[1]
    base, root, cap, rest, rate = [columns_ref[i] for i in range(5)]
    by_even = halo_ref[0] + their_halo_ref[0]
    by_odd = halo_ref[1] + their_halo_ref[1]
    even = even_area()
    lo = jnp.where(even, by_odd, by_even)
    hi = jnp.where(even, by_even, by_odd)
    spot = row_iota(rest.shape)
    rest = jnp.where(spot == 0, rest + lo[6:7], rest)
    rest = jnp.where(spot == rows - 1, rest + hi[6:7], rest)

    def pair(i):
        return jnp.where(spot == 0, lo[i : i + 1], jnp.where(spot == rows - 1, hi[i : i + 1], 0.0))

    h_kh, h_k, h_cap, h_rest, o_k, h_rate = [pair(i) for i in range(6)]
    edge_lane = lane_iota(rest.shape)

    def sides(x):
        return from_left(x) + from_right(x)

    h_live = h_k > 0.0
    h_base = jnp.where(h_live, h_kh / jnp.where(h_live, h_k, 1.0), 0.0)
    h_root = jnp.sqrt(h_k)
    o_root = jnp.sqrt(o_k)

    def around(x, halo):
        return from_above(x, halo[0:1]), from_below(x, halo[rows - 1 : rows])

    def flow(head, halo_head, tau, halo_tau):
        tau_u, tau_d = around(tau, halo_tau)
        head_u, head_d = around(head, halo_head)
        tau_l, tau_r = from_left(tau), from_right(tau)
        head_l, head_r = from_left(head), from_right(head)
        inflow = (
            tau_u * (head_u - head)
            + tau_d * (head_d - head)
            + tau_l * (head_l - head)
            + tau_r * (head_r - head)
        )
        return tau * inflow, tau * (tau_u + tau_d + tau_l + tau_r)

    start_in, start_sum = flow(base, h_base, root, h_root)
    rhs = rest - start_in
    first = base + RELAX * rest / (cap + start_sum)
    h_diag = h_cap + h_root * (o_root + root + sides(h_root))
    h_first = h_base + jnp.where(h_live, RELAX * h_rest / jnp.where(h_live, h_diag, 1.0), 0.0)
    half = 0.5 / depth_total
    tau = root * jnp.exp(half * rate * jnp.tanh(first - base))
    h_tau = h_root * jnp.exp(half * h_rate * jnp.tanh(h_first - h_base))
    first_in, first_sum = flow(first, h_first, tau, h_tau)
    first_flow = cap * (first - base) - first_in
    second = first - RELAX * (first_flow - rhs) / (cap + first_sum)
    head_ref[...] = second
    shift = second - base
    out_ref[...] = smooth_ref[...] + shift[None]


def shards(pressure, theta_old, source, soil_type, soil_params):
    layers, rows, width = pressure.shape
    areas = lax.axis_size("area")
    depths = lax.axis_size("depth")
    swap = depths == 2
    both = ("area", "depth")
    even_moves = full_swap([(i, i + 1) for i in range(0, areas - 1, 2)], areas, depths)
    odd_moves = full_swap([(i, i + 1) for i in range(1, areas - 1, 2)], areas, depths)
    down = [(i, i + 1) for i in range(depths - 1)]
    up = [(b, a) for a, b in down]
    swapped = [(0, 1), (1, 0)]

    def shape(*dims):
        return jax.ShapeDtypeStruct(dims, F32)

    params = pltpu.CompilerParams(vmem_limit_bytes=16 << 20)
    verts = 1 if swap else 2
    kind_count = soil_params.shape[1]
    in_hbm = [
        pltpu.with_memory_space_constraint(x, pltpu.HBM)
        for x in (pressure, soil_type, soil_params)
    ]
    packed = pl.pallas_call(
        functools.partial(pack_kernel, swap),
        out_shape=[shape(5, kind_count, 8, LANES)]
        + [shape(2, layers, width)] * 2
        + [shape(2, rows, width)] * verts,
        in_specs=[pl.BlockSpec(memory_space=pltpu.HBM)] * 3,
        out_specs=whole(3 + verts),
        scratch_shapes=[
            pltpu.VMEM((2, layers, width), F32),
            pltpu.VMEM((2, layers, width), jnp.int32),
            pltpu.VMEM((verts, rows, width), F32),
            pltpu.VMEM((verts, rows, width), jnp.int32),
            pltpu.VMEM(soil_params.shape, F32),
            pltpu.SemaphoreType.DMA((5 + 2 * verts,)),
        ],
        compiler_params=params,
        cost_estimate=pl.CostEstimate(flops=PACK_COST, transcendentals=0, bytes_accessed=0),
        name="pack",
    )(*in_hbm)
    from_odd = lax.ppermute(packed[2], both, odd_moves)
    from_even = lax.ppermute(packed[1], both, even_moves)
    if swap:
        vert = [lax.ppermute(packed[3], "depth", swapped)]
    else:
        vert = [lax.ppermute(packed[3], "depth", down), lax.ppermute(packed[4], "depth", up)]
    kept, kap, local_sums = pl.pallas_call(
        local_kernel,
        out_shape=[shape(8, layers, rows, width), shape(layers, rows, width), shape(2, rows, width)],
        in_specs=whole(5),
        out_specs=whole(3),
        compiler_params=params,
        name="local",
    )(pressure, theta_old, source, soil_type, packed[0])
    rims = [
        pl.pallas_call(
            functools.partial(rim_kernel, odd),
            out_shape=shape(6, layers, width),
            in_specs=whole(2),
            out_specs=whole(1)[0],
            compiler_params=params,
            name="rim",
        )(from_area, packed[0])
        for odd, from_area in enumerate((from_even, from_odd))
    ]
    sent = shape(layers, sent_width(layers, width))
    smooth, sums, to_even, to_odd, mine = pl.pallas_call(
        functools.partial(fine_kernel, swap),
        out_shape=[
            shape(layers, rows, width),
            shape(5, rows, width),
            sent,
            sent,
            shape(2, layers, width),
        ],
        in_specs=whole(9 + verts),
        out_specs=whole(5),
        scratch_shapes=[pltpu.VMEM((4, layers, width), F32)] * 2,
        compiler_params=params,
        name="fine",
    )(pressure, kept, kap, local_sums, packed[0], from_even, from_odd, *rims, *vert)
    from_odd = lax.ppermute(to_odd, both, odd_moves)
    from_even = lax.ppermute(to_even, both, even_moves)
    if swap:
        their_sums = lax.ppermute(sums, "depth", swapped)
    else:
        sums, their_sums = lax.psum(sums, "depth"), jnp.zeros_like(sums)
    halo = pl.pallas_call(
        edge_kernel,
        out_shape=shape(2, 8, width),
        in_specs=whole(7),
        out_specs=whole(1)[0],
        cost_estimate=pl.CostEstimate(flops=EDGE_COST, transcendentals=0, bytes_accessed=0),
        compiler_params=params,
        name="edge",
    )(rims[1], rims[0], mine, to_odd, to_even, from_odd, from_even)
    if swap:
        their_halo = lax.ppermute(halo, "depth", swapped)
    else:
        halo, their_halo = lax.psum(halo, "depth"), jnp.zeros_like(halo)
    columns = pl.pallas_call(
        columns_kernel,
        out_shape=shape(5, rows, width),
        in_specs=whole(2),
        out_specs=whole(1)[0],
        compiler_params=params,
        name="columns",
    )(sums, their_sums)
    out, head = pl.pallas_call(
        functools.partial(coarse_kernel, layers * depths),
        out_shape=[shape(layers, rows, width), shape(rows, width)],
        in_specs=whole(4),
        out_specs=whole(2),
        compiler_params=params,
        name="coarse",
    )(smooth, columns, halo, their_halo)
    return out, head


def solution(mesh):
    in_specs = (
        P("depth", "area", None),
        P("depth", "area", None),
        P("depth", "area", None),
        P("depth", "area", None),
        P(),
    )
    out_specs = (P("depth", "area", None), P("area", None))
    return jax.shard_map(shards, mesh=mesh, in_specs=in_specs, out_specs=out_specs, check_vma=False)
```

```python
import functools
import math

import jax
import jax.numpy as jnp
from jax import lax
from jax.experimental import pallas as pl
from jax.experimental.pallas import tpu as pltpu
from jax.sharding import PartitionSpec as P

INV_DT = 10.0
RELAX = 0.8
SMALL = 0.04
LOG2E = math.log2(math.e)
LANES = 128
PACK_COST = 4_000_000_000
EDGE_COST = 1000_000_000
F32 = jnp.float32

T_A, T_N, T_SK, T_D, T_R = range(5)
GATHERED = (2, 3, 4,)


def whole(count):
    return [pl.BlockSpec(memory_space=pltpu.VMEM)] * count


def build_table(params_ref):
    alpha = params_ref[2:3, :]
    return {
        T_A: jnp.log(alpha) * LOG2E,
        T_N: params_ref[3:4, :],
        T_SK: jnp.sqrt(params_ref[4:5, :]),
        T_D: (params_ref[1:2, :] - params_ref[0:1, :]) * INV_DT,
        T_R: params_ref[0:1, :] * INV_DT,
    }


def gather(table, kinds):
    return jnp.concatenate(
        [
            jnp.take_along_axis(
                table, kinds[:, c : c + LANES], axis=1, mode="promise_in_bounds"
            )
            for c in range(0, kinds.shape[1], LANES)
        ],
        axis=1,
    )


def spread_table(table, tab_ref, rows_ref):
    for row_id, row in table.items():
        rows_ref[row_id, :, 0 : row.shape[1]] = jnp.broadcast_to(row, (8, row.shape[1]))
        for kind in range(row.shape[1]):
            tab_ref[row_id, kind] = jnp.broadcast_to(row[:, kind : kind + 1], (8, LANES))


def pick(tab_ref, row_id, bits, width):
    level = [
        jnp.tile(tab_ref[row_id, kind], (bits[0].shape[0] // 8, width // LANES))
        for kind in range(tab_ref.shape[1])
    ]
    for bit in bits:
        pairs = [
            jnp.where(bit, level[i + 1], level[i]) for i in range(0, len(level) - 1, 2)
        ]
        level = pairs + ([level[-1]] if len(level) % 2 else [])
    return level[0]


def type_bits(kinds, count):
    return [(kinds & (1 << i)) != 0 for i in range((count - 1).bit_length())]


def power(pn):
    return (1.0 / pn - 1.0) * (0.25 * LOG2E)


def hydraulics(h, pa, pn, pc, psk):
    q = h * h + SMALL
    u = jnp.exp2(pn * (pa + (0.5 * LOG2E) * jnp.log(q)))
    one_plus = 1.0 + u
    inv = 1.0 / one_plus
    ratio = u * inv
    quarter = jnp.exp2(pc * jnp.log(one_plus))
    w = jnp.exp2((-4.0 * pc) * jnp.log(ratio))
    kappa = psk * quarter * (1.0 - w)
    half = quarter * quarter
    return kappa, half * half, ratio * lax.rsqrt(q)


def code(kinds):
    return (kinds + 1).astype(F32)


def code_params(codes, tab_ref):
    kinds = jnp.maximum(codes.astype(jnp.int32) - 1, 0)
    bits = type_bits(kinds, tab_ref.shape[1])
    pa, pn, psk, pd = [pick(tab_ref, i, bits, codes.shape[1]) for i in (T_A, T_N, T_SK, T_D)]
    return pa, pn, power(pn), jnp.where(codes > 0.5, psk, 0.0), pd


def even_area():
    return lax.rem(lax.axis_index("area"), 2) == 0


def paired():
    area, last = lax.axis_index("area"), lax.axis_size("area") - 1
    is_even = even_area()
    return (
        jnp.logical_or(jnp.logical_not(is_even), area < last),
        jnp.where(is_even, area, last - area) > 0,
    )


def full_swap(pairs, areas, depths):
    target = {a: b for a, b in pairs}
    target.update({b: a for a, b in pairs})
    moves = []
    for a in range(areas):
        for d in range(depths):
            other = d if a in target else d ^ 1
            if other < depths:
                moves.append((a * depths + d, target.get(a, a) * depths + other))
    return moves


def pack_kernel(swap, p_ref, soil_ref, params_ref, tab_ref, rows_ref, even_ref, odd_ref, *rest):
    layers, rows, _ = p_ref.shape
    count = 1 if swap else 2
    vert_refs = rest[:count]
    p_buf, soil_buf, vert_p, vert_soil, params_buf, sems = rest[count:]
    even = even_area()
    if swap:
        spots = [jnp.where(lax.axis_index("depth") == 0, layers - 1, 0)]
    else:
        spots = [layers - 1, 0]
    copies = [(params_ref, params_buf)]
    for side, row in enumerate((0, rows - 1)):
        copies.append((p_ref.at[:, row, :], p_buf.at[side]))
        copies.append((soil_ref.at[:, row, :], soil_buf.at[side]))
    for side, spot in enumerate(spots):
        copies.append((p_ref.at[spot], vert_p.at[side]))
        copies.append((soil_ref.at[spot], vert_soil.at[side]))
    copies = [
        pltpu.make_async_copy(source, target, sems.at[i])
        for i, (source, target) in enumerate(copies)
    ]
    for copy in copies:
        copy.start()
    copies[0].wait()
    spread_table(build_table(params_buf), tab_ref, rows_ref)
    for copy in copies[1:]:
        copy.wait()
    for i, low, high in ((0, p_buf[0], p_buf[1]), (1, code(soil_buf[0]), code(soil_buf[1]))):
        even_ref[i] = jnp.where(even, high, low)
        odd_ref[i] = jnp.where(even, low, high)
    for side, out_ref in enumerate(vert_refs):
        out_ref[0] = vert_p[side]
        out_ref[1] = code(vert_soil[side])


def row_iota(shape):
    return lax.broadcasted_iota(jnp.int32, shape, 0)


def lane_iota(shape):
    return lax.broadcasted_iota(jnp.int32, shape, 1)


def from_above(x, edge):
    return jnp.where(row_iota(x.shape) == 0, edge, pltpu.roll(x, 1, 0))


def from_below(x, edge):
    last = x.shape[0] - 1
    return jnp.where(row_iota(x.shape) == last, edge, pltpu.roll(x, last, 0))


def from_left(x):
    return jnp.where(lane_iota(x.shape) == 0, 0.0, pltpu.roll(x, 1, 1))


def from_right(x):
    last = x.shape[1] - 1
    return jnp.where(lane_iota(x.shape) == last, 0.0, pltpu.roll(x, last, 1))


def local_kernel(
    p_ref, theta_ref, source_ref, soil_ref, tab_ref, rows_ref, kept_ref, kap_ref, sums_ref
):
    layers, rows, width = p_ref.shape
    kind_count = tab_ref.shape[1]

    sum_fixed = sum_rate = jnp.zeros((rows, width), F32)
    held = None
    for layer in range(layers):
        bits = type_bits(soil_ref[layer], kind_count)
        pa, pn, psk, pd, pr = [
            gather(rows_ref[i], soil_ref[layer]) if i in GATHERED else pick(tab_ref, i, bits, width)
            for i in range(5)
        ]
        pc, pcap = power(pn), pd * (pn - 1.0)
        h = p_ref[layer]
        kap, sat, over = hydraulics(h, pa, pn, pc, psk)
        fixed = pr - INV_DT * theta_ref[layer] - source_ref[layer]
        k_l, k_r = from_left(kap), from_right(kap)
        k_u, k_d = from_above(kap, 0.0), from_below(kap, 0.0)
        inflow = (
            k_l * (pltpu.roll(h, 1, 1) - h)
            + k_r * (pltpu.roll(h, width - 1, 1) - h)
            + k_u * (pltpu.roll(h, 1, 0) - h)
            + k_d * (pltpu.roll(h, rows - 1, 0) - h)
        )
        total = (k_l + k_r) + (k_u + k_d)
        kap_ref[layer] = kap
        for i, field in enumerate((pa, pn, pc, psk, pd, pcap)):
            kept_ref[2 + i, layer] = field
        sum_fixed, sum_rate = sum_fixed + fixed, sum_rate + jnp.exp2(pa)
        if held is not None:
            o_h, o_kap, o_inflow, o_total, o_fixed, o_cap = held
            inflow = inflow + o_kap * (o_h - h + 1.0)
            total = total + o_kap
            o_inflow = o_inflow + kap * (h - o_h - 1.0)
            kept_ref[0, layer - 1] = o_fixed - o_kap * o_inflow
            kept_ref[1, layer - 1] = o_cap + o_kap * (o_total + kap)
        held = (h, kap, inflow, total, pd * sat + fixed, pcap * sat * over)
    _, kap, inflow, total, fixed, cap = held
    kept_ref[0, layers - 1] = fixed - kap * inflow
    kept_ref[1, layers - 1] = cap + kap * total
    sums_ref[0] = sum_fixed
    sums_ref[1] = sum_rate


def rim_kernel(odd, from_ref, tab_ref, rim_ref):
    live = paired()[odd]

    def step(i, carry):
        at = pl.ds(i * 8, 8)
        fields = code_params(jnp.where(live, from_ref[1, at, :], 0.0), tab_ref)
        for spot, field in enumerate(fields):
            rim_ref[spot, at, :] = field
        rim_ref[5, at, :] = hydraulics(from_ref[0, at, :], *fields[:4])[0]
        return carry

    lax.fori_loop(0, from_ref.shape[1] // 8, step, 0, unroll=True)


def tail_spots(layers, width):
    chunks = 2 * width // LANES
    return [(j % layers, width + j // layers * LANES) for j in range(chunks)]


def sent_width(layers, width):
    return width + pl.cdiv(2 * width // LANES, layers) * LANES


def fine_kernel(
    swap,
    p_ref,
    kept_ref,
    kap_ref,
    local_ref,
    tab_ref,
    from_even_ref,
    from_odd_ref,
    rim_even_ref,
    rim_odd_ref,
    *rest,
):
    layers, rows, width = p_ref.shape
    verts = 1 if swap else 2
    vert_refs = rest[:verts]
    smooth_ref, sums_ref, to_even_ref, to_odd_ref, mine_ref, side_ref, edge_ref = rest[verts:]
    even = even_area()
    spot = row_iota((rows, width))
    is_first, is_last = spot == 0, spot == rows - 1

    for i, by_even, by_odd in (
        (0, rim_even_ref[5], rim_odd_ref[5]),
        (2, from_even_ref[0], from_odd_ref[0]),
    ):
        side_ref[i] = jnp.where(even, by_odd, by_even)
        side_ref[i + 1] = jnp.where(even, by_even, by_odd)
    vert = [(ref[0], hydraulics(ref[0], *code_params(ref[1], tab_ref)[:4])[0]) for ref in vert_refs]
    if swap:
        at_top = lax.axis_index("depth") == 0
        ((vert_h, vert_k),) = vert
        top_h = bottom_h = vert_h
        top_k = jnp.where(at_top, 0.0, vert_k)
        bottom_k = jnp.where(at_top, vert_k, 0.0)
    else:
        (top_h, top_k), (bottom_h, bottom_k) = vert

    sum_kh = sum_k = sum_cap = sum_sat = flux_x = flux_y = jnp.zeros((rows, width), F32)
    for layer in range(layers):
        h = p_ref[layer]
        kap = kap_ref[layer]
        lo_k, hi_k, lo_h, hi_h = [side_ref[i, layer : layer + 1, :] for i in range(4)]
        total = jnp.where(is_first, lo_k, jnp.where(is_last, hi_k, 0.0))
        inflow = total * (jnp.where(is_first, lo_h, hi_h) - h)
        if layer == 0:
            inflow, total = inflow + top_k * (top_h - h + 1.0), total + top_k
        if layer == layers - 1:
            inflow, total = inflow + bottom_k * (bottom_h - h - 1.0), total + bottom_k
        balance = kept_ref[0, layer] - kap * inflow
        diagonal = kept_ref[1, layer] + kap * total
        h = h - RELAX * balance / diagonal
        smooth_ref[layer] = h

        pa, pn, pc, psk, pd, pcap = [kept_ref[2 + i, layer] for i in range(6)]
        kap, sat, over = hydraulics(h, pa, pn, pc, psk)
        cond = kap * kap
        flux_x = flux_x + kap * from_below(kap, 0.0) * (pltpu.roll(h, rows - 1, 0) - h)
        flux_y = flux_y + kap * from_right(kap) * (pltpu.roll(h, width - 1, 1) - h)
        for i, value in enumerate((h, kap)):
            edge_ref[2 * i, layer : layer + 1, :] = value[0:1, :]
            edge_ref[2 * i + 1, layer : layer + 1, :] = value[rows - 1 : rows, :]
        sum_kh = sum_kh + cond * h
        sum_k = sum_k + cond
        sum_cap = sum_cap + pcap * sat * over
        sum_sat = sum_sat + pd * sat

    restricted = (
        (flux_x - from_above(flux_x, 0.0)) + (flux_y - from_left(flux_y)) - sum_sat - local_ref[0]
    )
    for at, value in enumerate((sum_kh, sum_k, sum_cap, restricted, local_ref[1])):
        sums_ref[at] = value
    low_h, high_h, low_k, high_k = [edge_ref[i] for i in range(4)]
    to_even_ref[:, 0:width] = jnp.where(even, high_h, low_h)
    to_odd_ref[:, 0:width] = jnp.where(even, low_h, high_h)
    mine_ref[0] = jnp.where(even, high_k, low_k)
    mine_ref[1] = jnp.where(even, low_k, high_k)
    low_tail = jnp.concatenate([restricted[0:1], sum_k[1:2]], axis=1)
    high_tail = jnp.concatenate([restricted[rows - 1 : rows], sum_k[rows - 2 : rows - 1]], axis=1)
    for out_ref, tail in (
        (to_even_ref, jnp.where(even, high_tail, low_tail)),
        (to_odd_ref, jnp.where(even, low_tail, high_tail)),
    ):
        for j, (row, lane) in enumerate(tail_spots(layers, width)):
            out_ref[row : row + 1, lane : lane + LANES] = tail[:, j * LANES : (j + 1) * LANES]


def edge_block(odd, rim_ref, mine_ref, to_ref, from_ref):
    _, layers, width = rim_ref.shape
    pa, pn, pc, psk, pd = [rim_ref[i] for i in range(5)]
    theirs = from_ref[:, 0:width]
    kap, sat, over = hydraulics(theirs, pa, pn, pc, psk)
    cond = kap * kap
    tail = jnp.concatenate(
        [from_ref[row : row + 1, lane : lane + LANES] for row, lane in tail_spots(layers, width)],
        axis=1,
    )

    def total(x):
        return jnp.sum(x, axis=0, keepdims=True)

    flux = total(mine_ref[odd] * kap * (theirs - to_ref[:, 0:width]))
    block = jnp.concatenate(
        [
            total(cond * theirs),
            total(cond),
            total(pd * (pn - 1.0) * sat * over),
            tail[:, 0:width] - flux,
            tail[:, width:],
            total(jnp.exp2(pa)),
            flux,
            jnp.zeros_like(flux),
        ],
        axis=0,
    )
    return jnp.where(paired()[odd], block, 0.0)


def odd_edge_kernel(rim_ref, mine_ref, to_ref, from_ref, block_ref):
    block_ref[...] = edge_block(1, rim_ref, mine_ref, to_ref, from_ref)


def even_edge_kernel(rim_ref, mine_ref, to_ref, from_ref, odd_block_ref, halo_ref):
    halo_ref[0] = edge_block(0, rim_ref, mine_ref, to_ref, from_ref)
    halo_ref[1] = odd_block_ref[...]


def columns_kernel(sums_ref, their_sums_ref, columns_ref):
    kh, kk, cap, rest, rate = [sums_ref[i] + their_sums_ref[i] for i in range(5)]
    for i, value in enumerate((kh / kk, jnp.sqrt(kk), cap, rest, rate)):
        columns_ref[i] = value


def coarse_kernel(
    depth_total, smooth_ref, columns_ref, halo_ref, their_halo_ref, out_ref, head_ref
):
    rows = smooth_ref.shape[1]
    base, root, cap, rest, rate = [columns_ref[i] for i in range(5)]
    by_even = halo_ref[0] + their_halo_ref[0]
    by_odd = halo_ref[1] + their_halo_ref[1]
    even = even_area()
    lo = jnp.where(even, by_odd, by_even)
    hi = jnp.where(even, by_even, by_odd)
    spot = row_iota(rest.shape)
    rest = jnp.where(spot == 0, rest + lo[6:7], rest)
    rest = jnp.where(spot == rows - 1, rest + hi[6:7], rest)

    def pair(i):
        return jnp.where(spot == 0, lo[i : i + 1], jnp.where(spot == rows - 1, hi[i : i + 1], 0.0))

    h_kh, h_k, h_cap, h_rest, o_k, h_rate = [pair(i) for i in range(6)]
    edge_lane = lane_iota(rest.shape)

    def sides(x):
        return from_left(x) + from_right(x)

    h_live = h_k > 0.0
    h_base = jnp.where(h_live, h_kh / jnp.where(h_live, h_k, 1.0), 0.0)
    h_root = jnp.sqrt(h_k)
    o_root = jnp.sqrt(o_k)

    def around(x, halo):
        return from_above(x, halo[0:1]), from_below(x, halo[rows - 1 : rows])

    def flow(head, halo_head, tau, halo_tau):
        tau_u, tau_d = around(tau, halo_tau)
        head_u, head_d = around(head, halo_head)
        tau_l, tau_r = from_left(tau), from_right(tau)
        head_l, head_r = from_left(head), from_right(head)
        inflow = (
            tau_u * (head_u - head)
            + tau_d * (head_d - head)
            + tau_l * (head_l - head)
            + tau_r * (head_r - head)
        )
        return tau * inflow, tau * (tau_u + tau_d + tau_l + tau_r)

    start_in, start_sum = flow(base, h_base, root, h_root)
    rhs = rest - start_in
    first = base + RELAX * rest / (cap + start_sum)
    h_diag = h_cap + h_root * (o_root + root + sides(h_root))
    h_first = h_base + jnp.where(h_live, RELAX * h_rest / jnp.where(h_live, h_diag, 1.0), 0.0)
    half = 0.5 / depth_total
    tau = root * jnp.exp(half * rate * jnp.tanh(first - base))
    h_tau = h_root * jnp.exp(half * h_rate * jnp.tanh(h_first - h_base))
    first_in, first_sum = flow(first, h_first, tau, h_tau)
    first_flow = cap * (first - base) - first_in
    second = first - RELAX * (first_flow - rhs) / (cap + first_sum)
    head_ref[...] = second
    shift = second - base
    out_ref[...] = smooth_ref[...] + shift[None]


def shards(pressure, theta_old, source, soil_type, soil_params):
    layers, rows, width = pressure.shape
    areas = lax.axis_size("area")
    depths = lax.axis_size("depth")
    swap = depths == 2
    both = ("area", "depth")
    even_moves = full_swap([(i, i + 1) for i in range(0, areas - 1, 2)], areas, depths)
    odd_moves = full_swap([(i, i + 1) for i in range(1, areas - 1, 2)], areas, depths)
    down = [(i, i + 1) for i in range(depths - 1)]
    up = [(b, a) for a, b in down]
    swapped = [(0, 1), (1, 0)]

    def shape(*dims):
        return jax.ShapeDtypeStruct(dims, F32)

    params = pltpu.CompilerParams(vmem_limit_bytes=16 << 20)
    verts = 1 if swap else 2
    kind_count = soil_params.shape[1]
    in_hbm = [
        pltpu.with_memory_space_constraint(x, pltpu.HBM)
        for x in (pressure, soil_type, soil_params)
    ]
    packed = pl.pallas_call(
        functools.partial(pack_kernel, swap),
        out_shape=[shape(5, kind_count, 8, LANES), shape(5, 8, LANES)]
        + [shape(2, layers, width)] * 2
        + [shape(2, rows, width)] * verts,
        in_specs=[pl.BlockSpec(memory_space=pltpu.HBM)] * 3,
        out_specs=whole(4 + verts),
        scratch_shapes=[
            pltpu.VMEM((2, layers, width), F32),
            pltpu.VMEM((2, layers, width), jnp.int32),
            pltpu.VMEM((verts, rows, width), F32),
            pltpu.VMEM((verts, rows, width), jnp.int32),
            pltpu.VMEM(soil_params.shape, F32),
            pltpu.SemaphoreType.DMA((5 + 2 * verts,)),
        ],
        compiler_params=params,
        cost_estimate=pl.CostEstimate(flops=PACK_COST, transcendentals=0, bytes_accessed=0),
        name="pack",
    )(*in_hbm)
    from_odd = lax.ppermute(packed[3], both, odd_moves)
    from_even = lax.ppermute(packed[2], both, even_moves)
    if swap:
        vert = [lax.ppermute(packed[4], "depth", swapped)]
    else:
        vert = [lax.ppermute(packed[4], "depth", down), lax.ppermute(packed[5], "depth", up)]
    kept, kap, local_sums = pl.pallas_call(
        local_kernel,
        out_shape=[shape(8, layers, rows, width), shape(layers, rows, width), shape(2, rows, width)],
        in_specs=whole(6),
        out_specs=whole(3),
        compiler_params=params,
        name="local",
    )(pressure, theta_old, source, soil_type, packed[0], packed[1])
    rims = [
        pl.pallas_call(
            functools.partial(rim_kernel, odd),
            out_shape=shape(6, layers, width),
            in_specs=whole(2),
            out_specs=whole(1)[0],
            compiler_params=params,
            name="rim",
        )(from_area, packed[0])
        for odd, from_area in enumerate((from_even, from_odd))
    ]
    sent = shape(layers, sent_width(layers, width))
    smooth, sums, to_even, to_odd, mine = pl.pallas_call(
        functools.partial(fine_kernel, swap),
        out_shape=[
            shape(layers, rows, width),
            shape(5, rows, width),
            sent,
            sent,
            shape(2, layers, width),
        ],
        in_specs=whole(9 + verts),
        out_specs=whole(5),
        scratch_shapes=[pltpu.VMEM((4, layers, width), F32)] * 2,
        compiler_params=params,
        name="fine",
    )(pressure, kept, kap, local_sums, packed[0], from_even, from_odd, *rims, *vert)
    from_odd = lax.ppermute(to_odd, both, odd_moves)
    from_even = lax.ppermute(to_even, both, even_moves)
    if swap:
        their_sums = lax.ppermute(sums, "depth", swapped)
    else:
        sums, their_sums = lax.psum(sums, "depth"), jnp.zeros_like(sums)
    odd_block = pl.pallas_call(
        odd_edge_kernel,
        out_shape=shape(8, width),
        in_specs=whole(4),
        out_specs=whole(1)[0],
        compiler_params=params,
        cost_estimate=pl.CostEstimate(flops=EDGE_COST, transcendentals=0, bytes_accessed=0),
        name="odd_edge",
    )(rims[1], mine, to_odd, from_odd)
    halo = pl.pallas_call(
        even_edge_kernel,
        out_shape=shape(2, 8, width),
        in_specs=whole(5),
        out_specs=whole(1)[0],
        compiler_params=params,
        name="even_edge",
    )(rims[0], mine, to_even, from_even, odd_block)
    if swap:
        their_halo = lax.ppermute(halo, "depth", swapped)
    else:
        halo, their_halo = lax.psum(halo, "depth"), jnp.zeros_like(halo)
    columns = pl.pallas_call(
        columns_kernel,
        out_shape=shape(5, rows, width),
        in_specs=whole(2),
        out_specs=whole(1)[0],
        compiler_params=params,
        name="columns",
    )(sums, their_sums)
    out, head = pl.pallas_call(
        functools.partial(coarse_kernel, layers * depths),
        out_shape=[shape(layers, rows, width), shape(rows, width)],
        in_specs=whole(4),
        out_specs=whole(2),
        compiler_params=params,
        name="coarse",
    )(smooth, columns, halo, their_halo)
    return out, head


def solution(mesh):
    in_specs = (
        P("depth", "area", None),
        P("depth", "area", None),
        P("depth", "area", None),
        P("depth", "area", None),
        P(),
    )
    out_specs = (P("depth", "area", None), P("area", None))
    return jax.shard_map(shards, mesh=mesh, in_specs=in_specs, out_specs=out_specs, check_vma=False)
```

```python
import functools
import math

import jax
import jax.numpy as jnp
from jax import lax
from jax.experimental import pallas as pl
from jax.experimental.pallas import tpu as pltpu
from jax.sharding import PartitionSpec as P

INV_DT = 10.0
RELAX = 0.8
SMALL = 0.04
LOG2E = math.log2(math.e)
LANES = 128
PACK_COST = 4_000_000_000
EDGE_COST = 1000_000_000
F32 = jnp.float32

T_A, T_N, T_SK, T_D, T_R = range(5)
GATHERED = (2, 3, 4,)


def whole(count):
    return [pl.BlockSpec(memory_space=pltpu.VMEM)] * count


def build_table(params_ref):
    alpha = params_ref[2:3, :]
    return {
        T_A: jnp.log(alpha) * LOG2E,
        T_N: params_ref[3:4, :],
        T_SK: jnp.sqrt(params_ref[4:5, :]),
        T_D: (params_ref[1:2, :] - params_ref[0:1, :]) * INV_DT,
        T_R: params_ref[0:1, :] * INV_DT,
    }


def gather(table, kinds):
    return jnp.concatenate(
        [
            jnp.take_along_axis(
                table, kinds[:, c : c + LANES], axis=1, mode="promise_in_bounds"
            )
            for c in range(0, kinds.shape[1], LANES)
        ],
        axis=1,
    )


def spread_table(table, tab_ref, rows_ref):
    for row_id, row in table.items():
        rows_ref[row_id, :, 0 : row.shape[1]] = jnp.broadcast_to(row, (8, row.shape[1]))
        for kind in range(row.shape[1]):
            tab_ref[row_id, kind] = jnp.broadcast_to(row[:, kind : kind + 1], (8, LANES))


def pick(tab_ref, row_id, bits, width):
    level = [
        jnp.tile(tab_ref[row_id, kind], (bits[0].shape[0] // 8, width // LANES))
        for kind in range(tab_ref.shape[1])
    ]
    for bit in bits:
        pairs = [
            jnp.where(bit, level[i + 1], level[i]) for i in range(0, len(level) - 1, 2)
        ]
        level = pairs + ([level[-1]] if len(level) % 2 else [])
    return level[0]


def type_bits(kinds, count):
    return [(kinds & (1 << i)) != 0 for i in range((count - 1).bit_length())]


def power(pn):
    return (1.0 / pn - 1.0) * (0.25 * LOG2E)


def hydraulics(h, pa, pn, pc, psk):
    q = h * h + SMALL
    u = jnp.exp2(pn * (pa + (0.5 * LOG2E) * jnp.log(q)))
    one_plus = 1.0 + u
    inv = 1.0 / one_plus
    ratio = u * inv
    quarter = jnp.exp2(pc * jnp.log(one_plus))
    w = jnp.exp2((-4.0 * pc) * jnp.log(ratio))
    kappa = psk * quarter * (1.0 - w)
    half = quarter * quarter
    return kappa, half * half, ratio * lax.rsqrt(q)


def code(kinds):
    return (kinds + 1).astype(F32)


def code_params(codes, tab_ref):
    kinds = jnp.maximum(codes.astype(jnp.int32) - 1, 0)
    bits = type_bits(kinds, tab_ref.shape[1])
    pa, pn, psk, pd = [pick(tab_ref, i, bits, codes.shape[1]) for i in (T_A, T_N, T_SK, T_D)]
    return pa, pn, power(pn), jnp.where(codes > 0.5, psk, 0.0), pd


def even_area():
    return lax.rem(lax.axis_index("area"), 2) == 0


def paired():
    area, last = lax.axis_index("area"), lax.axis_size("area") - 1
    is_even = even_area()
    return (
        jnp.logical_or(jnp.logical_not(is_even), area < last),
        jnp.where(is_even, area, last - area) > 0,
    )


def full_swap(pairs, areas, depths):
    target = {a: b for a, b in pairs}
    target.update({b: a for a, b in pairs})
    moves = []
    for a in range(areas):
        for d in range(depths):
            other = d if a in target else d ^ 1
            if other < depths:
                moves.append((a * depths + d, target.get(a, a) * depths + other))
    return moves


def pack_kernel(swap, p_ref, soil_ref, params_ref, tab_ref, rows_ref, even_ref, odd_ref, *rest):
    layers, rows, _ = p_ref.shape
    count = 1 if swap else 2
    vert_refs = rest[:count]
    p_buf, soil_buf, vert_p, vert_soil, params_buf, sems = rest[count:]
    even = even_area()
    if swap:
        spots = [jnp.where(lax.axis_index("depth") == 0, layers - 1, 0)]
    else:
        spots = [layers - 1, 0]
    copies = [(params_ref, params_buf)]
    for side, row in enumerate((0, rows - 1)):
        copies.append((p_ref.at[:, row, :], p_buf.at[side]))
        copies.append((soil_ref.at[:, row, :], soil_buf.at[side]))
    for side, spot in enumerate(spots):
        copies.append((p_ref.at[spot], vert_p.at[side]))
        copies.append((soil_ref.at[spot], vert_soil.at[side]))
    copies = [
        pltpu.make_async_copy(source, target, sems.at[i])
        for i, (source, target) in enumerate(copies)
    ]
    for copy in copies:
        copy.start()
    copies[0].wait()
    spread_table(build_table(params_buf), tab_ref, rows_ref)
    for copy in copies[1:]:
        copy.wait()
    for i, low, high in ((0, p_buf[0], p_buf[1]), (1, code(soil_buf[0]), code(soil_buf[1]))):
        even_ref[i] = jnp.where(even, high, low)
        odd_ref[i] = jnp.where(even, low, high)
    for side, out_ref in enumerate(vert_refs):
        out_ref[0] = vert_p[side]
        out_ref[1] = code(vert_soil[side])


def row_iota(shape):
    return lax.broadcasted_iota(jnp.int32, shape, 0)


def lane_iota(shape):
    return lax.broadcasted_iota(jnp.int32, shape, 1)


def from_above(x, edge):
    return jnp.where(row_iota(x.shape) == 0, edge, pltpu.roll(x, 1, 0))


def from_below(x, edge):
    last = x.shape[0] - 1
    return jnp.where(row_iota(x.shape) == last, edge, pltpu.roll(x, last, 0))


def from_left(x):
    return jnp.where(lane_iota(x.shape) == 0, 0.0, pltpu.roll(x, 1, 1))


def from_right(x):
    last = x.shape[1] - 1
    return jnp.where(lane_iota(x.shape) == last, 0.0, pltpu.roll(x, last, 1))


def local_kernel(
    p_ref, theta_ref, source_ref, soil_ref, tab_ref, rows_ref, kept_ref, kap_ref, sums_ref
):
    layers, rows, width = p_ref.shape
    kind_count = tab_ref.shape[1]

    sum_fixed = sum_rate = jnp.zeros((rows, width), F32)
    held = None
    for layer in range(layers):
        bits = type_bits(soil_ref[layer], kind_count)
        pa, pn, psk, pd, pr = [
            gather(rows_ref[i], soil_ref[layer]) if i in GATHERED else pick(tab_ref, i, bits, width)
            for i in range(5)
        ]
        pc, pcap = power(pn), pd * (pn - 1.0)
        h = p_ref[layer]
        kap, sat, over = hydraulics(h, pa, pn, pc, psk)
        fixed = pr - INV_DT * theta_ref[layer] - source_ref[layer]
        k_l, k_r = from_left(kap), from_right(kap)
        k_u, k_d = from_above(kap, 0.0), from_below(kap, 0.0)
        inflow = (
            k_l * (pltpu.roll(h, 1, 1) - h)
            + k_r * (pltpu.roll(h, width - 1, 1) - h)
            + k_u * (pltpu.roll(h, 1, 0) - h)
            + k_d * (pltpu.roll(h, rows - 1, 0) - h)
        )
        total = (k_l + k_r) + (k_u + k_d)
        kap_ref[layer] = kap
        for i, field in enumerate((pa, pn, pc, psk, pd, pcap)):
            kept_ref[2 + i, layer] = field
        sum_fixed, sum_rate = sum_fixed + fixed, sum_rate + jnp.exp2(pa)
        if held is not None:
            o_h, o_kap, o_inflow, o_total, o_fixed, o_cap = held
            inflow = inflow + o_kap * (o_h - h + 1.0)
            total = total + o_kap
            o_inflow = o_inflow + kap * (h - o_h - 1.0)
            kept_ref[0, layer - 1] = o_fixed - o_kap * o_inflow
            kept_ref[1, layer - 1] = o_cap + o_kap * (o_total + kap)
        held = (h, kap, inflow, total, pd * sat + fixed, pcap * sat * over)
    _, kap, inflow, total, fixed, cap = held
    kept_ref[0, layers - 1] = fixed - kap * inflow
    kept_ref[1, layers - 1] = cap + kap * total
    sums_ref[0] = sum_fixed
    sums_ref[1] = sum_rate


def rim_kernel(odd, from_ref, tab_ref, rim_ref):
    live = paired()[odd]

    def step(i, carry):
        at = pl.ds(i * 8, 8)
        fields = code_params(jnp.where(live, from_ref[1, at, :], 0.0), tab_ref)
        for spot, field in enumerate(fields):
            rim_ref[spot, at, :] = field
        rim_ref[5, at, :] = hydraulics(from_ref[0, at, :], *fields[:4])[0]
        return carry

    lax.fori_loop(0, from_ref.shape[1] // 8, step, 0, unroll=True)


def tail_spots(layers, width):
    chunks = 2 * width // LANES
    return [(j % layers, width + j // layers * LANES) for j in range(chunks)]


def sent_width(layers, width):
    return width + pl.cdiv(2 * width // LANES, layers) * LANES


def fine_kernel(
    swap,
    p_ref,
    kept_ref,
    kap_ref,
    local_ref,
    tab_ref,
    from_even_ref,
    from_odd_ref,
    rim_even_ref,
    rim_odd_ref,
    *rest,
):
    layers, rows, width = p_ref.shape
    verts = 1 if swap else 2
    vert_refs = rest[:verts]
    smooth_ref, sums_ref, to_even_ref, to_odd_ref, mine_ref, side_ref, edge_ref = rest[verts:]
    even = even_area()
    spot = row_iota((rows, width))
    is_first, is_last = spot == 0, spot == rows - 1

    for i, by_even, by_odd in (
        (0, rim_even_ref[5], rim_odd_ref[5]),
        (2, from_even_ref[0], from_odd_ref[0]),
    ):
        side_ref[i] = jnp.where(even, by_odd, by_even)
        side_ref[i + 1] = jnp.where(even, by_even, by_odd)
    vert = [(ref[0], hydraulics(ref[0], *code_params(ref[1], tab_ref)[:4])[0]) for ref in vert_refs]
    if swap:
        at_top = lax.axis_index("depth") == 0
        ((vert_h, vert_k),) = vert
        top_h = bottom_h = vert_h
        top_k = jnp.where(at_top, 0.0, vert_k)
        bottom_k = jnp.where(at_top, vert_k, 0.0)
    else:
        (top_h, top_k), (bottom_h, bottom_k) = vert

    sum_kh = sum_k = sum_cap = sum_sat = flux_x = flux_y = jnp.zeros((rows, width), F32)
    for layer in range(layers):
        h = p_ref[layer]
        kap = kap_ref[layer]
        lo_k, hi_k, lo_h, hi_h = [side_ref[i, layer : layer + 1, :] for i in range(4)]
        total = jnp.where(is_first, lo_k, jnp.where(is_last, hi_k, 0.0))
        inflow = total * (jnp.where(is_first, lo_h, hi_h) - h)
        if layer == 0:
            inflow, total = inflow + top_k * (top_h - h + 1.0), total + top_k
        if layer == layers - 1:
            inflow, total = inflow + bottom_k * (bottom_h - h - 1.0), total + bottom_k
        balance = kept_ref[0, layer] - kap * inflow
        diagonal = kept_ref[1, layer] + kap * total
        h = h - RELAX * balance / diagonal
        smooth_ref[layer] = h

        pa, pn, pc, psk, pd, pcap = [kept_ref[2 + i, layer] for i in range(6)]
        kap, sat, over = hydraulics(h, pa, pn, pc, psk)
        cond = kap * kap
        flux_x = flux_x + kap * from_below(kap, 0.0) * (pltpu.roll(h, rows - 1, 0) - h)
        flux_y = flux_y + kap * from_right(kap) * (pltpu.roll(h, width - 1, 1) - h)
        for i, value in enumerate((h, kap)):
            edge_ref[2 * i, layer : layer + 1, :] = value[0:1, :]
            edge_ref[2 * i + 1, layer : layer + 1, :] = value[rows - 1 : rows, :]
        sum_kh = sum_kh + cond * h
        sum_k = sum_k + cond
        sum_cap = sum_cap + pcap * sat * over
        sum_sat = sum_sat + pd * sat

    restricted = (
        (flux_x - from_above(flux_x, 0.0)) + (flux_y - from_left(flux_y)) - sum_sat - local_ref[0]
    )
    for at, value in enumerate((sum_kh, sum_k, sum_cap, restricted, local_ref[1])):
        sums_ref[at] = value
    low_h, high_h, low_k, high_k = [edge_ref[i] for i in range(4)]
    to_even_ref[:, 0:width] = jnp.where(even, high_h, low_h)
    to_odd_ref[:, 0:width] = jnp.where(even, low_h, high_h)
    mine_ref[0] = jnp.where(even, high_k, low_k)
    mine_ref[1] = jnp.where(even, low_k, high_k)
    low_tail = jnp.concatenate([restricted[0:1], sum_k[1:2]], axis=1)
    high_tail = jnp.concatenate([restricted[rows - 1 : rows], sum_k[rows - 2 : rows - 1]], axis=1)
    for out_ref, tail in (
        (to_even_ref, jnp.where(even, high_tail, low_tail)),
        (to_odd_ref, jnp.where(even, low_tail, high_tail)),
    ):
        for j, (row, lane) in enumerate(tail_spots(layers, width)):
            out_ref[row : row + 1, lane : lane + LANES] = tail[:, j * LANES : (j + 1) * LANES]


def edge_block(odd, rim_ref, mine_ref, to_ref, from_ref):
    _, layers, width = rim_ref.shape
    pa, pn, pc, psk, pd = [rim_ref[i] for i in range(5)]
    theirs = from_ref[:, 0:width]
    kap, sat, over = hydraulics(theirs, pa, pn, pc, psk)
    cond = kap * kap
    tail = jnp.concatenate(
        [from_ref[row : row + 1, lane : lane + LANES] for row, lane in tail_spots(layers, width)],
        axis=1,
    )

    def total(x):
        return jnp.sum(x, axis=0, keepdims=True)

    flux = total(mine_ref[odd] * kap * (theirs - to_ref[:, 0:width]))
    block = jnp.concatenate(
        [
            total(cond * theirs),
            total(cond),
            total(pd * (pn - 1.0) * sat * over),
            tail[:, 0:width] - flux,
            tail[:, width:],
            total(jnp.exp2(pa)),
            flux,
            jnp.zeros_like(flux),
        ],
        axis=0,
    )
    return jnp.where(paired()[odd], block, 0.0)


def odd_edge_kernel(rim_ref, mine_ref, to_ref, from_ref, block_ref):
    block_ref[...] = edge_block(1, rim_ref, mine_ref, to_ref, from_ref)


def fold_spots(row, width):
    chunks = width // LANES
    return [((row * chunks + c) % 8, width + (row * chunks + c) // 8 * LANES) for c in range(chunks)]


def even_edge_kernel(rim_ref, mine_ref, to_ref, from_ref, odd_block_ref, halo_ref, block_ref):
    width = block_ref.shape[1]
    block_ref[...] = edge_block(0, rim_ref, mine_ref, to_ref, from_ref)
    for side, source in enumerate((block_ref, odd_block_ref)):
        halo_ref[4 * side : 4 * side + 4, 0:width] = source[0:4, :]
        for row in range(3):
            for c, (at, lane) in enumerate(fold_spots(3 * side + row, width)):
                halo_ref[at : at + 1, lane : lane + LANES] = source[
                    4 + row : 5 + row, c * LANES : (c + 1) * LANES
                ]


def columns_kernel(sums_ref, their_sums_ref, columns_ref):
    kh, kk, cap, rest, rate = [sums_ref[i] + their_sums_ref[i] for i in range(5)]
    for i, value in enumerate((kh / kk, jnp.sqrt(kk), cap, rest, rate)):
        columns_ref[i] = value


def coarse_kernel(
    depth_total, smooth_ref, columns_ref, halo_ref, their_halo_ref, out_ref, head_ref
):
    rows = smooth_ref.shape[1]
    base, root, cap, rest, rate = [columns_ref[i] for i in range(5)]
    width = columns_ref.shape[2]
    head = halo_ref[:, 0:width] + their_halo_ref[:, 0:width]
    sides = []
    for side in range(2):
        rows_of = [head[i : i + 1] for i in range(4 * side, 4 * side + 4)]
        for row in range(3 * side, 3 * side + 3):
            rows_of.append(
                jnp.concatenate(
                    [
                        halo_ref[at : at + 1, lane : lane + LANES]
                        + their_halo_ref[at : at + 1, lane : lane + LANES]
                        for at, lane in fold_spots(row, width)
                    ],
                    axis=1,
                )
            )
        sides.append(rows_of)
    even = even_area()
    lo = [jnp.where(even, b, a) for a, b in zip(*sides)]
    hi = [jnp.where(even, a, b) for a, b in zip(*sides)]
    spot = row_iota(rest.shape)
    rest = jnp.where(spot == 0, rest + lo[6], rest)
    rest = jnp.where(spot == rows - 1, rest + hi[6], rest)

    def pair(i):
        return jnp.where(spot == 0, lo[i], jnp.where(spot == rows - 1, hi[i], 0.0))

    h_kh, h_k, h_cap, h_rest, o_k, h_rate = [pair(i) for i in range(6)]
    edge_lane = lane_iota(rest.shape)

    def lateral(x):
        return from_left(x) + from_right(x)

    h_live = h_k > 0.0
    h_base = jnp.where(h_live, h_kh / jnp.where(h_live, h_k, 1.0), 0.0)
    h_root = jnp.sqrt(h_k)
    o_root = jnp.sqrt(o_k)

    def around(x, halo):
        return from_above(x, halo[0:1]), from_below(x, halo[rows - 1 : rows])

    def flow(head, halo_head, tau, halo_tau):
        tau_u, tau_d = around(tau, halo_tau)
        head_u, head_d = around(head, halo_head)
        tau_l, tau_r = from_left(tau), from_right(tau)
        head_l, head_r = from_left(head), from_right(head)
        inflow = (
            tau_u * (head_u - head)
            + tau_d * (head_d - head)
            + tau_l * (head_l - head)
            + tau_r * (head_r - head)
        )
        return tau * inflow, tau * (tau_u + tau_d + tau_l + tau_r)

    start_in, start_sum = flow(base, h_base, root, h_root)
    rhs = rest - start_in
    first = base + RELAX * rest / (cap + start_sum)
    h_diag = h_cap + h_root * (o_root + root + lateral(h_root))
    h_first = h_base + jnp.where(h_live, RELAX * h_rest / jnp.where(h_live, h_diag, 1.0), 0.0)
    half = 0.5 / depth_total
    tau = root * jnp.exp(half * rate * jnp.tanh(first - base))
    h_tau = h_root * jnp.exp(half * h_rate * jnp.tanh(h_first - h_base))
    first_in, first_sum = flow(first, h_first, tau, h_tau)
    first_flow = cap * (first - base) - first_in
    second = first - RELAX * (first_flow - rhs) / (cap + first_sum)
    head_ref[...] = second
    shift = second - base
    out_ref[...] = smooth_ref[...] + shift[None]


def shards(pressure, theta_old, source, soil_type, soil_params):
    layers, rows, width = pressure.shape
    areas = lax.axis_size("area")
    depths = lax.axis_size("depth")
    swap = depths == 2
    both = ("area", "depth")
    even_moves = full_swap([(i, i + 1) for i in range(0, areas - 1, 2)], areas, depths)
    odd_moves = full_swap([(i, i + 1) for i in range(1, areas - 1, 2)], areas, depths)
    down = [(i, i + 1) for i in range(depths - 1)]
    up = [(b, a) for a, b in down]
    swapped = [(0, 1), (1, 0)]

    def shape(*dims):
        return jax.ShapeDtypeStruct(dims, F32)

    params = pltpu.CompilerParams(vmem_limit_bytes=16 << 20)
    verts = 1 if swap else 2
    kind_count = soil_params.shape[1]
    in_hbm = [
        pltpu.with_memory_space_constraint(x, pltpu.HBM)
        for x in (pressure, soil_type, soil_params)
    ]
    packed = pl.pallas_call(
        functools.partial(pack_kernel, swap),
        out_shape=[shape(5, kind_count, 8, LANES), shape(5, 8, LANES)]
        + [shape(2, layers, width)] * 2
        + [shape(2, rows, width)] * verts,
        in_specs=[pl.BlockSpec(memory_space=pltpu.HBM)] * 3,
        out_specs=whole(4 + verts),
        scratch_shapes=[
            pltpu.VMEM((2, layers, width), F32),
            pltpu.VMEM((2, layers, width), jnp.int32),
            pltpu.VMEM((verts, rows, width), F32),
            pltpu.VMEM((verts, rows, width), jnp.int32),
            pltpu.VMEM(soil_params.shape, F32),
            pltpu.SemaphoreType.DMA((5 + 2 * verts,)),
        ],
        compiler_params=params,
        cost_estimate=pl.CostEstimate(flops=PACK_COST, transcendentals=0, bytes_accessed=0),
        name="pack",
    )(*in_hbm)
    from_odd = lax.ppermute(packed[3], both, odd_moves)
    from_even = lax.ppermute(packed[2], both, even_moves)
    if swap:
        vert = [lax.ppermute(packed[4], "depth", swapped)]
    else:
        vert = [lax.ppermute(packed[4], "depth", down), lax.ppermute(packed[5], "depth", up)]
    kept, kap, local_sums = pl.pallas_call(
        local_kernel,
        out_shape=[shape(8, layers, rows, width), shape(layers, rows, width), shape(2, rows, width)],
        in_specs=whole(6),
        out_specs=whole(3),
        compiler_params=params,
        name="local",
    )(pressure, theta_old, source, soil_type, packed[0], packed[1])
    rims = [
        pl.pallas_call(
            functools.partial(rim_kernel, odd),
            out_shape=shape(6, layers, width),
            in_specs=whole(2),
            out_specs=whole(1)[0],
            compiler_params=params,
            name="rim",
        )(from_area, packed[0])
        for odd, from_area in enumerate((from_even, from_odd))
    ]
    sent = shape(layers, sent_width(layers, width))
    smooth, sums, to_even, to_odd, mine = pl.pallas_call(
        functools.partial(fine_kernel, swap),
        out_shape=[
            shape(layers, rows, width),
            shape(5, rows, width),
            sent,
            sent,
            shape(2, layers, width),
        ],
        in_specs=whole(9 + verts),
        out_specs=whole(5),
        scratch_shapes=[pltpu.VMEM((4, layers, width), F32)] * 2,
        compiler_params=params,
        name="fine",
    )(pressure, kept, kap, local_sums, packed[0], from_even, from_odd, *rims, *vert)
    from_odd = lax.ppermute(to_odd, both, odd_moves)
    from_even = lax.ppermute(to_even, both, even_moves)
    if swap:
        their_sums = lax.ppermute(sums, "depth", swapped)
    else:
        sums, their_sums = lax.psum(sums, "depth"), jnp.zeros_like(sums)
    odd_block = pl.pallas_call(
        odd_edge_kernel,
        out_shape=shape(8, width),
        in_specs=whole(4),
        out_specs=whole(1)[0],
        compiler_params=params,
        cost_estimate=pl.CostEstimate(flops=EDGE_COST, transcendentals=0, bytes_accessed=0),
        name="odd_edge",
    )(rims[1], mine, to_odd, from_odd)
    halo = pl.pallas_call(
        even_edge_kernel,
        out_shape=shape(8, width + pl.cdiv(6 * width // LANES, 8) * LANES),
        in_specs=whole(5),
        out_specs=whole(1)[0],
        scratch_shapes=[pltpu.VMEM((8, width), F32)],
        compiler_params=params,
        name="even_edge",
    )(rims[0], mine, to_even, from_even, odd_block)
    if swap:
        their_halo = lax.ppermute(halo, "depth", swapped)
    else:
        halo, their_halo = lax.psum(halo, "depth"), jnp.zeros_like(halo)
    columns = pl.pallas_call(
        columns_kernel,
        out_shape=shape(5, rows, width),
        in_specs=whole(2),
        out_specs=whole(1)[0],
        compiler_params=params,
        name="columns",
    )(sums, their_sums)
    out, head = pl.pallas_call(
        functools.partial(coarse_kernel, layers * depths),
        out_shape=[shape(layers, rows, width), shape(rows, width)],
        in_specs=whole(4),
        out_specs=whole(2),
        compiler_params=params,
        name="coarse",
    )(smooth, columns, halo, their_halo)
    return out, head


def solution(mesh):
    in_specs = (
        P("depth", "area", None),
        P("depth", "area", None),
        P("depth", "area", None),
        P("depth", "area", None),
        P(),
    )
    out_specs = (P("depth", "area", None), P("area", None))
    return jax.shard_map(shards, mesh=mesh, in_specs=in_specs, out_specs=out_specs, check_vma=False)
```

```python
import functools
import math

import jax
import jax.numpy as jnp
from jax import lax
from jax.experimental import pallas as pl
from jax.experimental.pallas import tpu as pltpu
from jax.sharding import PartitionSpec as P

INV_DT = 10.0
RELAX = 0.8
SMALL = 0.04
LOG2E = math.log2(math.e)
LANES = 128
PACK_COST = 4_000_000_000
EDGE_COST = 1000_000_000
F32 = jnp.float32

T_A, T_N, T_SK, T_D, T_R = range(5)
GATHERED = (2, 3, 4,)


def whole(count):
    return [pl.BlockSpec(memory_space=pltpu.VMEM)] * count


def build_table(params_ref):
    alpha = params_ref[2:3, :]
    return {
        T_A: jnp.log(alpha) * LOG2E,
        T_N: params_ref[3:4, :],
        T_SK: jnp.sqrt(params_ref[4:5, :]),
        T_D: (params_ref[1:2, :] - params_ref[0:1, :]) * INV_DT,
        T_R: params_ref[0:1, :] * INV_DT,
    }


def gather(table, kinds):
    return jnp.concatenate(
        [
            jnp.take_along_axis(
                table, kinds[:, c : c + LANES], axis=1, mode="promise_in_bounds"
            )
            for c in range(0, kinds.shape[1], LANES)
        ],
        axis=1,
    )


def spread_table(table, tab_ref, rows_ref):
    for row_id, row in table.items():
        rows_ref[row_id, :, 0 : row.shape[1]] = jnp.broadcast_to(row, (8, row.shape[1]))
        for kind in range(row.shape[1]):
            tab_ref[row_id, kind] = jnp.broadcast_to(row[:, kind : kind + 1], (8, LANES))


def pick(tab_ref, row_id, bits, width):
    level = [
        jnp.tile(tab_ref[row_id, kind], (bits[0].shape[0] // 8, width // LANES))
        for kind in range(tab_ref.shape[1])
    ]
    for bit in bits:
        pairs = [
            jnp.where(bit, level[i + 1], level[i]) for i in range(0, len(level) - 1, 2)
        ]
        level = pairs + ([level[-1]] if len(level) % 2 else [])
    return level[0]


def type_bits(kinds, count):
    return [(kinds & (1 << i)) != 0 for i in range((count - 1).bit_length())]


def power(pn):
    return (1.0 / pn - 1.0) * (0.25 * LOG2E)


def hydraulics(h, pa, pn, pc, psk):
    q = h * h + SMALL
    u = jnp.exp2(pn * (pa + (0.5 * LOG2E) * jnp.log(q)))
    one_plus = 1.0 + u
    inv = 1.0 / one_plus
    ratio = u * inv
    quarter = jnp.exp2(pc * jnp.log(one_plus))
    w = jnp.exp2((-4.0 * pc) * jnp.log(ratio))
    kappa = psk * quarter * (1.0 - w)
    half = quarter * quarter
    return kappa, half * half, ratio * lax.rsqrt(q)


def code(kinds):
    return (kinds + 1).astype(F32)


def code_params(codes, tab_ref):
    kinds = jnp.maximum(codes.astype(jnp.int32) - 1, 0)
    bits = type_bits(kinds, tab_ref.shape[1])
    pa, pn, psk, pd = [pick(tab_ref, i, bits, codes.shape[1]) for i in (T_A, T_N, T_SK, T_D)]
    return pa, pn, power(pn), jnp.where(codes > 0.5, psk, 0.0), pd


def even_area():
    return lax.rem(lax.axis_index("area"), 2) == 0


def paired():
    area, last = lax.axis_index("area"), lax.axis_size("area") - 1
    is_even = even_area()
    return (
        jnp.logical_or(jnp.logical_not(is_even), area < last),
        jnp.where(is_even, area, last - area) > 0,
    )


def full_swap(pairs, areas, depths):
    target = {a: b for a, b in pairs}
    target.update({b: a for a, b in pairs})
    moves = []
    for a in range(areas):
        for d in range(depths):
            other = d if a in target else d ^ 1
            if other < depths:
                moves.append((a * depths + d, target.get(a, a) * depths + other))
    return moves


def table_kernel(params_ref, tab_ref, rows_ref):
    spread_table(build_table(params_ref), tab_ref, rows_ref)


def pack_kernel(swap, p_ref, soil_ref, even_ref, odd_ref, *rest):
    layers, rows, _ = p_ref.shape
    count = 1 if swap else 2
    vert_refs = rest[:count]
    p_buf, soil_buf, vert_p, vert_soil, sems = rest[count:]
    even = even_area()
    if swap:
        spots = [jnp.where(lax.axis_index("depth") == 0, layers - 1, 0)]
    else:
        spots = [layers - 1, 0]
    copies = []
    for side, row in enumerate((0, rows - 1)):
        copies.append((p_ref.at[:, row, :], p_buf.at[side]))
        copies.append((soil_ref.at[:, row, :], soil_buf.at[side]))
    for side, spot in enumerate(spots):
        copies.append((p_ref.at[spot], vert_p.at[side]))
        copies.append((soil_ref.at[spot], vert_soil.at[side]))
    copies = [
        pltpu.make_async_copy(source, target, sems.at[i])
        for i, (source, target) in enumerate(copies)
    ]
    for copy in copies:
        copy.start()
    for copy in copies:
        copy.wait()
    for i, low, high in ((0, p_buf[0], p_buf[1]), (1, code(soil_buf[0]), code(soil_buf[1]))):
        even_ref[i] = jnp.where(even, high, low)
        odd_ref[i] = jnp.where(even, low, high)
    for side, out_ref in enumerate(vert_refs):
        out_ref[0] = vert_p[side]
        out_ref[1] = code(vert_soil[side])


def row_iota(shape):
    return lax.broadcasted_iota(jnp.int32, shape, 0)


def lane_iota(shape):
    return lax.broadcasted_iota(jnp.int32, shape, 1)


def from_above(x, edge):
    return jnp.where(row_iota(x.shape) == 0, edge, pltpu.roll(x, 1, 0))


def from_below(x, edge):
    last = x.shape[0] - 1
    return jnp.where(row_iota(x.shape) == last, edge, pltpu.roll(x, last, 0))


def from_left(x):
    return jnp.where(lane_iota(x.shape) == 0, 0.0, pltpu.roll(x, 1, 1))


def from_right(x):
    last = x.shape[1] - 1
    return jnp.where(lane_iota(x.shape) == last, 0.0, pltpu.roll(x, last, 1))


def local_kernel(
    p_ref, theta_ref, source_ref, soil_ref, tab_ref, rows_ref, kept_ref, kap_ref, sums_ref
):
    layers, rows, width = p_ref.shape
    kind_count = tab_ref.shape[1]

    sum_fixed = sum_rate = jnp.zeros((rows, width), F32)
    held = None
    for layer in range(layers):
        bits = type_bits(soil_ref[layer], kind_count)
        pa, pn, psk, pd, pr = [
            gather(rows_ref[i], soil_ref[layer]) if i in GATHERED else pick(tab_ref, i, bits, width)
            for i in range(5)
        ]
        pc, pcap = power(pn), pd * (pn - 1.0)
        h = p_ref[layer]
        kap, sat, over = hydraulics(h, pa, pn, pc, psk)
        fixed = pr - INV_DT * theta_ref[layer] - source_ref[layer]
        k_l, k_r = from_left(kap), from_right(kap)
        k_u, k_d = from_above(kap, 0.0), from_below(kap, 0.0)
        inflow = (
            k_l * (pltpu.roll(h, 1, 1) - h)
            + k_r * (pltpu.roll(h, width - 1, 1) - h)
            + k_u * (pltpu.roll(h, 1, 0) - h)
            + k_d * (pltpu.roll(h, rows - 1, 0) - h)
        )
        total = (k_l + k_r) + (k_u + k_d)
        kap_ref[layer] = kap
        for i, field in enumerate((pa, pn, pc, psk, pd, pcap)):
            kept_ref[2 + i, layer] = field
        sum_fixed, sum_rate = sum_fixed + fixed, sum_rate + jnp.exp2(pa)
        if held is not None:
            o_h, o_kap, o_inflow, o_total, o_fixed, o_cap = held
            inflow = inflow + o_kap * (o_h - h + 1.0)
            total = total + o_kap
            o_inflow = o_inflow + kap * (h - o_h - 1.0)
            kept_ref[0, layer - 1] = o_fixed - o_kap * o_inflow
            kept_ref[1, layer - 1] = o_cap + o_kap * (o_total + kap)
        held = (h, kap, inflow, total, pd * sat + fixed, pcap * sat * over)
    _, kap, inflow, total, fixed, cap = held
    kept_ref[0, layers - 1] = fixed - kap * inflow
    kept_ref[1, layers - 1] = cap + kap * total
    sums_ref[0] = sum_fixed
    sums_ref[1] = sum_rate


def rim_kernel(odd, from_ref, tab_ref, rim_ref):
    live = paired()[odd]

    def step(i, carry):
        at = pl.ds(i * 8, 8)
        fields = code_params(jnp.where(live, from_ref[1, at, :], 0.0), tab_ref)
        for spot, field in enumerate(fields):
            rim_ref[spot, at, :] = field
        rim_ref[5, at, :] = hydraulics(from_ref[0, at, :], *fields[:4])[0]
        return carry

    lax.fori_loop(0, from_ref.shape[1] // 8, step, 0, unroll=True)


def tail_spots(layers, width):
    chunks = 2 * width // LANES
    return [(j % layers, width + j // layers * LANES) for j in range(chunks)]


def sent_width(layers, width):
    return width + pl.cdiv(2 * width // LANES, layers) * LANES


def fine_kernel(
    swap,
    p_ref,
    kept_ref,
    kap_ref,
    local_ref,
    tab_ref,
    from_even_ref,
    from_odd_ref,
    rim_even_ref,
    rim_odd_ref,
    *rest,
):
    layers, rows, width = p_ref.shape
    verts = 1 if swap else 2
    vert_refs = rest[:verts]
    smooth_ref, sums_ref, to_even_ref, to_odd_ref, mine_ref, side_ref, edge_ref = rest[verts:]
    even = even_area()
    spot = row_iota((rows, width))
    is_first, is_last = spot == 0, spot == rows - 1

    for i, by_even, by_odd in (
        (0, rim_even_ref[5], rim_odd_ref[5]),
        (2, from_even_ref[0], from_odd_ref[0]),
    ):
        side_ref[i] = jnp.where(even, by_odd, by_even)
        side_ref[i + 1] = jnp.where(even, by_even, by_odd)
    vert = [(ref[0], hydraulics(ref[0], *code_params(ref[1], tab_ref)[:4])[0]) for ref in vert_refs]
    if swap:
        at_top = lax.axis_index("depth") == 0
        ((vert_h, vert_k),) = vert
        top_h = bottom_h = vert_h
        top_k = jnp.where(at_top, 0.0, vert_k)
        bottom_k = jnp.where(at_top, vert_k, 0.0)
    else:
        (top_h, top_k), (bottom_h, bottom_k) = vert

    sum_kh = sum_k = sum_cap = sum_sat = flux_x = flux_y = jnp.zeros((rows, width), F32)
    for layer in range(layers):
        h = p_ref[layer]
        kap = kap_ref[layer]
        lo_k, hi_k, lo_h, hi_h = [side_ref[i, layer : layer + 1, :] for i in range(4)]
        total = jnp.where(is_first, lo_k, jnp.where(is_last, hi_k, 0.0))
        inflow = total * (jnp.where(is_first, lo_h, hi_h) - h)
        if layer == 0:
            inflow, total = inflow + top_k * (top_h - h + 1.0), total + top_k
        if layer == layers - 1:
            inflow, total = inflow + bottom_k * (bottom_h - h - 1.0), total + bottom_k
        balance = kept_ref[0, layer] - kap * inflow
        diagonal = kept_ref[1, layer] + kap * total
        h = h - RELAX * balance / diagonal
        smooth_ref[layer] = h

        pa, pn, pc, psk, pd, pcap = [kept_ref[2 + i, layer] for i in range(6)]
        kap, sat, over = hydraulics(h, pa, pn, pc, psk)
        cond = kap * kap
        flux_x = flux_x + kap * from_below(kap, 0.0) * (pltpu.roll(h, rows - 1, 0) - h)
        flux_y = flux_y + kap * from_right(kap) * (pltpu.roll(h, width - 1, 1) - h)
        for i, value in enumerate((h, kap)):
            edge_ref[2 * i, layer : layer + 1, :] = value[0:1, :]
            edge_ref[2 * i + 1, layer : layer + 1, :] = value[rows - 1 : rows, :]
        sum_kh = sum_kh + cond * h
        sum_k = sum_k + cond
        sum_cap = sum_cap + pcap * sat * over
        sum_sat = sum_sat + pd * sat

    restricted = (
        (flux_x - from_above(flux_x, 0.0)) + (flux_y - from_left(flux_y)) - sum_sat - local_ref[0]
    )
    for at, value in enumerate((sum_kh, sum_k, sum_cap, restricted, local_ref[1])):
        sums_ref[at] = value
    low_h, high_h, low_k, high_k = [edge_ref[i] for i in range(4)]
    to_even_ref[:, 0:width] = jnp.where(even, high_h, low_h)
    to_odd_ref[:, 0:width] = jnp.where(even, low_h, high_h)
    mine_ref[0] = jnp.where(even, high_k, low_k)
    mine_ref[1] = jnp.where(even, low_k, high_k)
    low_tail = jnp.concatenate([restricted[0:1], sum_k[1:2]], axis=1)
    high_tail = jnp.concatenate([restricted[rows - 1 : rows], sum_k[rows - 2 : rows - 1]], axis=1)
    for out_ref, tail in (
        (to_even_ref, jnp.where(even, high_tail, low_tail)),
        (to_odd_ref, jnp.where(even, low_tail, high_tail)),
    ):
        for j, (row, lane) in enumerate(tail_spots(layers, width)):
            out_ref[row : row + 1, lane : lane + LANES] = tail[:, j * LANES : (j + 1) * LANES]


def edge_block(odd, rim_ref, mine_ref, to_ref, from_ref):
    _, layers, width = rim_ref.shape
    pa, pn, pc, psk, pd = [rim_ref[i] for i in range(5)]
    theirs = from_ref[:, 0:width]
    kap, sat, over = hydraulics(theirs, pa, pn, pc, psk)
    cond = kap * kap
    tail = jnp.concatenate(
        [from_ref[row : row + 1, lane : lane + LANES] for row, lane in tail_spots(layers, width)],
        axis=1,
    )

    def total(x):
        return jnp.sum(x, axis=0, keepdims=True)

    flux = total(mine_ref[odd] * kap * (theirs - to_ref[:, 0:width]))
    block = jnp.concatenate(
        [
            total(cond * theirs),
            total(cond),
            total(pd * (pn - 1.0) * sat * over),
            tail[:, 0:width] - flux,
            tail[:, width:],
            total(jnp.exp2(pa)),
            flux,
            jnp.zeros_like(flux),
        ],
        axis=0,
    )
    return jnp.where(paired()[odd], block, 0.0)


def odd_edge_kernel(rim_ref, mine_ref, to_ref, from_ref, block_ref):
    block_ref[...] = edge_block(1, rim_ref, mine_ref, to_ref, from_ref)


def fold_spots(row, width):
    chunks = width // LANES
    return [((row * chunks + c) % 8, width + (row * chunks + c) // 8 * LANES) for c in range(chunks)]


def even_edge_kernel(rim_ref, mine_ref, to_ref, from_ref, odd_block_ref, halo_ref, block_ref):
    width = block_ref.shape[1]
    block_ref[...] = edge_block(0, rim_ref, mine_ref, to_ref, from_ref)
    for side, source in enumerate((block_ref, odd_block_ref)):
        halo_ref[4 * side : 4 * side + 4, 0:width] = source[0:4, :]
        for row in range(3):
            for c, (at, lane) in enumerate(fold_spots(3 * side + row, width)):
                halo_ref[at : at + 1, lane : lane + LANES] = source[
                    4 + row : 5 + row, c * LANES : (c + 1) * LANES
                ]


def columns_kernel(sums_ref, their_sums_ref, columns_ref):
    kh, kk, cap, rest, rate = [sums_ref[i] + their_sums_ref[i] for i in range(5)]
    for i, value in enumerate((kh / kk, jnp.sqrt(kk), cap, rest, rate)):
        columns_ref[i] = value


def coarse_kernel(
    depth_total, smooth_ref, columns_ref, halo_ref, their_halo_ref, out_ref, head_ref
):
    rows = smooth_ref.shape[1]
    base, root, cap, rest, rate = [columns_ref[i] for i in range(5)]
    width = columns_ref.shape[2]
    head = halo_ref[:, 0:width] + their_halo_ref[:, 0:width]
    sides = []
    for side in range(2):
        rows_of = [head[i : i + 1] for i in range(4 * side, 4 * side + 4)]
        for row in range(3 * side, 3 * side + 3):
            rows_of.append(
                jnp.concatenate(
                    [
                        halo_ref[at : at + 1, lane : lane + LANES]
                        + their_halo_ref[at : at + 1, lane : lane + LANES]
                        for at, lane in fold_spots(row, width)
                    ],
                    axis=1,
                )
            )
        sides.append(rows_of)
    even = even_area()
    lo = [jnp.where(even, b, a) for a, b in zip(*sides)]
    hi = [jnp.where(even, a, b) for a, b in zip(*sides)]
    spot = row_iota(rest.shape)
    rest = jnp.where(spot == 0, rest + lo[6], rest)
    rest = jnp.where(spot == rows - 1, rest + hi[6], rest)

    def pair(i):
        return jnp.where(spot == 0, lo[i], jnp.where(spot == rows - 1, hi[i], 0.0))

    h_kh, h_k, h_cap, h_rest, o_k, h_rate = [pair(i) for i in range(6)]
    edge_lane = lane_iota(rest.shape)

    def lateral(x):
        return from_left(x) + from_right(x)

    h_live = h_k > 0.0
    h_base = jnp.where(h_live, h_kh / jnp.where(h_live, h_k, 1.0), 0.0)
    h_root = jnp.sqrt(h_k)
    o_root = jnp.sqrt(o_k)

    def around(x, halo):
        return from_above(x, halo[0:1]), from_below(x, halo[rows - 1 : rows])

    def flow(head, halo_head, tau, halo_tau):
        tau_u, tau_d = around(tau, halo_tau)
        head_u, head_d = around(head, halo_head)
        tau_l, tau_r = from_left(tau), from_right(tau)
        head_l, head_r = from_left(head), from_right(head)
        inflow = (
            tau_u * (head_u - head)
            + tau_d * (head_d - head)
            + tau_l * (head_l - head)
            + tau_r * (head_r - head)
        )
        return tau * inflow, tau * (tau_u + tau_d + tau_l + tau_r)

    start_in, start_sum = flow(base, h_base, root, h_root)
    rhs = rest - start_in
    first = base + RELAX * rest / (cap + start_sum)
    h_diag = h_cap + h_root * (o_root + root + lateral(h_root))
    h_first = h_base + jnp.where(h_live, RELAX * h_rest / jnp.where(h_live, h_diag, 1.0), 0.0)
    half = 0.5 / depth_total
    tau = root * jnp.exp(half * rate * jnp.tanh(first - base))
    h_tau = h_root * jnp.exp(half * h_rate * jnp.tanh(h_first - h_base))
    first_in, first_sum = flow(first, h_first, tau, h_tau)
    first_flow = cap * (first - base) - first_in
    second = first - RELAX * (first_flow - rhs) / (cap + first_sum)
    head_ref[...] = second
    shift = second - base
    out_ref[...] = smooth_ref[...] + shift[None]


def shards(pressure, theta_old, source, soil_type, soil_params):
    layers, rows, width = pressure.shape
    areas = lax.axis_size("area")
    depths = lax.axis_size("depth")
    swap = depths == 2
    both = ("area", "depth")
    even_moves = full_swap([(i, i + 1) for i in range(0, areas - 1, 2)], areas, depths)
    odd_moves = full_swap([(i, i + 1) for i in range(1, areas - 1, 2)], areas, depths)
    down = [(i, i + 1) for i in range(depths - 1)]
    up = [(b, a) for a, b in down]
    swapped = [(0, 1), (1, 0)]

    def shape(*dims):
        return jax.ShapeDtypeStruct(dims, F32)

    params = pltpu.CompilerParams(vmem_limit_bytes=16 << 20)
    verts = 1 if swap else 2
    kind_count = soil_params.shape[1]
    in_hbm = [
        pltpu.with_memory_space_constraint(x, pltpu.HBM)
        for x in (pressure, soil_type)
    ]
    tab, tab_rows = pl.pallas_call(
        table_kernel,
        out_shape=[shape(5, kind_count, 8, LANES), shape(5, 8, LANES)],
        in_specs=whole(1),
        out_specs=whole(2),
        compiler_params=params,
        name="table",
    )(soil_params)
    packed = pl.pallas_call(
        functools.partial(pack_kernel, swap),
        out_shape=[shape(2, layers, width)] * 2 + [shape(2, rows, width)] * verts,
        in_specs=[pl.BlockSpec(memory_space=pltpu.HBM)] * 2,
        out_specs=whole(2 + verts),
        scratch_shapes=[
            pltpu.VMEM((2, layers, width), F32),
            pltpu.VMEM((2, layers, width), jnp.int32),
            pltpu.VMEM((verts, rows, width), F32),
            pltpu.VMEM((verts, rows, width), jnp.int32),
            pltpu.SemaphoreType.DMA((4 + 2 * verts,)),
        ],
        compiler_params=params,
        cost_estimate=pl.CostEstimate(flops=PACK_COST, transcendentals=0, bytes_accessed=0),
        name="pack",
    )(*in_hbm)
    from_odd = lax.ppermute(packed[1], both, odd_moves)
    from_even = lax.ppermute(packed[0], both, even_moves)
    if swap:
        vert = [lax.ppermute(packed[2], "depth", swapped)]
    else:
        vert = [lax.ppermute(packed[2], "depth", down), lax.ppermute(packed[3], "depth", up)]
    kept, kap, local_sums = pl.pallas_call(
        local_kernel,
        out_shape=[shape(8, layers, rows, width), shape(layers, rows, width), shape(2, rows, width)],
        in_specs=whole(6),
        out_specs=whole(3),
        compiler_params=params,
        name="local",
    )(pressure, theta_old, source, soil_type, tab, tab_rows)
    rims = [
        pl.pallas_call(
            functools.partial(rim_kernel, odd),
            out_shape=shape(6, layers, width),
            in_specs=whole(2),
            out_specs=whole(1)[0],
            compiler_params=params,
            name="rim",
        )(from_area, tab)
        for odd, from_area in enumerate((from_even, from_odd))
    ]
    sent = shape(layers, sent_width(layers, width))
    smooth, sums, to_even, to_odd, mine = pl.pallas_call(
        functools.partial(fine_kernel, swap),
        out_shape=[
            shape(layers, rows, width),
            shape(5, rows, width),
            sent,
            sent,
            shape(2, layers, width),
        ],
        in_specs=whole(9 + verts),
        out_specs=whole(5),
        scratch_shapes=[pltpu.VMEM((4, layers, width), F32)] * 2,
        compiler_params=params,
        name="fine",
    )(pressure, kept, kap, local_sums, tab, from_even, from_odd, *rims, *vert)
    from_odd = lax.ppermute(to_odd, both, odd_moves)
    from_even = lax.ppermute(to_even, both, even_moves)
    if swap:
        their_sums = lax.ppermute(sums, "depth", swapped)
    else:
        sums, their_sums = lax.psum(sums, "depth"), jnp.zeros_like(sums)
    odd_block = pl.pallas_call(
        odd_edge_kernel,
        out_shape=shape(8, width),
        in_specs=whole(4),
        out_specs=whole(1)[0],
        compiler_params=params,
        cost_estimate=pl.CostEstimate(flops=EDGE_COST, transcendentals=0, bytes_accessed=0),
        name="odd_edge",
    )(rims[1], mine, to_odd, from_odd)
    halo = pl.pallas_call(
        even_edge_kernel,
        out_shape=shape(8, width + pl.cdiv(6 * width // LANES, 8) * LANES),
        in_specs=whole(5),
        out_specs=whole(1)[0],
        scratch_shapes=[pltpu.VMEM((8, width), F32)],
        compiler_params=params,
        name="even_edge",
    )(rims[0], mine, to_even, from_even, odd_block)
    if swap:
        their_halo = lax.ppermute(halo, "depth", swapped)
    else:
        halo, their_halo = lax.psum(halo, "depth"), jnp.zeros_like(halo)
    columns = pl.pallas_call(
        columns_kernel,
        out_shape=shape(5, rows, width),
        in_specs=whole(2),
        out_specs=whole(1)[0],
        compiler_params=params,
        name="columns",
    )(sums, their_sums)
    out, head = pl.pallas_call(
        functools.partial(coarse_kernel, layers * depths),
        out_shape=[shape(layers, rows, width), shape(rows, width)],
        in_specs=whole(4),
        out_specs=whole(2),
        compiler_params=params,
        name="coarse",
    )(smooth, columns, halo, their_halo)
    return out, head


def solution(mesh):
    in_specs = (
        P("depth", "area", None),
        P("depth", "area", None),
        P("depth", "area", None),
        P("depth", "area", None),
        P(),
    )
    out_specs = (P("depth", "area", None), P("area", None))
    return jax.shard_map(shards, mesh=mesh, in_specs=in_specs, out_specs=out_specs, check_vma=False)
```
